128 devices in a mesh: gx: 16 (over y, x), gy: 8 (over z, core).
Axes of the slice: x: 4, y: 4, z: 4, core: 2. Of those that a mesh axis runs over, the one named last changes fastest.
Arguments:
- charge_blocks: float32 [524288, 128], P(('gx', 'gy')), may hold values from -6 to 6
- block_tile: int32 [524288], P(('gx', 'gy')), may hold values from 0 to 196607, as said below
- block_count: int32 [128], P(('gx', 'gy')), may hold values from 2048 to 4096, as said below
- near_kernel: float32 [9, 9, 9], replicated, may hold values from -0.21875 to 0.21875
- mid_kernel: float32 [9, 9, 9], replicated, may hold values from -0.109375 to 0.109375
- top_weights: float32 [4], replicated, may hold values from 0.00072168784 to 0.1
- top_widths: float32 [4], replicated, may hold values from 1 to 12
Outputs:
- potential: float32 [512, 192, 256], P('gx', 'gy')
The draws below stay inside these ranges and needn't reach their ends.
Inputs may be any that keep to these rules, and one draw needn't show every extreme that they name: `block_tile`: of the 4096 slots of one device, exactly 32 name tiles in the pencil of each device, dead slots included. Slots 0 to block_count - 1 of a device are live, the others hold values that are ignored.
All inputs are finite; a program needn't handle non-finite values.
Results may differ from the reference program's by a relative error of at most 0.000082.
Values sent between devices are 32-bit elements; how exact they have to be, the bound alone decides.
No kernel may reach another device: no remote copies, remote signals or barrier semaphores. Data moves between devices by JAX's collectives and lax.ppermute only.
A program may use at most 128 MiB of HBM per device.

```python
import jax
import jax.numpy as jnp
from jax import lax

CX = 32
CY = 24
NZ = 256
CAP = 32
RADIUS = 4
ZB = 128
GAUSS = 4
NX = 512
NY = 192
BLK = 4096
SLOTS = 524288
N_GX = 16
N_GY = 8


def draw_block_tile(key, part):
    device_total = N_GX * N_GY
    subkeys = jax.random.split(jax.random.fold_in(key, 17), 5)
    owners = jnp.tile(jnp.arange(device_total, dtype=jnp.int32), CAP)
    destination = jax.vmap(lambda subkey: jax.random.permutation(subkey, owners))(jax.random.split(subkeys[0], device_total))
    local_x = jax.random.randint(subkeys[1], (device_total, BLK), 0, CX)
    local_y = jax.random.randint(subkeys[2], (device_total, BLK), 0, CY)
    local_z = jax.random.randint(subkeys[3], (device_total, BLK), 0, NZ // ZB)
    source = jnp.arange(device_total, dtype=jnp.int32)[:, None]
    special = jax.random.randint(subkeys[4], (), 0, device_total)
    top_hit = (source == special) & (destination == device_total - 1)
    low_hit = (source == special) & (destination == 0)
    local_x = jnp.where(top_hit, CX - 1, jnp.where(low_hit, 0, local_x))
    local_y = jnp.where(top_hit, CY - 1, jnp.where(low_hit, 0, local_y))
    local_z = jnp.where(top_hit, NZ // ZB - 1, jnp.where(low_hit, 0, local_z))
    global_x = destination // N_GY * CX + local_x
    global_y = destination % N_GY * CY + local_y
    tile_index = (global_x * NY + global_y) * (NZ // ZB) + local_z
    return tile_index.reshape(-1).astype(jnp.int32)


def draw_block_count(key, part):
    device_total = N_GX * N_GY
    subkeys = jax.random.split(jax.random.fold_in(key, 29), 3)
    counts = jax.random.randint(subkeys[0], (device_total,), BLK // 2, BLK + 1)
    fullest = jax.random.randint(subkeys[1], (), 0, device_total)
    emptiest = (fullest + 1 + jax.random.randint(subkeys[2], (), 0, device_total - 1)) % device_total
    device_ids = jnp.arange(device_total, dtype=jnp.int32)
    counts = jnp.where(device_ids == fullest, BLK, jnp.where(device_ids == emptiest, BLK // 2, counts))
    return counts.astype(jnp.int32)


def gaussian_terms(key):
    subkeys = jax.random.split(jax.random.fold_in(key, 41), 2)
    widest = jnp.float32(min(NX, NY, NZ) // 16)
    widths = jnp.exp(jax.random.uniform(subkeys[0], (GAUSS,), jnp.float32, 0.0, jnp.log(widest)))
    factors = jnp.exp(jax.random.uniform(subkeys[1], (GAUSS,), jnp.float32, jnp.log(0.03), jnp.log(0.1)))
    weights = factors / (widths * jnp.sqrt(widths))
    return (widths.astype(jnp.float32), weights.astype(jnp.float32))


def draw_top_widths(key, part):
    return gaussian_terms(key)[0]


def draw_top_weights(key, part):
    return gaussian_terms(key)[1]


def level_of(key, dims, cuts, low, largest):
    factor_of, own = 1.0, jax.random.fold_in(key, 6)
    for dim, shards_of in cuts:
        heights = jnp.exp(jax.random.uniform(jax.random.fold_in(own, dim), (shards_of,), jnp.float32, low / len(cuts), largest / len(cuts)))
        factor_of = factor_of * jnp.repeat(heights, dims[dim] // shards_of).reshape([-1 if axis == dim else 1 for axis in range(len(dims))])
    return factor_of


def gaussian(stream_key, shape, width, bound, shards=(), held_as=jnp.bfloat16):
    values = width * jax.random.normal(stream_key, shape, jnp.float32)
    if shards:
        values = values * level_of(stream_key, shape, shards, -0.22, 0.18)
    return jnp.clip(values, -bound, bound).astype(held_as)


def setup_inputs(seed: int = 0) -> dict:
    key_list = jax.random.split(jax.random.key(seed), 8)
    charge_blocks = gaussian(key_list[0], (SLOTS, ZB), 1.0, 6.0, ((0, 128),), jnp.float32)
    block_tile = draw_block_tile(jax.random.fold_in(key_list[7], 71), 0)
    block_count = draw_block_count(jax.random.fold_in(key_list[7], 71), 0)
    near_kernel = gaussian(key_list[3], (2 * RADIUS + 1, 2 * RADIUS + 1, 2 * RADIUS + 1), ((2 * RADIUS + 1) ** 3) ** -0.5, 0.21875, (), jnp.float32)
    mid_kernel = gaussian(key_list[4], (2 * RADIUS + 1, 2 * RADIUS + 1, 2 * RADIUS + 1), (4 * (2 * RADIUS + 1) ** 3) ** -0.5, 0.109375, (), jnp.float32)
    top_weights = draw_top_weights(jax.random.fold_in(key_list[7], 71), 0)
    top_widths = draw_top_widths(jax.random.fold_in(key_list[7], 71), 0)
    return dict(charge_blocks=charge_blocks, block_tile=block_tile, block_count=block_count, near_kernel=near_kernel, mid_kernel=mid_kernel, top_weights=top_weights, top_widths=top_widths)


PRECISE = lax.Precision.HIGHEST


def restrict_axis(values, axis_dim):
    before = jnp.roll(values, 1, axis_dim)
    behind = jnp.roll(values, -1, axis_dim)
    summed = values + 0.5 * (before + behind)
    return lax.slice_in_dim(summed, 0, values.shape[axis_dim], 2, axis_dim)


def restrict(values):
    return restrict_axis(restrict_axis(restrict_axis(values, 0), 1), 2)


def prolong_axis(coarse, axis_dim):
    following = jnp.roll(coarse, -1, axis_dim)
    paired = jnp.stack([coarse, 0.5 * (coarse + following)], axis=axis_dim + 1)
    layout = list(coarse.shape)
    layout[axis_dim] = 2 * layout[axis_dim]
    return paired.reshape(layout)


def prolong(coarse):
    return prolong_axis(prolong_axis(prolong_axis(coarse, 0), 1), 2)


def correlate(values, kernel):
    diameter = 2 * RADIUS + 1
    flipped = kernel[::-1, ::-1, ::-1]
    embedded = jnp.zeros(values.shape, jnp.float32).at[:diameter, :diameter, :diameter].set(flipped)
    embedded = jnp.roll(embedded, (-RADIUS, -RADIUS, -RADIUS), (0, 1, 2))
    spectrum = jnp.fft.rfftn(embedded) * jnp.fft.rfftn(values)
    return jnp.fft.irfftn(spectrum, s=values.shape).astype(jnp.float32)


def gaussians(period, widths, row_count):
    row_ids = jnp.arange(row_count, dtype=jnp.int32)[:, None]
    col_ids = jnp.arange(period, dtype=jnp.int32)[None, :]
    offset = (row_ids - col_ids) % period
    distance = jnp.minimum(offset, period - offset).astype(jnp.float32)
    return jnp.exp(-(distance * distance)[None] / (widths * widths)[:, None, None])


def top_level(top_charge, top_weights, top_widths):
    size_a, size_b, size_c = top_charge.shape
    gauss_x = gaussians(size_a, top_widths, size_a)
    gauss_y = gaussians(size_b, top_widths, size_b)
    gauss_z = gaussians(size_c, top_widths, size_c)
    along_x = jnp.einsum("kia,abc->kibc", gauss_x, top_charge, precision=PRECISE)
    along_y = jnp.einsum("kjb,kibc->kijc", gauss_y, along_x, precision=PRECISE)
    along_z = jnp.einsum("kzc,kijc->kijz", gauss_z, along_y, precision=PRECISE)
    return jnp.einsum("k,kijz->ijz", top_weights, along_z, precision=PRECISE)


def reference(charge_blocks, block_tile, block_count, near_kernel, mid_kernel, top_weights, top_widths):
    device_total = N_GX * N_GY
    slot_ids = jnp.arange(device_total * BLK, dtype=jnp.int32)
    owners = (slot_ids // BLK).astype(jnp.int32)
    live_slot = (slot_ids % BLK) < block_count[owners]
    masked = charge_blocks * live_slot[:, None].astype(jnp.float32)
    fine_charge = jax.ops.segment_sum(masked, block_tile, num_segments=NX * NY * (NZ // ZB)).reshape(NX, NY, NZ)
    mid_charge = restrict(fine_charge)
    top_charge = restrict(mid_charge)
    top_potential = top_level(top_charge, top_weights, top_widths)
    mid_potential = correlate(mid_charge, mid_kernel) + prolong(top_potential)
    return correlate(fine_charge, near_kernel) + prolong(mid_potential)
```

```python
import functools

import jax
import jax.numpy as jnp
import numpy as np
from jax import lax
from jax.experimental import pallas as pl
from jax.experimental.pallas import tpu as pltpu
from jax.sharding import PartitionSpec as P

CX = 32
CY = 24
NZ = 256
CAP = 32
DEVICES = 128
ROWS = CAP + 1
SIZE_X = 16
SIZE_Y = 8
DEAD = 2047
LOW = 9
HIGH = 10
YD = 32
F32 = jnp.float32
BF16 = jnp.bfloat16
PRECISE = lax.Precision.HIGHEST


def mm(a, b):
    return jnp.dot(a, b, preferred_element_type=F32)


def halves(value):
    top = value.astype(BF16)
    return top, (value - top.astype(F32)).astype(BF16)


def np_halves(matrix):
    matrix = np.asarray(matrix, np.float32)
    top = matrix.astype(BF16)
    return top, (matrix - top.astype(np.float32)).astype(BF16)


def route_kernel(tile_ref, info_ref, pos_ref, ids_ref, owner_s, code_s, acc_s):
    tile = tile_ref[...]
    column = tile >> 1
    high_part = column >> 6
    grid_x = (high_part * 43691) >> 17
    grid_y = column - grid_x * (CY * SIZE_Y)
    owner_y = ((grid_y >> 3) * 43) >> 7
    owner = (grid_x >> 5) * SIZE_Y + owner_y
    cell = (tile & 1) * (CX * CY) + (grid_x & (CX - 1)) * CY + (grid_y - owner_y * CY)
    slot = lax.broadcasted_iota(jnp.int32, tile.shape, 0) * 128 + lax.broadcasted_iota(
        jnp.int32, tile.shape, 1
    )
    code = jnp.where(slot < info_ref[0], cell, DEAD)
    owner_s[...] = owner
    code_s[...] = code
    lane_offset = info_ref[1]
    rows = lax.broadcasted_iota(jnp.int32, (128, 128), 0)
    before = lax.broadcasted_iota(jnp.int32, (128, 256), 0)
    after = lax.broadcasted_iota(jnp.int32, (128, 256), 1)
    prefix = jnp.where((before < after) | (after >= 128), 1.0, 0.0).astype(BF16)
    acc_s[...] = jnp.zeros_like(acc_s)

    def chunk(c, base):
        own = owner_s[pl.ds(c, 1), :]
        ids = code_s[pl.ds(c, 1), :]
        hit = rows == own
        one_hot = jnp.where(hit, 1.0, 0.0).astype(BF16)
        counted = mm(one_hot, prefix)
        rank = jnp.sum(jnp.where(hit, counted[:, :128] + base, 0.0), axis=0, keepdims=True)
        rank = rank.astype(jnp.int32)
        pos_ref[pl.ds(c, 1), :] = own * ROWS + rank
        place = jnp.where(rows == rank + lane_offset, 1.0, 0.0).astype(BF16)
        coarse = jnp.where(hit, (ids >> 4).astype(F32), 0.0)
        fine = jnp.where(hit, (ids & 15).astype(F32), 0.0)
        both = jnp.concatenate([coarse, fine], axis=0).astype(BF16)
        acc_s[...] += lax.dot_general(
            both, place, (((1,), (1,)), ((), ())), preferred_element_type=F32
        )
        return base + counted[:, 128:]

    lax.fori_loop(0, tile.shape[0], chunk, jnp.zeros((128, 128), F32), unroll=4)
    ids_ref[...] = acc_s[:128] * 16.0 + acc_s[128:]


def route(tile, info):
    return pl.pallas_call(
        route_kernel,
        out_shape=(
            jax.ShapeDtypeStruct((32, 128), jnp.int32),
            jax.ShapeDtypeStruct((128, 128), F32),
        ),
        in_specs=[
            pl.BlockSpec(memory_space=pltpu.VMEM),
            pl.BlockSpec(memory_space=pltpu.SMEM),
        ],
        out_specs=(
            pl.BlockSpec(memory_space=pltpu.VMEM),
            pl.BlockSpec(memory_space=pltpu.VMEM),
        ),
        scratch_shapes=[
            pltpu.VMEM((32, 128), jnp.int32),
            pltpu.VMEM((32, 128), jnp.int32),
            pltpu.VMEM((256, 128), F32),
        ],
        name="route",
    )(tile, info)


def pack_kernel(pos_ref, data_ref, ids_ref, out_ref):
    step = 16

    def body(b, carry):
        start = pl.multiple_of(b * step, step)
        block = data_ref[pl.ds(start, step), :]
        row = b // (128 // step)
        lane = (b % (128 // step)) * step
        for j in range(step):
            out_ref[pl.ds(pos_ref[row, lane + j], 1), :] = block[j : j + 1]
        return carry

    lax.fori_loop(0, 4096 // step, body, 0)

    def tail(b, carry):
        start = pl.multiple_of(b * 8, 8)
        block = ids_ref[pl.ds(start, 8), :]
        for j in range(8):
            out_ref[pl.ds((start + j) * ROWS + CAP, 1), :] = block[j : j + 1]
        return carry

    lax.fori_loop(0, DEVICES // 8, tail, 0)


def pack(pos, data, ids):
    return pl.pallas_call(
        pack_kernel,
        out_shape=jax.ShapeDtypeStruct((DEVICES * ROWS, 128), F32),
        in_specs=[
            pl.BlockSpec(memory_space=pltpu.SMEM),
            pl.BlockSpec(memory_space=pltpu.VMEM),
            pl.BlockSpec(memory_space=pltpu.VMEM),
        ],
        out_specs=pl.BlockSpec(memory_space=pltpu.VMEM),
        name="pack",
    )(pos, data, ids)


def gather_kernel(in_ref, out_ref, data_s, ids_s):
    for c in range(DEVICES // 4):
        total = None
        for j in range(4):
            base = (c * 4 + j) * ROWS
            top, rest = halves(in_ref[base : base + CAP, :])
            start = (c * 4 + j) * CAP
            data_s[start : start + CAP, :128] = top
            data_s[start : start + CAP, 128:] = rest
            line = in_ref[base + CAP : base + CAP + 1, :]
            total = line if total is None else total + line
        ids_s[c : c + 1, :] = total.astype(jnp.int32)
    rows = lax.broadcasted_iota(jnp.int32, (256, 128), 0)

    def block(b, carry):
        for half in range(2):
            first = half * (CX * CY) + b * 256
            acc = jnp.zeros((256, 256), F32)
            for k in range(16):
                parts = []
                for q in range(2):
                    ids = ids_s[2 * k + q : 2 * k + q + 1, :] - first
                    parts.append(jnp.where(rows == ids, 1.0, 0.0).astype(BF16))
                acc = acc + mm(jnp.concatenate(parts, axis=1), data_s[k * 256 : (k + 1) * 256, :])
            start = pl.multiple_of(b * 256, 256)
            out_ref[pl.ds(start, 256), half * 128 : half * 128 + 128] = acc[:, :128] + acc[:, 128:]
        return carry

    lax.fori_loop(0, 3, block, 0)


def collect(arrived):
    return pl.pallas_call(
        gather_kernel,
        out_shape=jax.ShapeDtypeStruct((CX * CY, NZ), F32),
        in_specs=[pl.BlockSpec(memory_space=pltpu.VMEM)],
        out_specs=pl.BlockSpec(memory_space=pltpu.VMEM),
        scratch_shapes=[
            pltpu.VMEM((DEVICES * CAP, 256), BF16),
            pltpu.VMEM((DEVICES // 4, 128), jnp.int32),
        ],
        name="collect",
    )(arrived)


def z_matrices(period, copies):
    half = period // 2
    z = np.arange(period)[:, None]
    f = np.arange(half)[None, :]
    angle = 2 * np.pi * ((z * f) % period) / period
    cosine, sine = np.cos(angle), -np.sin(angle)
    sine[:, 0] = (-1.0) ** np.arange(period)
    scale = np.full((half, 1), 2.0 / period)
    scale[0] = 1.0 / period
    forward = np.zeros((256, 256))
    inverse = np.zeros((256, 256))
    for c in range(copies):
        rows = slice(c * period, (c + 1) * period)
        real = slice(c * half, (c + 1) * half)
        imag = slice(128 + c * half, 128 + (c + 1) * half)
        forward[rows, real] = cosine
        forward[rows, imag] = sine
        inverse[real, rows] = scale * cosine.T
        inverse[imag, rows] = scale * sine.T
    return forward, inverse


def y_matrices():
    order = np.concatenate([np.arange(17), np.arange(31, 16, -1)])
    y = np.arange(YD)
    angle = 2 * np.pi * ((order[:, None] * y[None, :]) % YD) / YD
    cosine, sine = np.cos(angle), np.sin(angle)
    forward = np.block([[cosine, sine], [-sine, cosine]])
    inverse = np.block([[cosine.T, -sine.T], [sine.T, cosine.T]]) / YD
    return np.kron(np.eye(4), forward), np.kron(np.eye(4), inverse)


def stacked_rows(matrix):
    top, rest = np_halves(matrix)
    return np.concatenate([top, rest], axis=0)


def stacked_cols(matrix):
    top, rest = np_halves(matrix)
    return np.concatenate([top, rest], axis=1)


def right_product(value, matrix_ref):
    top, rest = halves(value)
    return (
        mm(top, matrix_ref[:256, :]) + mm(top, matrix_ref[256:, :]) + mm(rest, matrix_ref[:256, :])
    )


def left_product(matrix_ref, value):
    top, rest = halves(value)
    return (
        mm(matrix_ref[:, :256], top) + mm(matrix_ref[:, 256:], top) + mm(matrix_ref[:, :256], rest)
    )


def special_mask(copies, rows):
    lane = lax.broadcasted_iota(jnp.int32, (rows, 128), 1)
    row = lax.broadcasted_iota(jnp.int32, (rows, 128), 0)
    return (lane & (128 // copies - 1)) == 0, row


def forward_chunk(value, z_ref, y_ref, copies):
    z_freq = right_product(value, z_ref)
    stacks = []
    for h in range(2):
        pieces = []
        for q in range(4):
            slab = z_freq[(h * 4 + q) * YD : (h * 4 + q + 1) * YD]
            pieces += [slab[:, :128], slab[:, 128:]]
        stacks.append(jnp.concatenate(pieces, axis=0))
    freq = left_product(y_ref, jnp.concatenate(stacks, axis=1))
    lane_special, row = special_mask(copies, 16)
    special = lane_special & (row != 0)
    slabs = []
    for h in range(2):
        for q in range(4):
            slab = freq[q * 64 : (q + 1) * 64, h * 128 : (h + 1) * 128]
            ar, br, ai, bi = slab[:16], slab[16:32], slab[32:48], slab[48:]
            slabs.append(
                jnp.concatenate(
                    [
                        jnp.where(special, 0.5 * (ar + br), ar),
                        jnp.where(special, 0.5 * (ai + bi), br),
                        jnp.where(special, 0.5 * (ai - bi), ai),
                        jnp.where(special, 0.5 * (br - ar), bi),
                    ],
                    axis=0,
                )
            )
    return slabs


def inverse_chunk(slabs, z_ref, y_ref):
    stacks = [jnp.concatenate(slabs[h * 4 : h * 4 + 4], axis=0) for h in range(2)]
    space = left_product(y_ref, jnp.concatenate(stacks, axis=1))
    rows = []
    for h in range(2):
        for q in range(4):
            slab = space[q * 64 : (q + 1) * 64, h * 128 : (h + 1) * 128]
            rows.append(jnp.concatenate([slab[:YD], slab[YD:]], axis=1))
    return right_product(jnp.concatenate(rows, axis=0), z_ref)


def taps_kernel(copies, in_ref, z_ref, y_ref, real_ref, twin_ref, imag_ref):
    lane_special, row = special_mask(copies, YD)
    special = lane_special & ((row == 0) | (row == 16))
    for p in range(2):
        slabs = forward_chunk(in_ref[p * 256 : (p + 1) * 256, :], z_ref, y_ref, copies)
        for j in range(8):
            dx = p * 8 + j
            if dx > 8:
                break
            real, imag = slabs[j][:YD], slabs[j][YD:]
            at = slice(dx * YD, (dx + 1) * YD)
            real_ref[at, :] = real
            twin_ref[at, :] = jnp.where(special, imag, real)
            imag_ref[at, :] = jnp.where(special, 0.0, imag)


def taps(kernel, copies, z_matrix, y_matrix):
    flipped = kernel[:, ::-1, ::-1]
    tall = jnp.concatenate(
        [flipped[:, 8:], jnp.zeros((9, YD - 9, 9), F32), flipped[:, :8]], axis=1
    )
    period = 256 // copies
    wide = jnp.concatenate(
        [tall[:, :, 4:], jnp.zeros((9, YD, period - 9), F32), tall[:, :, :4]], axis=2
    )
    wide = jnp.concatenate([wide] * copies, axis=2)
    wide = jnp.concatenate([wide, jnp.zeros((7, YD, 256), F32)], axis=0)
    shape = jax.ShapeDtypeStruct((9 * YD, 128), F32)
    return pl.pallas_call(
        functools.partial(taps_kernel, copies),
        out_shape=(shape, shape, shape),
        in_specs=[pl.BlockSpec(memory_space=pltpu.VMEM)] * 3,
        out_specs=(pl.BlockSpec(memory_space=pltpu.VMEM),) * 3,
        name=f"taps{copies}",
    )(wide.reshape(16 * YD, 256), z_matrix, y_matrix)


def cutoff_kernel(
    copies, slabs_in, block_out, blocks, keep,
    in_ref, real_ref, twin_ref, imag_ref, zf_ref, yf_ref, zi_ref, yi_ref, out_ref, freq_s, conv_s,
):
    for p in range(slabs_in // 8):
        slabs = forward_chunk(in_ref[p * 256 : (p + 1) * 256, :], zf_ref, yf_ref, copies)
        for j in range(8):
            freq_s[(p * 8 + j) * 64 : (p * 8 + j + 1) * 64, :] = slabs[j]
    slabs_out = conv_s.shape[0] // 64
    if block_out * blocks < slabs_out:
        conv_s[block_out * blocks * 64 :, :] = jnp.zeros(
            ((slabs_out - block_out * blocks) * 64, 128), F32
        )
    lane_special, row = special_mask(copies, 8)

    def step(index, carry):
        v = index % 2
        first = (index // 2) * block_out
        sums = [[None] * 4 for _ in range(block_out)]
        for dx in range(9):
            coefs = []
            for half in range(2):
                at = pl.ds(pl.multiple_of(dx * YD + half * 16 + v * 8, 8), 8)
                coefs.append((real_ref[at, :], twin_ref[at, :], imag_ref[at, :]))
            for j in range(block_out):
                base = (first + j + dx) * 64 + v * 8
                for half in range(2):
                    at = pl.multiple_of(base + half * 16, 8)
                    re = freq_s[pl.ds(at, 8), :]
                    im = freq_s[pl.ds(pl.multiple_of(at + 32, 8), 8), :]
                    a, t, b = coefs[half]
                    new_re = a * re - b * im
                    new_im = b * re + t * im
                    old = sums[j]
                    old[2 * half] = new_re if dx == 0 else old[2 * half] + new_re
                    old[2 * half + 1] = new_im if dx == 0 else old[2 * half + 1] + new_im
        special = lane_special & ((row != 0) | (v != 0))
        for j in range(block_out):
            ar, ai, br, bi = sums[j]
            base = (first + j) * 64 + v * 8
            values = (
                jnp.where(special, ar - bi, ar),
                jnp.where(special, ar + bi, br),
                jnp.where(special, ai + br, ai),
                jnp.where(special, br - ai, bi),
            )
            for part in range(4):
                conv_s[pl.ds(pl.multiple_of(base + part * 16, 8), 8), :] = values[part]
        return carry

    lax.fori_loop(0, 2 * blocks, step, 0)
    for p in range(slabs_out // 8):
        slabs = [conv_s[(p * 8 + j) * 64 : (p * 8 + j + 1) * 64, :] for j in range(8)]
        space = inverse_chunk(slabs, zi_ref, yi_ref)
        for j in range(8):
            if p * 8 + j < out_ref.shape[0]:
                out_ref[p * 8 + j] = space[j * YD : j * YD + keep]


def cutoff(padded, spectrum, tables, copies, slabs_in, block_out, blocks, keep, name):
    slabs_out = -(-block_out * blocks // 8) * 8
    return pl.pallas_call(
        functools.partial(cutoff_kernel, copies, slabs_in, block_out, blocks, keep),
        out_shape=jax.ShapeDtypeStruct((block_out * blocks, keep, 256), F32),
        in_specs=[pl.BlockSpec(memory_space=pltpu.VMEM)] * 8,
        out_specs=pl.BlockSpec(memory_space=pltpu.VMEM),
        scratch_shapes=[
            pltpu.VMEM((slabs_in * 64, 128), F32),
            pltpu.VMEM((slabs_out * 64, 128), F32),
        ],
        cost_estimate=pl.CostEstimate(
            flops=slabs_in * 80_000_000, bytes_accessed=slabs_in * 65536, transcendentals=0
        ),
        name=name,
    )(padded, *spectrum, *tables)


def halo(block, axis, dim, low, high):
    count = lax.axis_size(axis)
    forward = [(i, (i + 1) % count) for i in range(count)]
    backward = [(target, source) for source, target in forward]
    length = block.shape[dim]
    before = lax.ppermute(lax.slice_in_dim(block, length - low, length, axis=dim), axis, forward)
    behind = lax.ppermute(lax.slice_in_dim(block, 0, high, axis=dim), axis, backward)
    return jnp.concatenate([before, block, behind], axis=dim)


def thin_x(values):
    length = values.shape[0]
    centre = values[1 : length - 1 : 2]
    return centre + 0.5 * (values[0 : length - 2 : 2] + values[2:length:2])


def thin_matrix(length):
    count = (length - 1) // 2
    matrix = np.zeros((count, length), np.float32)
    for i in range(count):
        matrix[i, 2 * i : 2 * i + 3] = (0.5, 1.0, 0.5)
    return matrix


def thin_cycle(length):
    matrix = np.zeros((length, length // 2), np.float32)
    for i in range(length // 2):
        matrix[2 * i, i] += 1.0
        matrix[(2 * i - 1) % length, i] += 0.5
        matrix[(2 * i + 1) % length, i] += 0.5
    return matrix


def grow_matrix(count, source):
    matrix = np.zeros((count, source), np.float32)
    for i in range(count):
        if i % 2 == 0:
            matrix[i, i // 2] = 1.0
        else:
            matrix[i, i // 2] = 0.5
            matrix[i, i // 2 + 1] = 0.5
    return matrix


def grow_cycle(source):
    matrix = np.zeros((source, 2 * source), np.float32)
    for i in range(source):
        matrix[i, 2 * i] = 1.0
        matrix[i, 2 * i + 1] += 0.5
        matrix[(i + 1) % source, 2 * i + 1] += 0.5
    return matrix


def thin(values):
    values = thin_x(values)
    values = jnp.einsum("xyz,zc->xyc", values, thin_cycle(values.shape[2]), precision=PRECISE)
    return jnp.einsum("by,xyc->xbc", thin_matrix(values.shape[1]), values, precision=PRECISE)


def grow(values, count_x, count_y):
    size_x, size_y, depth = values.shape
    values = jnp.einsum("jb,abc->ajc", grow_matrix(count_y, size_y), values, precision=PRECISE)
    values = jnp.einsum("ia,ajc->ijc", grow_matrix(count_x, size_x), values, precision=PRECISE)
    return jnp.einsum("ijc,cz->ijz", values, grow_cycle(depth), precision=PRECISE)


def gaussians(period, widths, first_row, row_count):
    row_ids = first_row + jnp.arange(row_count, dtype=jnp.int32)[:, None]
    col_ids = jnp.arange(period, dtype=jnp.int32)[None, :]
    offset = (row_ids - col_ids) % period
    distance = jnp.minimum(offset, period - offset).astype(F32)
    return jnp.exp(-(distance * distance)[None] / (widths * widths)[:, None, None])


def spread_all(values, axis):
    count = lax.axis_size(axis)
    copies = jnp.broadcast_to(values[None], (count,) + values.shape)
    return lax.all_to_all(copies, axis, split_axis=0, concat_axis=0, tiled=True)


def top_level(top_charge, top_weights, top_widths):
    rows_x, rows_y, depth = top_charge.shape
    gauss_x = gaussians(
        rows_x * SIZE_X, top_widths, lax.axis_index("gx") * rows_x, rows_x + 1
    )
    gauss_y = gaussians(
        rows_y * SIZE_Y, top_widths, lax.axis_index("gy") * rows_y, rows_y + 1
    )
    gauss_z = gaussians(depth, top_widths, 0, depth) * top_weights[:, None, None]
    column = spread_all(top_charge, "gx").reshape(SIZE_X * rows_x, rows_y, depth)
    plane = jnp.einsum("kia,abc->kibc", gauss_x, column, precision=PRECISE)
    whole = spread_all(plane, "gy")
    along_y = jnp.einsum(
        "kjsb,skibc->kijc",
        gauss_y.reshape(4, rows_y + 1, SIZE_Y, rows_y),
        whole,
        precision=PRECISE,
    )
    return jnp.einsum("kzc,kijc->ijz", gauss_z, along_y, precision=PRECISE)


def on_device(
    charge_blocks, block_tile, block_count, near_kernel, mid_kernel, top_weights, top_widths
):
    device = lax.axis_index("gx") * SIZE_Y + lax.axis_index("gy")
    info = jnp.stack([block_count[0], (device % 4) * CAP]).astype(jnp.int32)
    pos, ids = route(block_tile.reshape(32, 128), info)
    outgoing = pack(pos, charge_blocks, ids)
    arrived = lax.all_to_all(
        outgoing.reshape(DEVICES, ROWS, 1, 128),
        ("gx", "gy"),
        split_axis=0,
        concat_axis=0,
        tiled=True,
    ).reshape(DEVICES * ROWS, 128)

    z_fine, z_fine_back = z_matrices(256, 1)
    z_mid, z_mid_back = z_matrices(128, 2)
    y_forward, y_back = y_matrices()
    fine_tables = (
        stacked_rows(z_fine), stacked_cols(y_forward), stacked_rows(z_fine_back), stacked_cols(y_back)
    )
    mid_tables = (
        stacked_rows(z_mid), fine_tables[1], stacked_rows(z_mid_back), fine_tables[3]
    )
    fine_taps = taps(near_kernel, 1, fine_tables[0], fine_tables[1])
    mid_taps = taps(mid_kernel, 2, mid_tables[0], mid_tables[1])

    fine = collect(arrived).reshape(CX, CY, NZ)
    wide = halo(halo(fine, "gx", 0, LOW, HIGH), "gy", 1, LOW, HIGH)
    mid = thin(wide)
    top = thin(mid[3:20, 3:16])
    top_potential = top_level(top, top_weights, top_widths)
    near_input = wide[5:45, 5:37].reshape(40 * YD, NZ)
    near = cutoff(near_input, fine_taps, fine_tables, 1, 40, 8, 4, CY, "near")
    tall = jnp.pad(mid, ((0, 8), (0, YD - mid.shape[1]), (0, 0)))
    mid_input = jnp.concatenate([tall[:24], tall[9:33]], axis=2).reshape(24 * YD, 256)
    mid_pair = cutoff(mid_input, mid_taps, mid_tables, 2, 24, 9, 1, 16, "middle")
    mid_near = jnp.concatenate([mid_pair[:, :13, :128], mid_pair[:8, :13, 128:]], axis=0)
    mid_potential = mid_near + grow(top_potential, 17, 13)
    return near + grow(mid_potential, CX, CY)


def solution(mesh):
    placed = (P(("gx", "gy"), None), P(("gx", "gy")), P(("gx", "gy")), P(), P(), P(), P())
    return jax.shard_map(
        on_device, mesh=mesh, in_specs=placed, out_specs=P("gx", "gy", None), check_vma=False
    )
```

```python
import functools

import jax
import jax.numpy as jnp
import numpy as np
from jax import lax
from jax.experimental import pallas as pl
from jax.experimental.pallas import tpu as pltpu
from jax.sharding import PartitionSpec as P

CX = 32
CY = 24
NZ = 256
CAP = 32
DEVICES = 128
ROWS = CAP + 1
SIZE_X = 16
SIZE_Y = 8
DEAD = 2047
SEND = 376
TOP_ROWS = 40
YD = 32
F32 = jnp.float32
BF16 = jnp.bfloat16
VM = pl.BlockSpec(memory_space=pltpu.VMEM)
SM = pl.BlockSpec(memory_space=pltpu.SMEM)
ANY = pl.BlockSpec(memory_space=pl.ANY)


def call(body, name, out, ins, scratch=(), limit=20, flops=0, moved=0):
    many = isinstance(out, tuple)
    return pl.pallas_call(
        body,
        out_shape=out,
        in_specs=ins,
        out_specs=(VM,) * len(out) if many else VM,
        scratch_shapes=list(scratch),
        compiler_params=pltpu.CompilerParams(vmem_limit_bytes=limit << 20),
        cost_estimate=pl.CostEstimate(flops=flops, bytes_accessed=moved, transcendentals=0),
        name=name,
    )


def array(*shape):
    return jax.ShapeDtypeStruct(shape, F32)


def mm(a, b):
    return jnp.dot(a, b, preferred_element_type=F32)


def halves(value):
    top = value.astype(BF16)
    return top, (value - top.astype(F32)).astype(BF16)


def np_halves(matrix):
    matrix = np.asarray(matrix, np.float32)
    top = matrix.astype(BF16)
    return top, (matrix - top.astype(np.float32)).astype(BF16)


def route_kernel(tile_ref, info_ref, pos_ref, ids_ref, owner_s, code_s, acc_s):
    tile = tile_ref[...]
    column = tile >> 1
    high_part = column >> 6
    grid_x = (high_part * 43691) >> 17
    grid_y = column - grid_x * (CY * SIZE_Y)
    owner_y = ((grid_y >> 3) * 43) >> 7
    owner = (grid_x >> 5) * SIZE_Y + owner_y
    cell = (tile & 1) * (CX * CY) + (grid_x & (CX - 1)) * CY + (grid_y - owner_y * CY)
    slot = lax.broadcasted_iota(jnp.int32, tile.shape, 0) * 128 + lax.broadcasted_iota(
        jnp.int32, tile.shape, 1
    )
    code = jnp.where(slot < info_ref[0], cell, DEAD)
    owner_s[...] = owner
    code_s[...] = code
    lane_offset = info_ref[1]
    rows = lax.broadcasted_iota(jnp.int32, (128, 128), 0)
    before = lax.broadcasted_iota(jnp.int32, (128, 256), 0)
    after = lax.broadcasted_iota(jnp.int32, (128, 256), 1)
    prefix = jnp.where((before < after) | (after >= 128), 1.0, 0.0).astype(BF16)
    acc_s[...] = jnp.zeros_like(acc_s)

    def chunk(c, base):
        own = owner_s[pl.ds(c, 1), :]
        ids = code_s[pl.ds(c, 1), :]
        hit = rows == own
        one_hot = jnp.where(hit, 1.0, 0.0).astype(BF16)
        counted = mm(one_hot, prefix)
        rank = jnp.sum(jnp.where(hit, counted[:, :128] + base, 0.0), axis=0, keepdims=True)
        rank = rank.astype(jnp.int32)
        pos_ref[pl.ds(c, 1), :] = own * ROWS + rank
        place = jnp.where(rows == rank + lane_offset, 1.0, 0.0).astype(BF16)
        coarse = jnp.where(hit, (ids >> 4).astype(F32), 0.0)
        fine = jnp.where(hit, (ids & 15).astype(F32), 0.0)
        both = jnp.concatenate([coarse, fine], axis=0).astype(BF16)
        acc_s[...] += lax.dot_general(
            both, place, (((1,), (1,)), ((), ())), preferred_element_type=F32
        )
        return base + counted[:, 128:]

    lax.fori_loop(0, tile.shape[0], chunk, jnp.zeros((128, 128), F32), unroll=4)
    ids_ref[...] = acc_s[:128] * 16.0 + acc_s[128:]


def route(tile, info):
    return call(
        route_kernel,
        "route",
        (jax.ShapeDtypeStruct((32, 128), jnp.int32), array(128, 128)),
        [VM, SM],
        [
            pltpu.VMEM((32, 128), jnp.int32),
            pltpu.VMEM((32, 128), jnp.int32),
            pltpu.VMEM((256, 128), F32),
        ],
    )(tile, info)


def pack_kernel(pos_ref, data_ref, ids_ref, out_ref):
    step = 16

    def body(b, carry):
        start = pl.multiple_of(b * step, step)
        block = data_ref[pl.ds(start, step), :]
        row = b // (128 // step)
        lane = (b % (128 // step)) * step
        for j in range(step):
            out_ref[pl.ds(pos_ref[row, lane + j], 1), :] = block[j : j + 1]
        return carry

    lax.fori_loop(0, 4096 // step, body, 0)

    def tail(b, carry):
        start = pl.multiple_of(b * 8, 8)
        block = ids_ref[pl.ds(start, 8), :]
        for j in range(8):
            out_ref[pl.ds((start + j) * ROWS + CAP, 1), :] = block[j : j + 1]
        return carry

    lax.fori_loop(0, DEVICES // 8, tail, 0)


def pack(pos, data, ids):
    return call(pack_kernel, "pack", array(DEVICES * ROWS, 128), [SM, VM, VM])(pos, data, ids)


def thin_pair(count):
    matrix = np.zeros((count // 2 + 1, count))
    for i in range(count // 2 + 1):
        for source, weight in ((2 * i - 1, 0.5), (2 * i, 1.0), (2 * i + 1, 0.5)):
            if 0 <= source < count:
                matrix[i, source] = weight
    return matrix


def thin_cycle(length):
    matrix = np.zeros((length, length // 2))
    for i in range(length // 2):
        matrix[2 * i, i] += 1.0
        matrix[(2 * i - 1) % length, i] += 0.5
        matrix[(2 * i + 1) % length, i] += 0.5
    return matrix


def grow_matrix(count, source):
    matrix = np.zeros((count, source))
    for i in range(count):
        if i % 2 == 0:
            matrix[i, i // 2] = 1.0
        else:
            matrix[i, i // 2] = 0.5
            matrix[i, i // 2 + 1] = 0.5
    return matrix


def padded(matrix, rows, columns):
    out = np.zeros((rows, columns))
    out[: matrix.shape[0], : matrix.shape[1]] = matrix
    return out


def twice(matrix):
    return np.kron(np.eye(2), matrix)


def plain(matrix):
    return np.asarray(matrix, np.float32).astype(BF16)


def top_rows_matrix():
    rows_x = padded(thin_pair(17), 9, 17)
    rows_y = padded(thin_pair(13), 8, 16)
    rows_y[7] = 0.0
    matrix = np.zeros((2 * TOP_ROWS, 17 * 16))
    for i in range(9):
        for j in range(8):
            line = (j // 2) * 8 + i if i < 8 else 32 + j // 2
            matrix[(j % 2) * TOP_ROWS + line] = np.kron(rows_x[i], rows_y[j])
    return matrix


def exact_left(matrix_ref, value):
    top, rest = halves(value)
    return mm(matrix_ref[...], top) + mm(matrix_ref[...], rest)


def exact_right(value, matrix_ref):
    top, rest = halves(value)
    return mm(top, matrix_ref[...]) + mm(rest, matrix_ref[...])


def collect_kernel(
    in_ref, thin_z_ref, thin_y_ref, top_rows_ref, top_z_ref, *refs
):
    fine_ref, mid_ref, low_ref, high_ref, top_ref, data_s, ids_s, slab_s = refs[-8:]
    for c in range(DEVICES // 4):
        total = None
        for j in range(4):
            base = (c * 4 + j) * ROWS
            top, rest = halves(in_ref[base : base + CAP, :])
            start = (c * 4 + j) * CAP
            data_s[start : start + CAP, :128] = top
            data_s[start : start + CAP, 128:] = rest
            line = in_ref[base + CAP : base + CAP + 1, :]
            total = line if total is None else total + line
        ids_s[c : c + 1, :] = total.astype(jnp.int32)
    rows = lax.broadcasted_iota(jnp.int32, (256, 128), 0)

    def block(b, carry):
        first = pl.multiple_of(b * 256, 256)
        acc = jnp.zeros((256, 256), F32)
        for k in range(16):
            parts = []
            for q in range(2):
                ids = ids_s[2 * k + q : 2 * k + q + 1, :] - first
                parts.append(jnp.where(rows == ids, 1.0, 0.0).astype(BF16))
            acc = acc + mm(jnp.concatenate(parts, axis=1), data_s[k * 256 : (k + 1) * 256, :])
        fine_ref[pl.ds(first, 256), :] = acc[:, :128] + acc[:, 128:]
        return carry

    lax.fori_loop(0, 6, block, 0)
    for i in range(17):
        total = None
        for x, weight in ((2 * i, 1.0), (2 * i - 1, 0.5), (2 * i + 1, 0.5)):
            if 0 <= x < CX:
                term = jnp.concatenate(
                    [
                        fine_ref[h * CX * CY + x * CY : h * CX * CY + (x + 1) * CY, :]
                        for h in range(2)
                    ],
                    axis=1,
                )
                term = term if weight == 1.0 else weight * term
                total = term if total is None else total + term
        slab_s[i * CY : (i + 1) * CY, :] = total
    slab_s[17 * CY :, :] = jnp.zeros((7 * CY, NZ), F32)
    for g in range(3):
        part = exact_right(slab_s[g * 192 : (g + 1) * 192, :], thin_z_ref)
        mid_ref[g * 128 : (g + 1) * 128, :] = exact_left(thin_y_ref, part)
    stacked = exact_left(top_rows_ref, mid_ref[: 17 * 16, :])
    pair = jnp.concatenate([stacked[:TOP_ROWS], stacked[TOP_ROWS:]], axis=1)
    top_charge = exact_right(pair, top_z_ref)
    for s in range(SIZE_X):
        top_ref[s * TOP_ROWS : (s + 1) * TOP_ROWS, :] = top_charge
    for h in range(2):
        for c in range(4):
            at = slice((h * 4 + c) * CX, (h * 4 + c + 1) * CX)
            low_ref[at, :] = fine_ref[pl.ds(h * CX * CY + c, CX, stride=CY), :]
            high_ref[at, :] = fine_ref[pl.ds(h * CX * CY + CY - 4 + c, CX, stride=CY), :]
    for j in range(5):
        at = slice(256 + j * 24, 256 + (j + 1) * 24)
        low_ref[at, :] = mid_ref[pl.ds(j, 24, stride=16), :]
        high_ref[at, :] = mid_ref[pl.ds(8 + j, 24, stride=16), :]


def collect(arrived, *after):
    tables = (
        plain(thin_cycle(NZ)),
        plain(np.kron(np.eye(8), padded(thin_pair(CY), 16, CY))),
        plain(top_rows_matrix()),
        plain(twice(thin_cycle(128))),
    )
    return call(
        collect_kernel,
        "collect",
        (
            array(2 * CX * CY, 128),
            array(24 * 16, 128),
            array(SEND, 128),
            array(SEND, 128),
            array(SIZE_X * TOP_ROWS, 128),
        ),
        [VM] * 5 + [ANY] * len(after),
        [
            pltpu.VMEM((DEVICES * CAP, 256), BF16),
            pltpu.VMEM((DEVICES // 4, 128), jnp.int32),
            pltpu.VMEM((24 * CY, NZ), F32),
        ],
    )(arrived, *tables, *after)


def merge_kernel(fine_ref, mid_ref, before_ref, behind_ref, near_ref, wide_ref, low_ref, high_ref):
    for n in range(2 * CX):
        near_ref[n * YD : n * YD + CY, :] = fine_ref[n * CY : (n + 1) * CY, :]
    for h in range(2):
        for c in range(4):
            at = slice((h * 4 + c) * CX, (h * 4 + c + 1) * CX)
            start = h * CX * YD + CY + c
            near_ref[pl.ds(start, CX, stride=YD), :] = behind_ref[at, :]
            near_ref[pl.ds(start + 4, CX, stride=YD), :] = before_ref[at, :]
    for i in range(24):
        wide_ref[i * YD : i * YD + 16, :] = mid_ref[i * 16 : (i + 1) * 16, :]
        wide_ref[i * YD + 16 : (i + 1) * YD, :] = jnp.zeros((16, 128), F32)
    for j in range(5):
        at = slice(256 + j * 24, 256 + (j + 1) * 24)
        behind = behind_ref[at, :]
        if j == 0:
            behind = behind + wide_ref[pl.ds(12, 24, stride=YD), :]
        wide_ref[pl.ds(12 + j, 24, stride=YD), :] = behind
        before = before_ref[at, :]
        row = 28 + j if j < 4 else 0
        if j == 4:
            before = before + wide_ref[pl.ds(0, 24, stride=YD), :]
        wide_ref[pl.ds(row, 24, stride=YD), :] = before
    for ref, first, mid_first in ((low_ref, 0, 0), (high_ref, CX - 4, 12)):
        for h in range(2):
            base = (h * CX + first) * YD
            ref[h * 128 : (h + 1) * 128, :] = near_ref[base : base + 128, :]
        for i in range(5):
            base = (mid_first + i) * YD
            at = 256 + i * 24
            ref[at : at + 16, :] = wide_ref[base : base + 16, :]
            ref[at + 16 : at + 24, :] = (
                wide_ref[base + 16 : base + 24, :] + wide_ref[base + 24 : base + 32, :]
            )


def merge(fine, mid, before, behind):
    return call(
        merge_kernel,
        "merge",
        (array(2 * CX * YD, 128), array(24 * YD, 128), array(SEND, 128), array(SEND, 128)),
        [VM] * 4,
    )(fine, mid, before, behind)


def z_matrices(period, copies):
    half = period // 2
    z = np.arange(period)[:, None]
    f = np.arange(half)[None, :]
    angle = 2 * np.pi * ((z * f) % period) / period
    cosine, sine = np.cos(angle), -np.sin(angle)
    sine[:, 0] = (-1.0) ** np.arange(period)
    scale = np.full((half, 1), 2.0 / period)
    scale[0] = 1.0 / period
    forward = np.zeros((256, 256))
    inverse = np.zeros((256, 256))
    for c in range(copies):
        rows = slice(c * period, (c + 1) * period)
        real = slice(c * half, (c + 1) * half)
        imag = slice(128 + c * half, 128 + (c + 1) * half)
        forward[rows, real] = cosine
        forward[rows, imag] = sine
        inverse[real, rows] = scale * cosine.T
        inverse[imag, rows] = scale * sine.T
    return forward, inverse


def y_matrices():
    order = np.concatenate([np.arange(17), np.arange(31, 16, -1)])
    y = np.arange(YD)
    angle = 2 * np.pi * ((order[:, None] * y[None, :]) % YD) / YD
    cosine, sine = np.cos(angle), np.sin(angle)
    forward = np.block([[cosine, sine], [-sine, cosine]])
    inverse = np.block([[cosine.T, -sine.T], [sine.T, cosine.T]]) / YD
    return np.kron(np.eye(4), forward), np.kron(np.eye(4), inverse)


def stacked_rows(matrix):
    top, rest = np_halves(matrix)
    return np.concatenate([top, rest], axis=0)


def stacked_cols(matrix):
    top, rest = np_halves(matrix)
    return np.concatenate([top, rest], axis=1)


def right_product(value, matrix_ref):
    top, rest = halves(value)
    return (
        mm(top, matrix_ref[:256, :]) + mm(top, matrix_ref[256:, :]) + mm(rest, matrix_ref[:256, :])
    )


def left_product(matrix_ref, value):
    top, rest = halves(value)
    return (
        mm(matrix_ref[:, :256], top) + mm(matrix_ref[:, 256:], top) + mm(matrix_ref[:, :256], rest)
    )


def special_mask(copies, rows):
    lane = lax.broadcasted_iota(jnp.int32, (rows, 128), 1)
    row = lax.broadcasted_iota(jnp.int32, (rows, 128), 0)
    return (lane & (128 // copies - 1)) == 0, row


def forward_chunk(value, z_ref, y_ref, copies):
    z_freq = right_product(value, z_ref)
    stacks = []
    for h in range(2):
        pieces = []
        for q in range(4):
            slab = z_freq[(h * 4 + q) * YD : (h * 4 + q + 1) * YD]
            pieces += [slab[:, :128], slab[:, 128:]]
        stacks.append(jnp.concatenate(pieces, axis=0))
    freq = left_product(y_ref, jnp.concatenate(stacks, axis=1))
    lane_special, row = special_mask(copies, 16)
    special = lane_special & (row != 0)
    slabs = []
    for h in range(2):
        for q in range(4):
            slab = freq[q * 64 : (q + 1) * 64, h * 128 : (h + 1) * 128]
            ar, br, ai, bi = slab[:16], slab[16:32], slab[32:48], slab[48:]
            slabs.append(
                jnp.concatenate(
                    [
                        jnp.where(special, 0.5 * (ar + br), ar),
                        jnp.where(special, 0.5 * (ai + bi), br),
                        jnp.where(special, 0.5 * (ai - bi), ai),
                        jnp.where(special, 0.5 * (br - ar), bi),
                    ],
                    axis=0,
                )
            )
    return slabs


def inverse_chunk(slabs, z_ref, y_ref):
    stacks = [jnp.concatenate(slabs[h * 4 : h * 4 + 4], axis=0) for h in range(2)]
    space = left_product(y_ref, jnp.concatenate(stacks, axis=1))
    rows = []
    for h in range(2):
        for q in range(4):
            slab = space[q * 64 : (q + 1) * 64, h * 128 : (h + 1) * 128]
            rows.append(jnp.concatenate([slab[:YD], slab[YD:]], axis=1))
    return right_product(jnp.concatenate(rows, axis=0), z_ref)


def taps_kernel(copies, in_ref, z_ref, y_ref, after_ref, real_ref, twin_ref, imag_ref):
    lane_special, row = special_mask(copies, YD)
    special = lane_special & ((row == 0) | (row == 16))
    for p in range(2):
        slabs = forward_chunk(in_ref[p * 256 : (p + 1) * 256, :], z_ref, y_ref, copies)
        for j in range(8):
            dx = p * 8 + j
            if dx > 8:
                break
            real, imag = slabs[j][:YD], slabs[j][YD:]
            at = slice(dx * YD, (dx + 1) * YD)
            real_ref[at, :] = real
            twin_ref[at, :] = jnp.where(special, imag, real)
            imag_ref[at, :] = jnp.where(special, 0.0, imag)


def taps(kernel, copies, z_matrix, y_matrix, after):
    flipped = kernel[:, ::-1, ::-1]
    tall = jnp.concatenate(
        [flipped[:, 4:], jnp.zeros((9, YD - 9, 9), F32), flipped[:, :4]], axis=1
    )
    period = 256 // copies
    wide = jnp.concatenate(
        [tall[:, :, 4:], jnp.zeros((9, YD, period - 9), F32), tall[:, :, :4]], axis=2
    )
    wide = jnp.concatenate([wide] * copies, axis=2)
    wide = jnp.concatenate([wide, jnp.zeros((7, YD, 256), F32)], axis=0)
    return call(
        functools.partial(taps_kernel, copies),
        f"taps{copies}",
        (array(9 * YD, 128),) * 3,
        [VM] * 3 + [ANY],
    )(wide.reshape(16 * YD, 256), z_matrix, y_matrix, after)


def own_kernel(in_ref, z_ref, y_ref, out_ref):
    for p in range(CX // 8):
        value = jnp.concatenate(
            [in_ref[h * CX * YD + p * 256 : h * CX * YD + (p + 1) * 256, :] for h in range(2)], axis=1
        )
        slabs = forward_chunk(value, z_ref, y_ref, 1)
        for j in range(8):
            out_ref[(p * 8 + j) * 64 : (p * 8 + j + 1) * 64, :] = slabs[j]


def convolve(copies, block_out, blocks, spectrum, freq_s, conv_s):
    real_ref, twin_ref, imag_ref = spectrum
    lane_special, row = special_mask(copies, 8)

    def step(index, carry):
        v = index % 2
        first = (index // 2) * block_out
        sums = [[None] * 4 for _ in range(block_out)]
        for dx in range(9):
            coefs = []
            for half in range(2):
                at = pl.ds(pl.multiple_of(dx * YD + half * 16 + v * 8, 8), 8)
                coefs.append((real_ref[at, :], twin_ref[at, :], imag_ref[at, :]))
            for j in range(block_out):
                base = (first + j + dx) * 64 + v * 8
                for half in range(2):
                    at = pl.multiple_of(base + half * 16, 8)
                    re = freq_s[pl.ds(at, 8), :]
                    im = freq_s[pl.ds(pl.multiple_of(at + 32, 8), 8), :]
                    a, t, b = coefs[half]
                    new_re = a * re - b * im
                    new_im = b * re + t * im
                    old = sums[j]
                    old[2 * half] = new_re if dx == 0 else old[2 * half] + new_re
                    old[2 * half + 1] = new_im if dx == 0 else old[2 * half + 1] + new_im
        special = lane_special & ((row != 0) | (v != 0))
        for j in range(block_out):
            ar, ai, br, bi = sums[j]
            base = (first + j) * 64 + v * 8
            values = (
                jnp.where(special, ar - bi, ar),
                jnp.where(special, ar + bi, br),
                jnp.where(special, ai + br, ai),
                jnp.where(special, br - ai, bi),
            )
            for part in range(4):
                conv_s[pl.ds(pl.multiple_of(base + part * 16, 8), 8), :] = values[part]
        return carry

    lax.fori_loop(0, 2 * blocks, step, 0)


def wide_slab(ref, index):
    at = 256 + index * 24
    last = ref[at + 16 : at + 24, :]
    row = lax.broadcasted_iota(jnp.int32, (8, 128), 0)
    return jnp.concatenate(
        [ref[at : at + 16, :], jnp.where(row < 4, last, 0.0), jnp.where(row < 4, 0.0, last)], axis=0
    )


def levels_kernel(
    own_ref, before_ref, behind_ref, wide_ref,
    nr_ref, nt_ref, ni_ref, mr_ref, mt_ref, mi_ref,
    zf_ref, yf_ref, zi_ref, yi_ref, mzf_ref, mzi_ref,
    near_ref, mid_ref, freq_s, conv_s, mid_freq_s, mid_conv_s,
):
    freq_s[4 * 64 : 36 * 64, :] = own_ref[...]
    edges = [
        jnp.concatenate([ref[:128, :], ref[128:256, :]], axis=1) for ref in (before_ref, behind_ref)
    ]
    slabs = forward_chunk(jnp.concatenate(edges, axis=0), zf_ref, yf_ref, 1)
    for j in range(8):
        at = j if j < 4 else 32 + j
        freq_s[at * 64 : (at + 1) * 64, :] = slabs[j]
    zero = jnp.zeros((YD, 128), F32)
    for p in range(3):
        pairs = []
        for j in range(8):
            pair = []
            for n in (p * 8 + j, p * 8 + j + 9):
                if n > 24 or (n == p * 8 + j and n > 16):
                    slab = zero
                elif n < 4:
                    slab = wide_slab(before_ref, n)
                elif n > 20:
                    slab = wide_slab(behind_ref, n - 20)
                else:
                    slab = wide_ref[(n - 4) * YD : (n - 3) * YD, :]
                    if n == 4:
                        slab = slab + wide_slab(before_ref, 4)
                    if n == 20:
                        slab = slab + wide_slab(behind_ref, 0)
                pair.append(slab)
            pairs.append(jnp.concatenate(pair, axis=1))
        slabs = forward_chunk(jnp.concatenate(pairs, axis=0), mzf_ref, yf_ref, 2)
        for j in range(8):
            at = p * 8 + j
            mid_freq_s[at * 64 : (at + 1) * 64, :] = slabs[j]
    convolve(1, 8, 4, (nr_ref, nt_ref, ni_ref), freq_s, conv_s)
    for p in range(4):
        slabs = [conv_s[(p * 8 + j) * 64 : (p * 8 + j + 1) * 64, :] for j in range(8)]
        space = inverse_chunk(slabs, zi_ref, yi_ref)
        for j in range(8):
            x = p * 8 + j
            near_ref[x * CY : (x + 1) * CY, :] = space[j * YD : j * YD + CY]
    convolve(2, 9, 1, (mr_ref, mt_ref, mi_ref), mid_freq_s, mid_conv_s)
    mid_conv_s[9 * 64 :, :] = jnp.zeros((7 * 64, 128), F32)
    for p in range(2):
        slabs = [mid_conv_s[(p * 8 + j) * 64 : (p * 8 + j + 1) * 64, :] for j in range(8)]
        space = inverse_chunk(slabs, mzi_ref, yi_ref)
        for j in range(8):
            i = p * 8 + j
            if i < 9:
                mid_ref[i * 16 : (i + 1) * 16, :] = space[j * YD : j * YD + 16]


def gauss(index, period, width):
    distance = jnp.minimum(index, period - index).astype(F32)
    return jnp.exp(-(distance * distance) / (width * width))


def top_kernel(in_ref, weights_ref, widths_ref, info_ref, out_ref, plane_s, depth_s):
    first_x = info_ref[2] * 8
    first_y = info_ref[3] * 6
    row = lax.broadcasted_iota(jnp.int32, (16, 256), 0)
    column = lax.broadcasted_iota(jnp.int32, (16, 256), 1)
    source = jnp.where(column < 128, column, (column - 128) * 8 + 8)
    offset = (first_x + row - source) & 127
    parts = [
        jnp.where(column < 144, gauss(offset, 128, widths_ref[k]), 0.0) for k in range(4)
    ]
    left = halves(jnp.concatenate(parts, axis=0))
    for jp in range(4):
        tiles = [in_ref[s * TOP_ROWS + jp * 8 : s * TOP_ROWS + jp * 8 + 8, :] for s in range(16)]
        tiles.append(in_ref[pl.ds(32 + jp, SIZE_X, stride=TOP_ROWS), :])
        tiles.append(jnp.zeros((112, 128), F32))
        right = halves(jnp.concatenate(tiles, axis=0))
        plane = mm(left[0], right[0]) + mm(left[0], right[1]) + mm(left[1], right[0])
        for k in range(4):
            plane_s[(k * 4 + jp) * 16 : (k * 4 + jp + 1) * 16, :] = plane[k * 16 : (k + 1) * 16]
    row = lax.broadcasted_iota(jnp.int32, (128, 128), 0)
    column = lax.broadcasted_iota(jnp.int32, (128, 128), 1)
    for k in range(4):
        weight = gauss((row - column) & 63, 64, widths_ref[k]) * weights_ref[k]
        weight = halves(jnp.where((row >> 6) == (column >> 6), weight, 0.0))
        value = halves(plane_s[k * 64 : (k + 1) * 64, :])
        depth_s[k * 64 : (k + 1) * 64, :] = (
            mm(value[0], weight[0]) + mm(value[0], weight[1]) + mm(value[1], weight[0])
        )
    lane = lax.broadcasted_iota(jnp.int32, (16, 128), 1)
    tiles = []
    for ip in range(5):
        first = depth_s[pl.ds(2 * ip, 16, stride=16), :]
        second = depth_s[pl.ds(2 * ip + 1, 16, stride=16), :]
        even = jnp.where(lane < 64, first, pltpu.roll(second, 64, 1))
        odd = jnp.where(lane < 64, pltpu.roll(first, 64, 1), second)
        tiles.append(jnp.concatenate([even, odd, jnp.zeros((96, 128), F32)], axis=0))
    right = halves(jnp.concatenate(tiles, axis=1))
    row = lax.broadcasted_iota(jnp.int32, (64, 128), 0)
    column = lax.broadcasted_iota(jnp.int32, (64, 128), 1)
    target = (row >> 3) * 6 + (row & 7)
    source = first_y + (column & 3) * 2 + ((column >> 4) & 1)
    offset = target - source
    offset = jnp.where(offset < 0, offset + 48, offset)
    offset = jnp.where(offset >= 48, offset - 48, offset)
    chosen = (column >> 2) & 3
    left = jnp.zeros((64, 128), F32)
    for k in range(4):
        left = jnp.where(chosen == k, gauss(offset, 48, widths_ref[k]), left)
    left = halves(jnp.where(column < 32, left, 0.0))
    out_ref[...] = mm(left[0], right[0]) + mm(left[0], right[1]) + mm(left[1], right[0])


def finish_kernel(near_ref, mid_ref, top_ref, grow_top_ref, grow_y_ref, grow_z_ref, grow_fine_ref, out_ref, grown_s):
    total = top_ref[:8, :]
    for s in range(1, SIZE_Y):
        total = total + top_ref[s * 8 : (s + 1) * 8, :]
    lanes = []
    for ip in range(5):
        lanes.append(exact_right(total[:, ip * 128 : (ip + 1) * 128], grow_top_ref))
    deep = jnp.concatenate(lanes, axis=1)
    tiles = []
    for i in range(17):
        tile = deep[:, (i // 2) * 128 : (i // 2 + 1) * 128]
        if i % 2:
            tile = 0.5 * (tile + deep[:, (i // 2 + 1) * 128 : (i // 2 + 2) * 128])
        tiles.append(tile)
    flat = jnp.concatenate(tiles, axis=1)
    flat = jnp.concatenate([flat, jnp.zeros((120, 17 * 128), F32)], axis=0)
    tall = exact_left(grow_y_ref, flat)
    slabs = []
    for i in range(24):
        if i > 16:
            slabs.append(jnp.zeros((16, 128), F32))
            continue
        h = i // 9
        slabs.append(
            tall[:, i * 128 : (i + 1) * 128]
            + mid_ref[(i - 9 * h) * 16 : (i - 9 * h + 1) * 16, h * 128 : (h + 1) * 128]
        )
    for g in range(3):
        part = exact_right(jnp.concatenate(slabs[g * 8 : (g + 1) * 8], axis=0), grow_z_ref)
        grown_s[g * 192 : (g + 1) * 192, :] = exact_left(grow_fine_ref, part)
    for x in range(CX):
        at = slice(x * CY, (x + 1) * CY)
        i = x // 2
        value = grown_s[i * CY : (i + 1) * CY, :]
        if x % 2:
            value = 0.5 * (value + grown_s[(i + 1) * CY : (i + 2) * CY, :])
        out_ref[at, :] = near_ref[at, :] + value


def swap(to_low, to_high, axis):
    count = lax.axis_size(axis)
    forward = [(i, (i + 1) % count) for i in range(count)]
    backward = [(target, source) for source, target in forward]
    return lax.ppermute(to_high, axis, forward), lax.ppermute(to_low, axis, backward)


def on_device(
    charge_blocks, block_tile, block_count, near_kernel, mid_kernel, top_weights, top_widths
):
    at_x = lax.axis_index("gx")
    at_y = lax.axis_index("gy")
    info = jnp.stack(
        [block_count[0], ((at_x * SIZE_Y + at_y) % 4) * CAP, at_x, at_y]
    ).astype(jnp.int32)
    pos, ids = route(block_tile.reshape(32, 128), info)
    outgoing = pack(pos, charge_blocks, ids)
    arrived = lax.all_to_all(
        outgoing.reshape(DEVICES, ROWS, 1, 128),
        ("gx", "gy"),
        split_axis=0,
        concat_axis=0,
        tiled=True,
    ).reshape(DEVICES * ROWS, 128)

    z_fine, z_fine_back = z_matrices(256, 1)
    z_mid, z_mid_back = z_matrices(128, 2)
    y_forward, y_back = y_matrices()
    zf, yf = stacked_rows(z_fine), stacked_cols(y_forward)
    zi, yi = stacked_rows(z_fine_back), stacked_cols(y_back)
    mzf, mzi = stacked_rows(z_mid), stacked_rows(z_mid_back)
    near_taps = taps(near_kernel, 1, zf, yf, outgoing)
    mid_taps = taps(mid_kernel, 2, mzf, yf, outgoing)

    fine, mid, low, high, top = collect(arrived, *near_taps, *mid_taps)
    before, behind = swap(low, high, "gy")
    tops = lax.all_to_all(
        top.reshape(SIZE_X, TOP_ROWS, 128), "gx", split_axis=0, concat_axis=0, tiled=True
    ).reshape(SIZE_X * TOP_ROWS, 128)
    partial = call(
        top_kernel,
        "top",
        array(64, 640),
        [VM, SM, SM, SM],
        [pltpu.VMEM((256, 128), F32), pltpu.VMEM((256, 128), F32)],
    )(tops, top_weights, top_widths, info)
    partial = lax.all_to_all(
        partial.reshape(SIZE_Y, 8, 640), "gy", split_axis=0, concat_axis=0, tiled=True
    ).reshape(64, 640)
    near_rows, wide, low, high = merge(fine, mid, before, behind)
    before, behind = swap(low, high, "gx")
    own = call(own_kernel, "own", array(CX * 64, 128), [VM] * 3)(near_rows, zf, yf)
    near, mid_near = call(
        levels_kernel,
        "levels",
        (array(CX * CY, NZ), array(9 * 16, 256)),
        [VM] * 16,
        [
            pltpu.VMEM((40 * 64, 128), F32),
            pltpu.VMEM((32 * 64, 128), F32),
            pltpu.VMEM((24 * 64, 128), F32),
            pltpu.VMEM((16 * 64, 128), F32),
        ],
    )(own, before, behind, wide, *near_taps, *mid_taps, zf, yf, zi, yi, mzf, mzi)
    grow_z = grow_matrix(2 * 64, 65)
    grow_z[:, 0] += grow_z[:, 64]
    grow_fine_z = grow_matrix(2 * 128, 129)
    grow_fine_z[:, 0] += grow_fine_z[:, 128]
    out = call(
        finish_kernel, "finish", array(CX * CY, NZ), [VM] * 7, [pltpu.VMEM((24 * CY, NZ), F32)]
    )(
        near,
        mid_near,
        partial,
        plain(twice(grow_z[:, :64].T)),
        plain(padded(grow_matrix(13, 7), 16, 128)),
        plain(grow_fine_z[:, :128].T),
        plain(np.kron(np.eye(8), padded(grow_matrix(CY, 13), CY, 16))),
    )
    return out.reshape(CX, CY, NZ)


def solution(mesh):
    placed = (P(("gx", "gy"), None), P(("gx", "gy")), P(("gx", "gy")), P(), P(), P(), P())
    return jax.shard_map(
        on_device, mesh=mesh, in_specs=placed, out_specs=P("gx", "gy", None), check_vma=False
    )
```

```python
import functools

import jax
import jax.numpy as jnp
import numpy as np
from jax import lax
from jax.experimental import pallas as pl
from jax.experimental.pallas import tpu as pltpu
from jax.sharding import PartitionSpec as P

CX = 32
CY = 24
NZ = 256
CAP = 32
DEVICES = 128
ROWS = CAP + 1
SIZE_X = 16
SIZE_Y = 8
DEAD = 2047
SEND = 376
TOP_ROWS = 40
YD = 32
F32 = jnp.float32
BF16 = jnp.bfloat16
VM = pl.BlockSpec(memory_space=pltpu.VMEM)
SM = pl.BlockSpec(memory_space=pltpu.SMEM)
HB = pl.BlockSpec(memory_space=pltpu.HBM)


def call(body, name, out, ins, scratch=(), limit=20, flops=0, moved=0, outs=VM):
    many = isinstance(out, tuple)
    outs = outs if isinstance(outs, tuple) else (outs,) * (len(out) if many else 1)
    shapes = tuple(
        pltpu.HBM(shape.shape, shape.dtype) if spec is HB else shape
        for shape, spec in zip(out if many else (out,), outs)
    )
    kernel = pl.pallas_call(
        body,
        out_shape=shapes if many else shapes[0],
        in_specs=ins,
        out_specs=outs if many else outs[0],
        scratch_shapes=list(scratch),
        compiler_params=pltpu.CompilerParams(vmem_limit_bytes=limit << 20),
        cost_estimate=pl.CostEstimate(flops=flops, bytes_accessed=moved, transcendentals=0),
        name=name,
    )

    def run(*args):
        placed = [
            pltpu.with_memory_space_constraint(jnp.asarray(arg), pltpu.HBM) if spec is HB else arg
            for arg, spec in zip(args, ins)
        ]
        return kernel(*placed)

    return run


def started(pairs, sems, first=0):
    copies = []
    for n, (source, target) in enumerate(pairs):
        copy = pltpu.make_async_copy(source, target, sems.at[first + n])
        copy.start()
        copies.append(copy)
    return copies


def buffers(*tables):
    return [pltpu.VMEM(table.shape, table.dtype) for table in tables]


def array(*shape):
    return jax.ShapeDtypeStruct(shape, F32)


def mm(a, b):
    return jnp.dot(a, b, preferred_element_type=F32)


def halves(value):
    top = value.astype(BF16)
    return top, (value - top.astype(F32)).astype(BF16)


def np_halves(matrix):
    matrix = np.asarray(matrix, np.float32)
    top = matrix.astype(BF16)
    return top, (matrix - top.astype(np.float32)).astype(BF16)


def send_kernel(
    tile_ref, info_ref, data_ref, out_ref, data_s, out_s, pos_ref, pos_s, owner_s, code_s, acc_s, sems
):
    (data_copy,) = started([(data_ref, data_s)], sems)
    tile = tile_ref[...]
    column = tile >> 1
    high_part = column >> 6
    grid_x = (high_part * 43691) >> 17
    grid_y = column - grid_x * (CY * SIZE_Y)
    owner_y = ((grid_y >> 3) * 43) >> 7
    owner = (grid_x >> 5) * SIZE_Y + owner_y
    cell = (tile & 1) * (CX * CY) + (grid_x & (CX - 1)) * CY + (grid_y - owner_y * CY)
    slot = lax.broadcasted_iota(jnp.int32, tile.shape, 0) * 128 + lax.broadcasted_iota(
        jnp.int32, tile.shape, 1
    )
    code = jnp.where(slot < info_ref[0], cell, DEAD)
    owner_s[...] = owner
    code_s[...] = code
    lane_offset = info_ref[1]
    rows = lax.broadcasted_iota(jnp.int32, (128, 128), 0)
    before = lax.broadcasted_iota(jnp.int32, (128, 256), 0)
    after = lax.broadcasted_iota(jnp.int32, (128, 256), 1)
    prefix = jnp.where((before < after) | (after >= 128), 1.0, 0.0).astype(BF16)
    acc_s[...] = jnp.zeros_like(acc_s)

    def chunk(c, base):
        own = owner_s[pl.ds(c, 1), :]
        ids = code_s[pl.ds(c, 1), :]
        hit = rows == own
        one_hot = jnp.where(hit, 1.0, 0.0).astype(BF16)
        counted = mm(one_hot, prefix)
        rank = jnp.sum(jnp.where(hit, counted[:, :128] + base, 0.0), axis=0, keepdims=True)
        rank = rank.astype(jnp.int32)
        pos_ref[pl.ds(c, 1), :] = own * ROWS + rank
        place = jnp.where(rows == rank + lane_offset, 1.0, 0.0).astype(BF16)
        coarse = jnp.where(hit, (ids >> 4).astype(F32), 0.0)
        fine = jnp.where(hit, (ids & 15).astype(F32), 0.0)
        both = jnp.concatenate([coarse, fine], axis=0).astype(BF16)
        acc_s[...] += lax.dot_general(
            both, place, (((1,), (1,)), ((), ())), preferred_element_type=F32
        )
        return base + counted[:, 128:]

    lax.fori_loop(0, tile.shape[0], chunk, jnp.zeros((128, 128), F32), unroll=4)
    (pos_copy,) = started([(pos_ref, pos_s)], sems, 1)
    for b in range(DEVICES // 8):
        ids = acc_s[b * 8 : b * 8 + 8, :] * 16.0 + acc_s[128 + b * 8 : 136 + b * 8, :]
        for j in range(8):
            at = (b * 8 + j) * ROWS + CAP
            out_s[at : at + 1, :] = ids[j : j + 1]
    pos_copy.wait()
    data_copy.wait()

    def body(c, carry):
        for g in range(16):
            block = data_s[pl.ds(pl.multiple_of(c * 128 + g * 8, 8), 8), :]
            for j in range(8):
                out_s[pl.ds(pos_s[c, g * 8 + j], 1), :] = block[j : j + 1]
        return carry

    lax.fori_loop(0, 32, body, 0)
    (out_copy,) = started([(out_s, out_ref)], sems, 2)
    out_copy.wait()


def send(tile, info, data):
    return call(
        send_kernel,
        "send",
        array(DEVICES * ROWS, 128),
        [VM, SM, HB],
        [
            pltpu.VMEM((4096, 128), F32),
            pltpu.VMEM((DEVICES * ROWS, 128), F32),
            pltpu.VMEM((32, 128), jnp.int32),
            pltpu.SMEM((32, 128), jnp.int32),
            pltpu.VMEM((32, 128), jnp.int32),
            pltpu.VMEM((32, 128), jnp.int32),
            pltpu.VMEM((256, 128), F32),
            pltpu.SemaphoreType.DMA((3,)),
        ],
        outs=HB,
    )(tile, info, data)


def thin_pair(count):
    matrix = np.zeros((count // 2 + 1, count))
    for i in range(count // 2 + 1):
        for source, weight in ((2 * i - 1, 0.5), (2 * i, 1.0), (2 * i + 1, 0.5)):
            if 0 <= source < count:
                matrix[i, source] = weight
    return matrix


def thin_cycle(length):
    matrix = np.zeros((length, length // 2))
    for i in range(length // 2):
        matrix[2 * i, i] += 1.0
        matrix[(2 * i - 1) % length, i] += 0.5
        matrix[(2 * i + 1) % length, i] += 0.5
    return matrix


def grow_matrix(count, source):
    matrix = np.zeros((count, source))
    for i in range(count):
        if i % 2 == 0:
            matrix[i, i // 2] = 1.0
        else:
            matrix[i, i // 2] = 0.5
            matrix[i, i // 2 + 1] = 0.5
    return matrix


def padded(matrix, rows, columns):
    out = np.zeros((rows, columns))
    out[: matrix.shape[0], : matrix.shape[1]] = matrix
    return out


def twice(matrix):
    return np.kron(np.eye(2), matrix)


def plain(matrix):
    return np.asarray(matrix, np.float32).astype(BF16)


def top_rows_matrix():
    rows_x = padded(thin_pair(17), 9, 17)
    rows_y = padded(thin_pair(13), 8, 16)
    rows_y[7] = 0.0
    matrix = np.zeros((2 * TOP_ROWS, 17 * 16))
    for i in range(9):
        for j in range(8):
            line = (j // 2) * 8 + i if i < 8 else 32 + j // 2
            matrix[(j % 2) * TOP_ROWS + line] = np.kron(rows_x[i], rows_y[j])
    return matrix


def exact_left(matrix_ref, value):
    top, rest = halves(value)
    return mm(matrix_ref[...], top) + mm(matrix_ref[...], rest)


def exact_right(value, matrix_ref):
    top, rest = halves(value)
    return mm(top, matrix_ref[...]) + mm(rest, matrix_ref[...])


def collect_kernel(in_ref, *refs):
    tables = refs[:4]
    outs = refs[-18:-13]
    data_s, ids_s, slab_s = refs[-13:-10]
    thin_z_ref, thin_y_ref, top_rows_ref, top_z_ref = refs[-10:-6]
    fine_ref, mid_ref, low_ref, high_ref, top_ref, sems = refs[-6:]
    table_copies = started(list(zip(tables, refs[-10:-6])), sems)
    for c in range(DEVICES // 4):
        total = None
        for j in range(4):
            base = (c * 4 + j) * ROWS
            top, rest = halves(in_ref[base : base + CAP, :])
            start = (c * 4 + j) * CAP
            data_s[start : start + CAP, :128] = top
            data_s[start : start + CAP, 128:] = rest
            line = in_ref[base + CAP : base + CAP + 1, :]
            total = line if total is None else total + line
        ids_s[c : c + 1, :] = total.astype(jnp.int32)
    rows = lax.broadcasted_iota(jnp.int32, (256, 128), 0)

    def block(b, carry):
        first = pl.multiple_of(b * 256, 256)
        acc = jnp.zeros((256, 256), F32)
        for k in range(16):
            parts = []
            for q in range(2):
                ids = ids_s[2 * k + q : 2 * k + q + 1, :] - first
                parts.append(jnp.where(rows == ids, 1.0, 0.0).astype(BF16))
            acc = acc + mm(jnp.concatenate(parts, axis=1), data_s[k * 256 : (k + 1) * 256, :])
        fine_ref[pl.ds(first, 256), :] = acc[:, :128] + acc[:, 128:]
        return carry

    lax.fori_loop(0, 6, block, 0)
    out_copies = started([(fine_ref, outs[0])], sems, 4)
    for i in range(17):
        total = None
        for x, weight in ((2 * i, 1.0), (2 * i - 1, 0.5), (2 * i + 1, 0.5)):
            if 0 <= x < CX:
                term = jnp.concatenate(
                    [
                        fine_ref[h * CX * CY + x * CY : h * CX * CY + (x + 1) * CY, :]
                        for h in range(2)
                    ],
                    axis=1,
                )
                term = term if weight == 1.0 else weight * term
                total = term if total is None else total + term
        slab_s[i * CY : (i + 1) * CY, :] = total
    slab_s[17 * CY :, :] = jnp.zeros((7 * CY, NZ), F32)
    for copy in table_copies:
        copy.wait()
    for g in range(3):
        part = exact_right(slab_s[g * 192 : (g + 1) * 192, :], thin_z_ref)
        mid_ref[g * 128 : (g + 1) * 128, :] = exact_left(thin_y_ref, part)
    for h in range(2):
        for c in range(4):
            at = slice((h * 4 + c) * CX, (h * 4 + c + 1) * CX)
            low_ref[at, :] = fine_ref[pl.ds(h * CX * CY + c, CX, stride=CY), :]
            high_ref[at, :] = fine_ref[pl.ds(h * CX * CY + CY - 4 + c, CX, stride=CY), :]
    for j in range(5):
        at = slice(256 + j * 24, 256 + (j + 1) * 24)
        low_ref[at, :] = mid_ref[pl.ds(j, 24, stride=16), :]
        high_ref[at, :] = mid_ref[pl.ds(8 + j, 24, stride=16), :]
    out_copies += started([(mid_ref, outs[1]), (low_ref, outs[2]), (high_ref, outs[3])], sems, 5)
    stacked = exact_left(top_rows_ref, mid_ref[: 17 * 16, :])
    pair = jnp.concatenate([stacked[:TOP_ROWS], stacked[TOP_ROWS:]], axis=1)
    top_charge = exact_right(pair, top_z_ref)
    for s in range(SIZE_X):
        top_ref[s * TOP_ROWS : (s + 1) * TOP_ROWS, :] = top_charge
    out_copies += started([(top_ref, outs[4])], sems, 8)
    for copy in out_copies:
        copy.wait()


def collect(arrived, *after):
    tables = (
        plain(thin_cycle(NZ)),
        plain(np.kron(np.eye(8), padded(thin_pair(CY), 16, CY))),
        plain(top_rows_matrix()),
        plain(twice(thin_cycle(128))),
    )
    out = (
        array(2 * CX * CY, 128),
        array(24 * 16, 128),
        array(SEND, 128),
        array(SEND, 128),
        array(SIZE_X * TOP_ROWS, 128),
    )
    return call(
        collect_kernel,
        "collect",
        out,
        [VM] + [HB] * (4 + len(after)),
        [
            pltpu.VMEM((DEVICES * CAP, 256), BF16),
            pltpu.VMEM((DEVICES // 4, 128), jnp.int32),
            pltpu.VMEM((24 * CY, NZ), F32),
            *buffers(*tables),
            *buffers(*out),
            pltpu.SemaphoreType.DMA((9,)),
        ],
        outs=HB,
    )(arrived, *tables, *after)


def merge_kernel(
    fine_hbm, mid_hbm, before_ref, behind_ref, halo_hbm, wide_hbm, low_hbm, high_hbm,
    fine_s, mid_ref, halo_ref, wide_ref, low_ref, high_ref, sems,
):
    pairs = [(mid_hbm, mid_ref)]
    for h in range(2):
        for first, at in ((0, 0), (CX - 4, 4)):
            start = (h * CX + first) * CY
            pairs.append(
                (fine_hbm.at[pl.ds(start, 4 * CY)], fine_s.at[pl.ds((h * 8 + at) * CY, 4 * CY)])
            )
    mid_copy, *fine_copies = started(pairs, sems)
    for h in range(2):
        for c in range(4):
            at = slice((h * 4 + c) * CX, (h * 4 + c + 1) * CX)
            start = h * CX * 8 + c
            halo_ref[pl.ds(start, CX, stride=8), :] = behind_ref[at, :]
            halo_ref[pl.ds(start + 4, CX, stride=8), :] = before_ref[at, :]
    out_copies = started([(halo_ref, halo_hbm)], sems, 5)
    mid_copy.wait()
    for i in range(24):
        wide_ref[i * YD : i * YD + 16, :] = mid_ref[i * 16 : (i + 1) * 16, :]
        wide_ref[i * YD + 16 : (i + 1) * YD, :] = jnp.zeros((16, 128), F32)
    for j in range(5):
        at = slice(256 + j * 24, 256 + (j + 1) * 24)
        behind = behind_ref[at, :]
        if j == 0:
            behind = behind + wide_ref[pl.ds(12, 24, stride=YD), :]
        wide_ref[pl.ds(12 + j, 24, stride=YD), :] = behind
        before = before_ref[at, :]
        row = 28 + j if j < 4 else 0
        if j == 4:
            before = before + wide_ref[pl.ds(0, 24, stride=YD), :]
        wide_ref[pl.ds(row, 24, stride=YD), :] = before
    out_copies += started([(wide_ref, wide_hbm)], sems, 6)
    for copy in fine_copies:
        copy.wait()
    for ref, first, at_fine, mid_first in ((low_ref, 0, 0, 0), (high_ref, CX - 4, 4, 12)):
        for h in range(2):
            for x in range(4):
                at = h * 128 + x * YD
                source = (h * 8 + at_fine + x) * CY
                ref[at : at + CY, :] = fine_s[source : source + CY, :]
                source = (h * CX + first + x) * 8
                ref[at + CY : at + YD, :] = halo_ref[source : source + 8, :]
        for i in range(5):
            base = (mid_first + i) * YD
            at = 256 + i * 24
            ref[at : at + 16, :] = wide_ref[base : base + 16, :]
            ref[at + 16 : at + 24, :] = (
                wide_ref[base + 16 : base + 24, :] + wide_ref[base + 24 : base + 32, :]
            )
    out_copies += started([(low_ref, low_hbm), (high_ref, high_hbm)], sems, 7)
    for copy in out_copies:
        copy.wait()


def merge(fine, mid, before, behind):
    out = (array(2 * CX * 8, 128), array(24 * YD, 128), array(SEND, 128), array(SEND, 128))
    return call(
        merge_kernel,
        "merge",
        out,
        [HB, HB, VM, VM],
        [
            pltpu.VMEM((16 * CY, 128), F32),
            pltpu.VMEM((24 * 16, 128), F32),
            *buffers(*out),
            pltpu.SemaphoreType.DMA((9,)),
        ],
        outs=HB,
    )(fine, mid, before, behind)


def z_matrices(period, copies):
    half = period // 2
    z = np.arange(period)[:, None]
    f = np.arange(half)[None, :]
    angle = 2 * np.pi * ((z * f) % period) / period
    cosine, sine = np.cos(angle), -np.sin(angle)
    sine[:, 0] = (-1.0) ** np.arange(period)
    scale = np.full((half, 1), 2.0 / period)
    scale[0] = 1.0 / period
    forward = np.zeros((256, 256))
    inverse = np.zeros((256, 256))
    for c in range(copies):
        rows = slice(c * period, (c + 1) * period)
        real = slice(c * half, (c + 1) * half)
        imag = slice(128 + c * half, 128 + (c + 1) * half)
        forward[rows, real] = cosine
        forward[rows, imag] = sine
        inverse[real, rows] = scale * cosine.T
        inverse[imag, rows] = scale * sine.T
    return forward, inverse


def y_matrices():
    order = np.concatenate([np.arange(17), np.arange(31, 16, -1)])
    y = np.arange(YD)
    angle = 2 * np.pi * ((order[:, None] * y[None, :]) % YD) / YD
    cosine, sine = np.cos(angle), np.sin(angle)
    forward = np.block([[cosine, sine], [-sine, cosine]])
    inverse = np.block([[cosine.T, -sine.T], [sine.T, cosine.T]]) / YD
    return np.kron(np.eye(4), forward), np.kron(np.eye(4), inverse)


def stacked_rows(matrix):
    top, rest = np_halves(matrix)
    return np.concatenate([top, rest], axis=0)


def stacked_cols(matrix):
    top, rest = np_halves(matrix)
    return np.concatenate([top, rest], axis=1)


def right_product(value, matrix_ref):
    top, rest = halves(value)
    return (
        mm(top, matrix_ref[:256, :]) + mm(top, matrix_ref[256:, :]) + mm(rest, matrix_ref[:256, :])
    )


def left_product(matrix_ref, value):
    top, rest = halves(value)
    return (
        mm(matrix_ref[:, :256], top) + mm(matrix_ref[:, 256:], top) + mm(matrix_ref[:, :256], rest)
    )


def special_mask(copies, rows):
    lane = lax.broadcasted_iota(jnp.int32, (rows, 128), 1)
    row = lax.broadcasted_iota(jnp.int32, (rows, 128), 0)
    return (lane & (128 // copies - 1)) == 0, row


def forward_chunk(value, z_ref, y_ref, copies):
    z_freq = right_product(value, z_ref)
    stacks = []
    for h in range(2):
        pieces = []
        for q in range(4):
            slab = z_freq[(h * 4 + q) * YD : (h * 4 + q + 1) * YD]
            pieces += [slab[:, :128], slab[:, 128:]]
        stacks.append(jnp.concatenate(pieces, axis=0))
    freq = left_product(y_ref, jnp.concatenate(stacks, axis=1))
    lane_special, row = special_mask(copies, 16)
    special = lane_special & (row != 0)
    slabs = []
    for h in range(2):
        for q in range(4):
            slab = freq[q * 64 : (q + 1) * 64, h * 128 : (h + 1) * 128]
            ar, br, ai, bi = slab[:16], slab[16:32], slab[32:48], slab[48:]
            slabs.append(
                jnp.concatenate(
                    [
                        jnp.where(special, 0.5 * (ar + br), ar),
                        jnp.where(special, 0.5 * (ai + bi), br),
                        jnp.where(special, 0.5 * (ai - bi), ai),
                        jnp.where(special, 0.5 * (br - ar), bi),
                    ],
                    axis=0,
                )
            )
    return slabs


def inverse_chunk(slabs, z_ref, y_ref):
    stacks = [jnp.concatenate(slabs[h * 4 : h * 4 + 4], axis=0) for h in range(2)]
    space = left_product(y_ref, jnp.concatenate(stacks, axis=1))
    rows = []
    for h in range(2):
        for q in range(4):
            slab = space[q * 64 : (q + 1) * 64, h * 128 : (h + 1) * 128]
            rows.append(jnp.concatenate([slab[:YD], slab[YD:]], axis=1))
    return right_product(jnp.concatenate(rows, axis=0), z_ref)


def taps_kernel(copies, in_ref, z_ref, y_ref, after_ref, out_ref):
    lane_special, row = special_mask(copies, YD)
    special = lane_special & ((row == 0) | (row == 16))
    for p in range(2):
        slabs = forward_chunk(in_ref[p * 256 : (p + 1) * 256, :], z_ref, y_ref, copies)
        for j in range(8):
            dx = p * 8 + j
            if dx > 8:
                break
            real, imag = slabs[j][:YD], slabs[j][YD:]
            values = (real, jnp.where(special, imag, real), jnp.where(special, 0.0, imag))
            for part in range(3):
                at = (part * 9 + dx) * YD
                out_ref[at : at + YD, :] = values[part]


def taps(kernel, copies, z_matrix, y_matrix, after):
    flipped = kernel[:, ::-1, ::-1]
    tall = jnp.concatenate(
        [flipped[:, 4:], jnp.zeros((9, YD - 9, 9), F32), flipped[:, :4]], axis=1
    )
    period = 256 // copies
    wide = jnp.concatenate(
        [tall[:, :, 4:], jnp.zeros((9, YD, period - 9), F32), tall[:, :, :4]], axis=2
    )
    wide = jnp.concatenate([wide] * copies, axis=2)
    wide = jnp.concatenate([wide, jnp.zeros((7, YD, 256), F32)], axis=0)
    return call(
        functools.partial(taps_kernel, copies),
        f"taps{copies}",
        array(27 * YD, 128),
        [VM] * 3 + [HB],
    )(wide.reshape(16 * YD, 256), z_matrix, y_matrix, after)


def own_kernel(fine_hbm, halo_hbm, z_hbm, y_hbm, out_ref, fine_s, halo_s, z_ref, y_ref, sems):
    copies = started(
        [(z_hbm, z_ref), (y_hbm, y_ref), (fine_hbm, fine_s), (halo_hbm, halo_s)], sems
    )
    for copy in copies:
        copy.wait()
    for p in range(CX // 8):
        columns = []
        for h in range(2):
            rows = []
            for j in range(8):
                n = h * CX + p * 8 + j
                rows += [fine_s[n * CY : (n + 1) * CY, :], halo_s[n * 8 : (n + 1) * 8, :]]
            columns.append(jnp.concatenate(rows, axis=0))
        slabs = forward_chunk(jnp.concatenate(columns, axis=1), z_ref, y_ref, 1)
        for j in range(8):
            out_ref[(p * 8 + j) * 64 : (p * 8 + j + 1) * 64, :] = slabs[j]


def convolve(copies, block_out, blocks, taps_ref, freq_s, conv_s):
    lane_special, row = special_mask(copies, 8)

    def step(index, carry):
        v = index % 2
        first = (index // 2) * block_out
        sums = [[None] * 4 for _ in range(block_out)]
        for dx in range(9):
            coefs = []
            for half in range(2):
                at = dx * YD + half * 16 + v * 8
                coefs.append(
                    [
                        taps_ref[pl.ds(pl.multiple_of(at + part * 9 * YD, 8), 8), :]
                        for part in range(3)
                    ]
                )
            for j in range(block_out):
                base = (first + j + dx) * 64 + v * 8
                for half in range(2):
                    at = pl.multiple_of(base + half * 16, 8)
                    re = freq_s[pl.ds(at, 8), :]
                    im = freq_s[pl.ds(pl.multiple_of(at + 32, 8), 8), :]
                    a, t, b = coefs[half]
                    new_re = a * re - b * im
                    new_im = b * re + t * im
                    old = sums[j]
                    old[2 * half] = new_re if dx == 0 else old[2 * half] + new_re
                    old[2 * half + 1] = new_im if dx == 0 else old[2 * half + 1] + new_im
        special = lane_special & ((row != 0) | (v != 0))
        for j in range(block_out):
            ar, ai, br, bi = sums[j]
            base = (first + j) * 64 + v * 8
            values = (
                jnp.where(special, ar - bi, ar),
                jnp.where(special, ar + bi, br),
                jnp.where(special, ai + br, ai),
                jnp.where(special, br - ai, bi),
            )
            for part in range(4):
                conv_s[pl.ds(pl.multiple_of(base + part * 16, 8), 8), :] = values[part]
        return carry

    lax.fori_loop(0, 2 * blocks, step, 0)


def wide_slab(ref, index):
    at = 256 + index * 24
    last = ref[at + 16 : at + 24, :]
    row = lax.broadcasted_iota(jnp.int32, (8, 128), 0)
    return jnp.concatenate(
        [ref[at : at + 16, :], jnp.where(row < 4, last, 0.0), jnp.where(row < 4, 0.0, last)], axis=0
    )


def levels_kernel(
    own_ref, before_ref, behind_ref, *refs
):
    near_ref, mid_ref, freq_s, conv_s, mid_freq_s, mid_conv_s = refs[9:15]
    zf_ref, yf_ref, mzf_ref, wide_ref, near_taps, zi_ref, yi_ref, mid_taps, mzi_ref = refs[15:24]
    copies = started(list(zip(refs[:9], refs[15:24])), refs[24])
    freq_s[4 * 64 : 36 * 64, :] = own_ref[...]
    edges = [
        jnp.concatenate([ref[:128, :], ref[128:256, :]], axis=1) for ref in (before_ref, behind_ref)
    ]
    copies[0].wait()
    copies[1].wait()
    slabs = forward_chunk(jnp.concatenate(edges, axis=0), zf_ref, yf_ref, 1)
    for j in range(8):
        at = j if j < 4 else 32 + j
        freq_s[at * 64 : (at + 1) * 64, :] = slabs[j]
    zero = jnp.zeros((YD, 128), F32)
    copies[2].wait()
    copies[3].wait()
    for p in range(3):
        pairs = []
        for j in range(8):
            pair = []
            for n in (p * 8 + j, p * 8 + j + 9):
                if n > 24 or (n == p * 8 + j and n > 16):
                    slab = zero
                elif n < 4:
                    slab = wide_slab(before_ref, n)
                elif n > 20:
                    slab = wide_slab(behind_ref, n - 20)
                else:
                    slab = wide_ref[(n - 4) * YD : (n - 3) * YD, :]
                    if n == 4:
                        slab = slab + wide_slab(before_ref, 4)
                    if n == 20:
                        slab = slab + wide_slab(behind_ref, 0)
                pair.append(slab)
            pairs.append(jnp.concatenate(pair, axis=1))
        slabs = forward_chunk(jnp.concatenate(pairs, axis=0), mzf_ref, yf_ref, 2)
        for j in range(8):
            at = p * 8 + j
            mid_freq_s[at * 64 : (at + 1) * 64, :] = slabs[j]
    copies[4].wait()
    convolve(1, 8, 4, near_taps, freq_s, conv_s)
    copies[5].wait()
    copies[6].wait()
    for p in range(4):
        slabs = [conv_s[(p * 8 + j) * 64 : (p * 8 + j + 1) * 64, :] for j in range(8)]
        space = inverse_chunk(slabs, zi_ref, yi_ref)
        for j in range(8):
            x = p * 8 + j
            near_ref[x * CY : (x + 1) * CY, :] = space[j * YD : j * YD + CY]
    copies[7].wait()
    copies[8].wait()
    convolve(2, 9, 1, mid_taps, mid_freq_s, mid_conv_s)
    mid_conv_s[9 * 64 :, :] = jnp.zeros((7 * 64, 128), F32)
    for p in range(2):
        slabs = [mid_conv_s[(p * 8 + j) * 64 : (p * 8 + j + 1) * 64, :] for j in range(8)]
        space = inverse_chunk(slabs, mzi_ref, yi_ref)
        for j in range(8):
            i = p * 8 + j
            if i < 9:
                mid_ref[i * 16 : (i + 1) * 16, :] = space[j * YD : j * YD + 16]


def gauss(index, period, width):
    distance = jnp.minimum(index, period - index).astype(F32)
    return jnp.exp(-(distance * distance) / (width * width))


def top_kernel(in_ref, weights_ref, widths_ref, info_ref, out_ref, plane_s, depth_s):
    first_x = info_ref[2] * 8
    first_y = info_ref[3] * 6
    row = lax.broadcasted_iota(jnp.int32, (16, 256), 0)
    column = lax.broadcasted_iota(jnp.int32, (16, 256), 1)
    source = jnp.where(column < 128, column, (column - 128) * 8 + 8)
    offset = (first_x + row - source) & 127
    parts = [
        jnp.where(column < 144, gauss(offset, 128, widths_ref[k]), 0.0) for k in range(4)
    ]
    left = halves(jnp.concatenate(parts, axis=0))
    for jp in range(4):
        tiles = [in_ref[s * TOP_ROWS + jp * 8 : s * TOP_ROWS + jp * 8 + 8, :] for s in range(16)]
        tiles.append(in_ref[pl.ds(32 + jp, SIZE_X, stride=TOP_ROWS), :])
        tiles.append(jnp.zeros((112, 128), F32))
        right = halves(jnp.concatenate(tiles, axis=0))
        plane = mm(left[0], right[0]) + mm(left[0], right[1]) + mm(left[1], right[0])
        for k in range(4):
            plane_s[(k * 4 + jp) * 16 : (k * 4 + jp + 1) * 16, :] = plane[k * 16 : (k + 1) * 16]
    row = lax.broadcasted_iota(jnp.int32, (128, 128), 0)
    column = lax.broadcasted_iota(jnp.int32, (128, 128), 1)
    for k in range(4):
        weight = gauss((row - column) & 63, 64, widths_ref[k]) * weights_ref[k]
        weight = halves(jnp.where((row >> 6) == (column >> 6), weight, 0.0))
        value = halves(plane_s[k * 64 : (k + 1) * 64, :])
        depth_s[k * 64 : (k + 1) * 64, :] = (
            mm(value[0], weight[0]) + mm(value[0], weight[1]) + mm(value[1], weight[0])
        )
    lane = lax.broadcasted_iota(jnp.int32, (16, 128), 1)
    tiles = []
    for ip in range(5):
        first = depth_s[pl.ds(2 * ip, 16, stride=16), :]
        second = depth_s[pl.ds(2 * ip + 1, 16, stride=16), :]
        even = jnp.where(lane < 64, first, pltpu.roll(second, 64, 1))
        odd = jnp.where(lane < 64, pltpu.roll(first, 64, 1), second)
        tiles.append(jnp.concatenate([even, odd, jnp.zeros((96, 128), F32)], axis=0))
    right = halves(jnp.concatenate(tiles, axis=1))
    row = lax.broadcasted_iota(jnp.int32, (64, 128), 0)
    column = lax.broadcasted_iota(jnp.int32, (64, 128), 1)
    target = (row >> 3) * 6 + (row & 7)
    source = first_y + (column & 3) * 2 + ((column >> 4) & 1)
    offset = target - source
    offset = jnp.where(offset < 0, offset + 48, offset)
    offset = jnp.where(offset >= 48, offset - 48, offset)
    chosen = (column >> 2) & 3
    left = jnp.zeros((64, 128), F32)
    for k in range(4):
        left = jnp.where(chosen == k, gauss(offset, 48, widths_ref[k]), left)
    left = halves(jnp.where(column < 32, left, 0.0))
    out_ref[...] = mm(left[0], right[0]) + mm(left[0], right[1]) + mm(left[1], right[0])


def finish_kernel(
    near_ref, mid_ref, top_ref, *refs
):
    out_ref, grown_s = refs[4:6]
    grow_top_ref, grow_y_ref, grow_z_ref, grow_fine_ref, sems = refs[6:]
    copies = started(list(zip(refs[:4], refs[6:10])), sems)
    total = top_ref[:8, :]
    for s in range(1, SIZE_Y):
        total = total + top_ref[s * 8 : (s + 1) * 8, :]
    for copy in copies:
        copy.wait()
    lanes = []
    for ip in range(5):
        lanes.append(exact_right(total[:, ip * 128 : (ip + 1) * 128], grow_top_ref))
    deep = jnp.concatenate(lanes, axis=1)
    tiles = []
    for i in range(17):
        tile = deep[:, (i // 2) * 128 : (i // 2 + 1) * 128]
        if i % 2:
            tile = 0.5 * (tile + deep[:, (i // 2 + 1) * 128 : (i // 2 + 2) * 128])
        tiles.append(tile)
    flat = jnp.concatenate(tiles, axis=1)
    flat = jnp.concatenate([flat, jnp.zeros((120, 17 * 128), F32)], axis=0)
    tall = exact_left(grow_y_ref, flat)
    slabs = []
    for i in range(24):
        if i > 16:
            slabs.append(jnp.zeros((16, 128), F32))
            continue
        h = i // 9
        slabs.append(
            tall[:, i * 128 : (i + 1) * 128]
            + mid_ref[(i - 9 * h) * 16 : (i - 9 * h + 1) * 16, h * 128 : (h + 1) * 128]
        )
    for g in range(3):
        part = exact_right(jnp.concatenate(slabs[g * 8 : (g + 1) * 8], axis=0), grow_z_ref)
        grown_s[g * 192 : (g + 1) * 192, :] = exact_left(grow_fine_ref, part)
    for x in range(CX):
        at = slice(x * CY, (x + 1) * CY)
        i = x // 2
        value = grown_s[i * CY : (i + 1) * CY, :]
        if x % 2:
            value = 0.5 * (value + grown_s[(i + 1) * CY : (i + 2) * CY, :])
        out_ref[at, :] = near_ref[at, :] + value


def swap(to_low, to_high, axis):
    count = lax.axis_size(axis)
    forward = [(i, (i + 1) % count) for i in range(count)]
    backward = [(target, source) for source, target in forward]
    return lax.ppermute(to_high, axis, forward), lax.ppermute(to_low, axis, backward)


def on_device(
    charge_blocks, block_tile, block_count, near_kernel, mid_kernel, top_weights, top_widths
):
    at_x = lax.axis_index("gx")
    at_y = lax.axis_index("gy")
    info = jnp.stack(
        [block_count[0], ((at_x * SIZE_Y + at_y) % 4) * CAP, at_x, at_y]
    ).astype(jnp.int32)
    outgoing = send(block_tile.reshape(32, 128), info, charge_blocks)
    arrived = lax.all_to_all(
        outgoing.reshape(DEVICES, 1, ROWS * 128),
        ("gx", "gy"),
        split_axis=0,
        concat_axis=0,
        tiled=True,
    ).reshape(DEVICES * ROWS, 128)

    z_fine, z_fine_back = z_matrices(256, 1)
    z_mid, z_mid_back = z_matrices(128, 2)
    y_forward, y_back = y_matrices()
    zf, yf = stacked_rows(z_fine), stacked_cols(y_forward)
    zi, yi = stacked_rows(z_fine_back), stacked_cols(y_back)
    mzf, mzi = stacked_rows(z_mid), stacked_rows(z_mid_back)
    near_taps = taps(near_kernel, 1, zf, yf, outgoing)
    mid_taps = taps(mid_kernel, 2, mzf, yf, outgoing)

    fine, mid, low, high, top = collect(arrived, near_taps, mid_taps)
    before, behind = swap(low, high, "gy")
    tops = lax.all_to_all(
        top.reshape(SIZE_X, TOP_ROWS, 128), "gx", split_axis=0, concat_axis=0, tiled=True
    ).reshape(SIZE_X * TOP_ROWS, 128)
    partial = call(
        top_kernel,
        "top",
        array(64, 640),
        [VM, SM, SM, SM],
        [pltpu.VMEM((256, 128), F32), pltpu.VMEM((256, 128), F32)],
    )(tops, top_weights, top_widths, info)
    partial = lax.all_to_all(
        partial.reshape(SIZE_Y, 8, 640), "gy", split_axis=0, concat_axis=0, tiled=True
    ).reshape(64, 640)
    halo, wide, low, high = merge(fine, mid, before, behind)
    before, behind = swap(low, high, "gx")
    own = call(
        own_kernel,
        "own",
        array(CX * 64, 128),
        [HB] * 4,
        buffers(fine, halo, zf, yf) + [pltpu.SemaphoreType.DMA((4,))],
    )(fine, halo, zf, yf)
    tables = (zf, yf, mzf, wide, near_taps, zi, yi, mid_taps, mzi)
    near, mid_near = call(
        levels_kernel,
        "levels",
        (array(CX * CY, NZ), array(9 * 16, 256)),
        [VM] * 3 + [HB] * 9,
        [
            pltpu.VMEM((40 * 64, 128), F32),
            pltpu.VMEM((32 * 64, 128), F32),
            pltpu.VMEM((24 * 64, 128), F32),
            pltpu.VMEM((16 * 64, 128), F32),
            *buffers(*tables),
            pltpu.SemaphoreType.DMA((9,)),
        ],
    )(own, before, behind, *tables)
    grow_z = grow_matrix(2 * 64, 65)
    grow_z[:, 0] += grow_z[:, 64]
    grow_fine_z = grow_matrix(2 * 128, 129)
    grow_fine_z[:, 0] += grow_fine_z[:, 128]
    tables = (
        plain(twice(grow_z[:, :64].T)),
        plain(padded(grow_matrix(13, 7), 16, 128)),
        plain(grow_fine_z[:, :128].T),
        plain(np.kron(np.eye(8), padded(grow_matrix(CY, 13), CY, 16))),
    )
    out = call(
        finish_kernel,
        "finish",
        array(CX * CY, NZ),
        [VM] * 3 + [HB] * 4,
        [pltpu.VMEM((24 * CY, NZ), F32), *buffers(*tables), pltpu.SemaphoreType.DMA((4,))],
    )(near, mid_near, partial, *tables)
    return out.reshape(CX, CY, NZ)


def solution(mesh):
    placed = (P(("gx", "gy"), None), P(("gx", "gy")), P(("gx", "gy")), P(), P(), P(), P())
    return jax.shard_map(
        on_device, mesh=mesh, in_specs=placed, out_specs=P("gx", "gy", None), check_vma=False
    )
```

```python
import functools

import jax
import jax.numpy as jnp
import numpy as np
from jax import lax
from jax.experimental import pallas as pl
from jax.experimental.pallas import tpu as pltpu
from jax.sharding import PartitionSpec as P


CX = 32
CY = 24
NZ = 256
CAP = 32
DEVICES = 128
ROWS = CAP + 1
SIZE_X = 16
SIZE_Y = 8
DEAD = 2047
SEND = 376
TOP_ROWS = 40
YD = 32
F32 = jnp.float32
BF16 = jnp.bfloat16
VM = pl.BlockSpec(memory_space=pltpu.VMEM)
SM = pl.BlockSpec(memory_space=pltpu.SMEM)
HB = pl.BlockSpec(memory_space=pltpu.HBM)


def call(body, out, ins, scratch=(), limit=20, flops=0, moved=0, outs=VM):
    many = isinstance(out, tuple)
    outs = outs if isinstance(outs, tuple) else (outs,) * (len(out) if many else 1)
    shapes = tuple(
        pltpu.HBM(shape.shape, shape.dtype) if spec is HB else shape
        for shape, spec in zip(out if many else (out,), outs)
    )
    kernel = pl.pallas_call(
        body,
        out_shape=shapes if many else shapes[0],
        in_specs=ins,
        out_specs=outs if many else outs[0],
        scratch_shapes=list(scratch),
        compiler_params=pltpu.CompilerParams(vmem_limit_bytes=limit << 20),
        cost_estimate=pl.CostEstimate(flops=flops, bytes_accessed=moved, transcendentals=0),
    )

    def run(*args):
        placed = [
            pltpu.with_memory_space_constraint(jnp.asarray(arg), pltpu.HBM) if spec is HB else arg
            for arg, spec in zip(args, ins)
        ]
        return kernel(*placed)

    return run


def started(pairs, sems, first=0):
    copies = []
    for n, (source, target) in enumerate(pairs):
        copy = pltpu.make_async_copy(source, target, sems.at[first + n])
        copy.start()
        copies.append(copy)
    return copies


def buffers(*tables):
    return [pltpu.VMEM(table.shape, table.dtype) for table in tables]


def array(*shape):
    return jax.ShapeDtypeStruct(shape, F32)


def mm(a, b):
    return jnp.dot(a, b, preferred_element_type=F32)


def halves(value):
    top = value.astype(BF16)
    return top, (value - top.astype(F32)).astype(BF16)


def np_halves(matrix):
    matrix = np.asarray(matrix, np.float32)
    top = matrix.astype(BF16)
    return top, (matrix - top.astype(np.float32)).astype(BF16)


def send_kernel(
    tile_ref, info_ref, data_ref, out_ref, data_s, out_s, pos_ref, pos_s, owner_s, code_s, acc_s, sems
):
    (data_copy,) = started([(data_ref, data_s)], sems)
    tile = tile_ref[...]
    column = tile >> 1
    high_part = column >> 6
    grid_x = (high_part * 43691) >> 17
    grid_y = column - grid_x * (CY * SIZE_Y)
    owner_y = ((grid_y >> 3) * 43) >> 7
    owner = (grid_x >> 5) * SIZE_Y + owner_y
    cell = (tile & 1) * (CX * CY) + (grid_x & (CX - 1)) * CY + (grid_y - owner_y * CY)
    slot = lax.broadcasted_iota(jnp.int32, tile.shape, 0) * 128 + lax.broadcasted_iota(
        jnp.int32, tile.shape, 1
    )
    code = jnp.where(slot < info_ref[0], cell, DEAD)
    owner_s[...] = owner
    code_s[...] = code
    lane_offset = info_ref[1]
    lane = lax.broadcasted_iota(jnp.int32, (8, 128), 1)
    rows = lax.broadcasted_iota(jnp.int32, (128, 128), 0)
    before = lax.broadcasted_iota(jnp.int32, (128, 256), 0)
    after = lax.broadcasted_iota(jnp.int32, (128, 256), 1)
    prefix = jnp.where((before < after) | (after >= 128), 1.0, 0.0).astype(BF16)
    acc_s[...] = jnp.zeros_like(acc_s)

    def chunk(c, base):
        own = owner_s[pl.ds(c, 1), :]
        ids = code_s[pl.ds(c, 1), :]
        hit = rows == own
        one_hot = jnp.where(hit, 1.0, 0.0).astype(BF16)
        counted = mm(one_hot, prefix)
        rank = jnp.sum(jnp.where(hit, counted[:, :128] + base, 0.0), axis=0, keepdims=True)
        rank = rank.astype(jnp.int32)
        pos_ref[pl.ds(c, 1), :] = own * ROWS + rank
        place = rows[:CAP] == rank
        coarse = jnp.where(place, (ids >> 4).astype(F32), 0.0)
        fine = jnp.where(place, (ids & 15).astype(F32), 0.0)
        both = jnp.concatenate([coarse, fine, jnp.zeros((64, 128), F32)], axis=0).astype(BF16)
        acc_s[...] += lax.dot_general(
            one_hot, both, (((1,), (1,)), ((), ())), preferred_element_type=F32
        )
        return base + counted[:, 128:]

    lax.fori_loop(0, tile.shape[0], chunk, jnp.zeros((128, 128), F32), unroll=4)
    (pos_copy,) = started([(pos_ref, pos_s)], sems, 1)
    for b in range(DEVICES // 8):
        both = acc_s[b * 8 : b * 8 + 8, :]
        ids = both * 16.0 + pltpu.roll(both, 128 - CAP, 1)
        ids = pltpu.roll(jnp.where(lane < CAP, ids, 0.0), lane_offset, 1)
        for j in range(8):
            at = (b * 8 + j) * ROWS + CAP
            out_s[at : at + 1, :] = ids[j : j + 1]
    pos_copy.wait()
    data_copy.wait()

    def body(c, carry):
        for g in range(16):
            block = data_s[pl.ds(pl.multiple_of(c * 128 + g * 8, 8), 8), :]
            for j in range(8):
                out_s[pl.ds(pos_s[c, g * 8 + j], 1), :] = block[j : j + 1]
        return carry

    lax.fori_loop(0, 32, body, 0)
    (out_copy,) = started([(out_s, out_ref)], sems, 2)
    out_copy.wait()


def send(tile, info, data):
    return call(
        send_kernel,
        array(DEVICES * ROWS, 128),
        [VM, SM, HB],
        [
            pltpu.VMEM((4096, 128), F32),
            pltpu.VMEM((DEVICES * ROWS, 128), F32),
            pltpu.VMEM((32, 128), jnp.int32),
            pltpu.SMEM((32, 128), jnp.int32),
            pltpu.VMEM((32, 128), jnp.int32),
            pltpu.VMEM((32, 128), jnp.int32),
            pltpu.VMEM((128, 128), F32),
            pltpu.SemaphoreType.DMA((3,)),
        ],
        outs=HB,
    )(tile, info, data)


def thin_pair(count):
    matrix = np.zeros((count // 2 + 1, count))
    for i in range(count // 2 + 1):
        for source, weight in ((2 * i - 1, 0.5), (2 * i, 1.0), (2 * i + 1, 0.5)):
            if 0 <= source < count:
                matrix[i, source] = weight
    return matrix


def thin_cycle(length):
    matrix = np.zeros((length, length // 2))
    for i in range(length // 2):
        matrix[2 * i, i] += 1.0
        matrix[(2 * i - 1) % length, i] += 0.5
        matrix[(2 * i + 1) % length, i] += 0.5
    return matrix


def grow_matrix(count, source):
    matrix = np.zeros((count, source))
    for i in range(count):
        if i % 2 == 0:
            matrix[i, i // 2] = 1.0
        else:
            matrix[i, i // 2] = 0.5
            matrix[i, i // 2 + 1] = 0.5
    return matrix


def padded(matrix, rows, columns):
    out = np.zeros((rows, columns))
    out[: matrix.shape[0], : matrix.shape[1]] = matrix
    return out


def twice(matrix):
    return np.kron(np.eye(2), matrix)


def plain(matrix):
    return np.asarray(matrix, np.float32).astype(BF16)


def top_rows_matrix():
    rows_x = padded(thin_pair(17), 9, 17)
    rows_y = padded(thin_pair(13), 8, 16)
    rows_y[7] = 0.0
    matrix = np.zeros((2 * TOP_ROWS, 17 * 16))
    for i in range(9):
        for j in range(8):
            line = (j // 2) * 8 + i if i < 8 else 32 + j // 2
            matrix[(j % 2) * TOP_ROWS + line] = np.kron(rows_x[i], rows_y[j])
    return matrix


def exact_left(matrix_ref, value):
    top, rest = halves(value)
    return mm(matrix_ref[...], top) + mm(matrix_ref[...], rest)


def exact_right(value, matrix_ref):
    top, rest = halves(value)
    return mm(top, matrix_ref[...]) + mm(rest, matrix_ref[...])


def collect_kernel(in_ref, *refs):
    tables = refs[:4]
    outs = refs[-18:-13]
    data_s, ids_s, slab_s = refs[-13:-10]
    thin_z_ref, thin_y_ref, top_rows_ref, top_z_ref = refs[-10:-6]
    fine_ref, mid_ref, low_ref, high_ref, top_ref, sems = refs[-6:]
    table_copies = started(list(zip(tables, refs[-10:-6])), sems)
    for c in range(DEVICES // 4):
        total = None
        for j in range(4):
            base = (c * 4 + j) * ROWS
            top, rest = halves(in_ref[base : base + CAP, :])
            start = (c * 4 + j) * CAP
            data_s[start : start + CAP, :128] = top
            data_s[start : start + CAP, 128:] = rest
            line = in_ref[base + CAP : base + CAP + 1, :]
            total = line if total is None else total + line
        ids_s[c : c + 1, :] = total.astype(jnp.int32)
    rows = lax.broadcasted_iota(jnp.int32, (256, 128), 0).astype(F32).astype(BF16)
    one, zero = jnp.ones((256, 128), BF16), jnp.zeros((256, 128), BF16)

    def block(b, carry):
        first = pl.multiple_of(b * 256, 256)
        acc = jnp.zeros((256, 256), F32)
        for k in range(16):
            parts = []
            for q in range(2):
                ids = jnp.clip(ids_s[2 * k + q : 2 * k + q + 1, :] - first, -1, 256)
                line = jnp.broadcast_to(ids.astype(F32), (16, 128)).astype(BF16)
                parts.append(jnp.where(rows == jnp.concatenate([line] * 16, axis=0), one, zero))
            acc = acc + mm(jnp.concatenate(parts, axis=1), data_s[k * 256 : (k + 1) * 256, :])
        fine_ref[pl.ds(first, 256), :] = acc[:, :128] + acc[:, 128:]
        return carry

    lax.fori_loop(0, 6, block, 0)
    out_copies = started([(fine_ref, outs[0])], sems, 4)
    for i in range(17):
        total = None
        for x, weight in ((2 * i, 1.0), (2 * i - 1, 0.5), (2 * i + 1, 0.5)):
            if 0 <= x < CX:
                term = jnp.concatenate(
                    [
                        fine_ref[h * CX * CY + x * CY : h * CX * CY + (x + 1) * CY, :]
                        for h in range(2)
                    ],
                    axis=1,
                )
                term = term if weight == 1.0 else weight * term
                total = term if total is None else total + term
        slab_s[i * CY : (i + 1) * CY, :] = total
    slab_s[17 * CY :, :] = jnp.zeros((7 * CY, NZ), F32)
    for copy in table_copies:
        copy.wait()
    for g in range(3):
        part = exact_right(slab_s[g * 192 : (g + 1) * 192, :], thin_z_ref)
        mid_ref[g * 128 : (g + 1) * 128, :] = exact_left(thin_y_ref, part)
    for h in range(2):
        for c in range(4):
            at = slice((h * 4 + c) * CX, (h * 4 + c + 1) * CX)
            low_ref[at, :] = fine_ref[pl.ds(h * CX * CY + c, CX, stride=CY), :]
            high_ref[at, :] = fine_ref[pl.ds(h * CX * CY + CY - 4 + c, CX, stride=CY), :]
    for j in range(5):
        at = slice(256 + j * 24, 256 + (j + 1) * 24)
        low_ref[at, :] = mid_ref[pl.ds(j, 24, stride=16), :]
        high_ref[at, :] = mid_ref[pl.ds(8 + j, 24, stride=16), :]
    out_copies += started([(mid_ref, outs[1]), (low_ref, outs[2]), (high_ref, outs[3])], sems, 5)
    stacked = exact_left(top_rows_ref, mid_ref[: 17 * 16, :])
    pair = jnp.concatenate([stacked[:TOP_ROWS], stacked[TOP_ROWS:]], axis=1)
    top_charge = exact_right(pair, top_z_ref)
    for s in range(SIZE_X):
        top_ref[s * TOP_ROWS : (s + 1) * TOP_ROWS, :] = top_charge
    out_copies += started([(top_ref, outs[4])], sems, 8)
    for copy in out_copies:
        copy.wait()


def collect(arrived, *after):
    tables = (
        plain(thin_cycle(NZ)),
        plain(np.kron(np.eye(8), padded(thin_pair(CY), 16, CY))),
        plain(top_rows_matrix()),
        plain(twice(thin_cycle(128))),
    )
    out = (
        array(2 * CX * CY, 128),
        array(24 * 16, 128),
        array(SEND, 128),
        array(SEND, 128),
        array(SIZE_X * TOP_ROWS, 128),
    )
    return call(
        collect_kernel,
        out,
        [VM] + [HB] * (4 + len(after)),
        [
            pltpu.VMEM((DEVICES * CAP, 256), BF16),
            pltpu.VMEM((DEVICES // 4, 128), jnp.int32),
            pltpu.VMEM((24 * CY, NZ), F32),
            *buffers(*tables),
            *buffers(*out),
            pltpu.SemaphoreType.DMA((9,)),
        ],
        outs=HB,
    )(arrived, *tables, *after)


def merge_kernel(
    fine_hbm, mid_hbm, before_ref, behind_ref, halo_hbm, wide_hbm, low_hbm, high_hbm,
    fine_s, mid_ref, halo_ref, wide_ref, low_ref, high_ref, sems,
):
    pairs = [(mid_hbm, mid_ref)]
    for h in range(2):
        for first, at in ((0, 0), (CX - 4, 4)):
            start = (h * CX + first) * CY
            pairs.append(
                (fine_hbm.at[pl.ds(start, 4 * CY)], fine_s.at[pl.ds((h * 8 + at) * CY, 4 * CY)])
            )
    mid_copy, *fine_copies = started(pairs, sems)
    for h in range(2):
        for c in range(4):
            at = slice((h * 4 + c) * CX, (h * 4 + c + 1) * CX)
            start = h * CX * 8 + c
            halo_ref[pl.ds(start, CX, stride=8), :] = behind_ref[at, :]
            halo_ref[pl.ds(start + 4, CX, stride=8), :] = before_ref[at, :]
    out_copies = started([(halo_ref, halo_hbm)], sems, 5)
    mid_copy.wait()
    for i in range(24):
        wide_ref[i * YD : i * YD + 16, :] = mid_ref[i * 16 : (i + 1) * 16, :]
        wide_ref[i * YD + 16 : (i + 1) * YD, :] = jnp.zeros((16, 128), F32)
    for j in range(5):
        at = slice(256 + j * 24, 256 + (j + 1) * 24)
        behind = behind_ref[at, :]
        if j == 0:
            behind = behind + wide_ref[pl.ds(12, 24, stride=YD), :]
        wide_ref[pl.ds(12 + j, 24, stride=YD), :] = behind
        before = before_ref[at, :]
        row = 28 + j if j < 4 else 0
        if j == 4:
            before = before + wide_ref[pl.ds(0, 24, stride=YD), :]
        wide_ref[pl.ds(row, 24, stride=YD), :] = before
    out_copies += started([(wide_ref, wide_hbm)], sems, 6)
    for copy in fine_copies:
        copy.wait()
    for ref, first, at_fine, mid_first in ((low_ref, 0, 0, 0), (high_ref, CX - 4, 4, 12)):
        for h in range(2):
            for x in range(4):
                at = h * 128 + x * YD
                source = (h * 8 + at_fine + x) * CY
                ref[at : at + CY, :] = fine_s[source : source + CY, :]
                source = (h * CX + first + x) * 8
                ref[at + CY : at + YD, :] = halo_ref[source : source + 8, :]
        for i in range(5):
            base = (mid_first + i) * YD
            at = 256 + i * 24
            ref[at : at + 16, :] = wide_ref[base : base + 16, :]
            ref[at + 16 : at + 24, :] = (
                wide_ref[base + 16 : base + 24, :] + wide_ref[base + 24 : base + 32, :]
            )
    out_copies += started([(low_ref, low_hbm), (high_ref, high_hbm)], sems, 7)
    for copy in out_copies:
        copy.wait()


def merge(fine, mid, before, behind):
    out = (array(2 * CX * 8, 128), array(24 * YD, 128), array(SEND, 128), array(SEND, 128))
    return call(
        merge_kernel,
        out,
        [HB, HB, VM, VM],
        [
            pltpu.VMEM((16 * CY, 128), F32),
            pltpu.VMEM((24 * 16, 128), F32),
            *buffers(*out),
            pltpu.SemaphoreType.DMA((9,)),
        ],
        outs=HB,
    )(fine, mid, before, behind)


def z_matrices(period, copies):
    half = period // 2
    z = np.arange(period)[:, None]
    f = np.arange(half)[None, :]
    angle = 2 * np.pi * ((z * f) % period) / period
    cosine, sine = np.cos(angle), -np.sin(angle)
    sine[:, 0] = (-1.0) ** np.arange(period)
    scale = np.full((half, 1), 2.0 / period)
    scale[0] = 1.0 / period
    forward = np.zeros((256, 256))
    inverse = np.zeros((256, 256))
    for c in range(copies):
        rows = slice(c * period, (c + 1) * period)
        real = slice(c * half, (c + 1) * half)
        imag = slice(128 + c * half, 128 + (c + 1) * half)
        forward[rows, real] = cosine
        forward[rows, imag] = sine
        inverse[real, rows] = scale * cosine.T
        inverse[imag, rows] = scale * sine.T
    return forward, inverse


def y_matrices():
    order = np.concatenate([np.arange(17), np.arange(31, 16, -1)])
    y = np.arange(YD)
    angle = 2 * np.pi * ((order[:, None] * y[None, :]) % YD) / YD
    cosine, sine = np.cos(angle), np.sin(angle)
    forward = np.block([[cosine, sine], [-sine, cosine]])
    inverse = np.block([[cosine.T, -sine.T], [sine.T, cosine.T]]) / YD
    return np.kron(np.eye(4), forward), np.kron(np.eye(4), inverse)


def stacked_rows(matrix):
    top, rest = np_halves(matrix)
    return np.concatenate([top, rest], axis=0)


def stacked_cols(matrix):
    top, rest = np_halves(matrix)
    return np.concatenate([top, rest], axis=1)


def right_product(value, matrix_ref):
    top, rest = halves(value)
    return (
        mm(top, matrix_ref[:256, :]) + mm(top, matrix_ref[256:, :]) + mm(rest, matrix_ref[:256, :])
    )


def left_product(matrix_ref, value):
    top, rest = halves(value)
    return (
        mm(matrix_ref[:, :256], top) + mm(matrix_ref[:, 256:], top) + mm(matrix_ref[:, :256], rest)
    )


def special_mask(copies, rows):
    lane = lax.broadcasted_iota(jnp.int32, (rows, 128), 1)
    row = lax.broadcasted_iota(jnp.int32, (rows, 128), 0)
    return (lane & (128 // copies - 1)) == 0, row


def forward_chunk(value, z_ref, y_ref, copies):
    z_freq = right_product(value, z_ref)
    stacks = []
    for h in range(2):
        pieces = []
        for q in range(4):
            slab = z_freq[(h * 4 + q) * YD : (h * 4 + q + 1) * YD]
            pieces += [slab[:, :128], slab[:, 128:]]
        stacks.append(jnp.concatenate(pieces, axis=0))
    freq = left_product(y_ref, jnp.concatenate(stacks, axis=1))
    lane_special, row = special_mask(copies, 16)
    special = lane_special & (row != 0)
    slabs = []
    for h in range(2):
        for q in range(4):
            slab = freq[q * 64 : (q + 1) * 64, h * 128 : (h + 1) * 128]
            ar, br, ai, bi = slab[:16], slab[16:32], slab[32:48], slab[48:]
            slabs.append(
                jnp.concatenate(
                    [
                        jnp.where(special, 0.5 * (ar + br), ar),
                        jnp.where(special, 0.5 * (ai + bi), br),
                        jnp.where(special, 0.5 * (ai - bi), ai),
                        jnp.where(special, 0.5 * (br - ar), bi),
                    ],
                    axis=0,
                )
            )
    return slabs


def inverse_chunk(slabs, z_ref, y_ref):
    stacks = [jnp.concatenate(slabs[h * 4 : h * 4 + 4], axis=0) for h in range(2)]
    space = left_product(y_ref, jnp.concatenate(stacks, axis=1))
    rows = []
    for h in range(2):
        for q in range(4):
            slab = space[q * 64 : (q + 1) * 64, h * 128 : (h + 1) * 128]
            rows.append(jnp.concatenate([slab[:YD], slab[YD:]], axis=1))
    return right_product(jnp.concatenate(rows, axis=0), z_ref)


def taps_kernel(copies, in_ref, z_ref, y_ref, after_ref, out_ref):
    lane_special, row = special_mask(copies, YD)
    special = lane_special & ((row == 0) | (row == 16))
    for p in range(2):
        slabs = forward_chunk(in_ref[p * 256 : (p + 1) * 256, :], z_ref, y_ref, copies)
        for j in range(8):
            dx = p * 8 + j
            if dx > 8:
                break
            real, imag = slabs[j][:YD], slabs[j][YD:]
            values = (real, jnp.where(special, imag, real), jnp.where(special, 0.0, imag))
            for part in range(3):
                at = (part * 9 + dx) * YD
                out_ref[at : at + YD, :] = values[part]


def taps(kernel, copies, z_matrix, y_matrix, after):
    flipped = kernel[:, ::-1, ::-1]
    tall = jnp.concatenate(
        [flipped[:, 4:], jnp.zeros((9, YD - 9, 9), F32), flipped[:, :4]], axis=1
    )
    period = 256 // copies
    wide = jnp.concatenate(
        [tall[:, :, 4:], jnp.zeros((9, YD, period - 9), F32), tall[:, :, :4]], axis=2
    )
    wide = jnp.concatenate([wide] * copies, axis=2)
    wide = jnp.concatenate([wide, jnp.zeros((7, YD, 256), F32)], axis=0)
    return call(
        functools.partial(taps_kernel, copies), array(27 * YD, 128), [VM] * 3 + [HB]
    )(wide.reshape(16 * YD, 256), z_matrix, y_matrix, after)


def own_kernel(fine_hbm, halo_hbm, z_ref, y_ref, out_ref, fine_s, halo_s, sems):
    waits = []
    for p in range(CX // 8):
        pairs = []
        for h in range(2):
            for source, target, rows in ((fine_hbm, fine_s, CY), (halo_hbm, halo_s, 8)):
                at = pl.ds((h * CX + p * 8) * rows, 8 * rows)
                pairs.append((source.at[at], target.at[at]))
        waits.append(started(pairs, sems, p * 4))
    for p in range(CX // 8):
        for copy in waits[p]:
            copy.wait()
        columns = []
        for h in range(2):
            rows = []
            for j in range(8):
                n = h * CX + p * 8 + j
                rows += [fine_s[n * CY : (n + 1) * CY, :], halo_s[n * 8 : (n + 1) * 8, :]]
            columns.append(jnp.concatenate(rows, axis=0))
        slabs = forward_chunk(jnp.concatenate(columns, axis=1), z_ref, y_ref, 1)
        for j in range(8):
            out_ref[(p * 8 + j) * 64 : (p * 8 + j + 1) * 64, :] = slabs[j]


def convolve(copies, first, count, taps_ref, freq_s, conv_s):
    lane_special, row = special_mask(copies, 8)
    for v in range(2):
        sums = [[None] * 4 for _ in range(count)]
        for dx in range(9):
            coefs = []
            for half in range(2):
                at = dx * YD + half * 16 + v * 8
                coefs.append([taps_ref[at + part * 288 : at + part * 288 + 8, :] for part in range(3)])
            for j in range(count):
                old = sums[j]
                for half in range(2):
                    at = (first + j + dx) * 64 + v * 8 + half * 16
                    re = freq_s[at : at + 8, :]
                    im = freq_s[at + 32 : at + 40, :]
                    a, t, b = coefs[half]
                    new_re = a * re - b * im
                    new_im = b * re + t * im
                    old[2 * half] = new_re if dx == 0 else old[2 * half] + new_re
                    old[2 * half + 1] = new_im if dx == 0 else old[2 * half + 1] + new_im
        special = lane_special & (row != 0) if v == 0 else lane_special
        for j in range(count):
            ar, ai, br, bi = sums[j]
            at = (first + j) * 64 + v * 8
            conv_s[at : at + 8, :] = jnp.where(special, ar - bi, ar)
            conv_s[at + 16 : at + 24, :] = jnp.where(special, ar + bi, br)
            conv_s[at + 32 : at + 40, :] = jnp.where(special, ai + br, ai)
            conv_s[at + 48 : at + 56, :] = jnp.where(special, br - ai, bi)


def wide_slab(ref, index):
    at = 256 + index * 24
    last = ref[at + 16 : at + 24, :]
    row = lax.broadcasted_iota(jnp.int32, (8, 128), 0)
    return jnp.concatenate(
        [ref[at : at + 16, :], jnp.where(row < 4, last, 0.0), jnp.where(row < 4, 0.0, last)], axis=0
    )


def levels_kernel(
    own_ref, before_ref, behind_ref, *refs
):
    zf_ref, yf_ref, mzf_ref, zi_ref, yi_ref, mzi_ref = refs[:6]
    near_ref, mid_ref, freq_s, conv_s, mid_freq_s, mid_conv_s = refs[9:15]
    wide_ref, near_taps, mid_taps = refs[15:18]
    copies = started(list(zip(refs[6:9], refs[15:18])), refs[18])
    freq_s[4 * 64 : 36 * 64, :] = own_ref[...]
    edges = [
        jnp.concatenate([ref[:128, :], ref[128:256, :]], axis=1) for ref in (before_ref, behind_ref)
    ]
    slabs = forward_chunk(jnp.concatenate(edges, axis=0), zf_ref, yf_ref, 1)
    for j in range(8):
        at = j if j < 4 else 32 + j
        freq_s[at * 64 : (at + 1) * 64, :] = slabs[j]
    zero = jnp.zeros((YD, 128), F32)
    copies[0].wait()
    for p in range(3):
        pairs = []
        for j in range(8):
            pair = []
            for n in (p * 8 + j, p * 8 + j + 9):
                if n > 24 or (n == p * 8 + j and n > 16):
                    slab = zero
                elif n < 4:
                    slab = wide_slab(before_ref, n)
                elif n > 20:
                    slab = wide_slab(behind_ref, n - 20)
                else:
                    slab = wide_ref[(n - 4) * YD : (n - 3) * YD, :]
                    if n == 4:
                        slab = slab + wide_slab(before_ref, 4)
                    if n == 20:
                        slab = slab + wide_slab(behind_ref, 0)
                pair.append(slab)
            pairs.append(jnp.concatenate(pair, axis=1))
        slabs = forward_chunk(jnp.concatenate(pairs, axis=0), mzf_ref, yf_ref, 2)
        for j in range(8):
            at = p * 8 + j
            mid_freq_s[at * 64 : (at + 1) * 64, :] = slabs[j]
    for copy in copies[1:]:
        copy.wait()
    for p in range(4):
        convolve(1, p * 8, 8, near_taps, freq_s, conv_s)
        slabs = [conv_s[(p * 8 + j) * 64 : (p * 8 + j + 1) * 64, :] for j in range(8)]
        space = inverse_chunk(slabs, zi_ref, yi_ref)
        for j in range(8):
            x = p * 8 + j
            near_ref[x * CY : (x + 1) * CY, :] = space[j * YD : j * YD + CY]
    mid_conv_s[9 * 64 :, :] = jnp.zeros((7 * 64, 128), F32)
    for first, count in ((0, 5), (5, 4)):
        convolve(2, first, count, mid_taps, mid_freq_s, mid_conv_s)
    for p in range(2):
        slabs = [mid_conv_s[(p * 8 + j) * 64 : (p * 8 + j + 1) * 64, :] for j in range(8)]
        space = inverse_chunk(slabs, mzi_ref, yi_ref)
        for j in range(8):
            i = p * 8 + j
            if i < 9:
                mid_ref[i * 16 : (i + 1) * 16, :] = space[j * YD : j * YD + 16]


def gauss(index, period, width):
    distance = jnp.minimum(index, period - index).astype(F32)
    return jnp.exp(-(distance * distance) / (width * width))


def top_kernel(in_ref, weights_ref, widths_ref, info_ref, out_ref, plane_s, depth_s):
    first_x = info_ref[2] * 8
    first_y = info_ref[3] * 6
    row = lax.broadcasted_iota(jnp.int32, (16, 256), 0)
    column = lax.broadcasted_iota(jnp.int32, (16, 256), 1)
    source = jnp.where(column < 128, column, (column - 128) * 8 + 8)
    offset = (first_x + row - source) & 127
    parts = [
        jnp.where(column < 144, gauss(offset, 128, widths_ref[k]), 0.0) for k in range(4)
    ]
    left = halves(jnp.concatenate(parts, axis=0))
    for jp in range(4):
        tiles = [in_ref[s * TOP_ROWS + jp * 8 : s * TOP_ROWS + jp * 8 + 8, :] for s in range(16)]
        tiles.append(in_ref[pl.ds(32 + jp, SIZE_X, stride=TOP_ROWS), :])
        tiles.append(jnp.zeros((112, 128), F32))
        right = halves(jnp.concatenate(tiles, axis=0))
        plane = mm(left[0], right[0]) + mm(left[0], right[1]) + mm(left[1], right[0])
        for k in range(4):
            plane_s[(k * 4 + jp) * 16 : (k * 4 + jp + 1) * 16, :] = plane[k * 16 : (k + 1) * 16]
    row = lax.broadcasted_iota(jnp.int32, (128, 128), 0)
    column = lax.broadcasted_iota(jnp.int32, (128, 128), 1)
    for k in range(4):
        weight = gauss((row - column) & 63, 64, widths_ref[k]) * weights_ref[k]
        weight = halves(jnp.where((row >> 6) == (column >> 6), weight, 0.0))
        value = halves(plane_s[k * 64 : (k + 1) * 64, :])
        depth_s[k * 64 : (k + 1) * 64, :] = (
            mm(value[0], weight[0]) + mm(value[0], weight[1]) + mm(value[1], weight[0])
        )
    lane = lax.broadcasted_iota(jnp.int32, (16, 128), 1)
    tiles = []
    for ip in range(5):
        first = depth_s[pl.ds(2 * ip, 16, stride=16), :]
        second = depth_s[pl.ds(2 * ip + 1, 16, stride=16), :]
        even = jnp.where(lane < 64, first, pltpu.roll(second, 64, 1))
        odd = jnp.where(lane < 64, pltpu.roll(first, 64, 1), second)
        tiles.append(jnp.concatenate([even, odd, jnp.zeros((96, 128), F32)], axis=0))
    right = halves(jnp.concatenate(tiles, axis=1))
    row = lax.broadcasted_iota(jnp.int32, (64, 128), 0)
    column = lax.broadcasted_iota(jnp.int32, (64, 128), 1)
    target = (row >> 3) * 6 + (row & 7)
    source = first_y + (column & 3) * 2 + ((column >> 4) & 1)
    offset = target - source
    offset = jnp.where(offset < 0, offset + 48, offset)
    offset = jnp.where(offset >= 48, offset - 48, offset)
    chosen = (column >> 2) & 3
    left = jnp.zeros((64, 128), F32)
    for k in range(4):
        left = jnp.where(chosen == k, gauss(offset, 48, widths_ref[k]), left)
    left = halves(jnp.where(column < 32, left, 0.0))
    out_ref[...] = mm(left[0], right[0]) + mm(left[0], right[1]) + mm(left[1], right[0])


def finish_kernel(
    near_ref, mid_ref, top_ref, *refs
):
    grow_top_ref, grow_y_ref, grow_z_ref, grow_fine_ref, out_ref, grown_s = refs
    total = top_ref[:8, :]
    for s in range(1, SIZE_Y):
        total = total + top_ref[s * 8 : (s + 1) * 8, :]
    lanes = []
    for ip in range(5):
        lanes.append(exact_right(total[:, ip * 128 : (ip + 1) * 128], grow_top_ref))
    deep = jnp.concatenate(lanes, axis=1)
    tiles = []
    for i in range(17):
        tile = deep[:, (i // 2) * 128 : (i // 2 + 1) * 128]
        if i % 2:
            tile = 0.5 * (tile + deep[:, (i // 2 + 1) * 128 : (i // 2 + 2) * 128])
        tiles.append(tile)
    flat = jnp.concatenate(tiles, axis=1)
    flat = jnp.concatenate([flat, jnp.zeros((120, 17 * 128), F32)], axis=0)
    tall = exact_left(grow_y_ref, flat)
    slabs = []
    for i in range(24):
        if i > 16:
            slabs.append(jnp.zeros((16, 128), F32))
            continue
        h = i // 9
        slabs.append(
            tall[:, i * 128 : (i + 1) * 128]
            + mid_ref[(i - 9 * h) * 16 : (i - 9 * h + 1) * 16, h * 128 : (h + 1) * 128]
        )
    for g in range(3):
        part = exact_right(jnp.concatenate(slabs[g * 8 : (g + 1) * 8], axis=0), grow_z_ref)
        grown_s[g * 192 : (g + 1) * 192, :] = exact_left(grow_fine_ref, part)
    for x in range(CX):
        at = slice(x * CY, (x + 1) * CY)
        i = x // 2
        value = grown_s[i * CY : (i + 1) * CY, :]
        if x % 2:
            value = 0.5 * (value + grown_s[(i + 1) * CY : (i + 2) * CY, :])
        out_ref[at, :] = near_ref[at, :] + value


def swap(to_low, to_high, axis):
    count = lax.axis_size(axis)
    forward = [(i, (i + 1) % count) for i in range(count)]
    backward = [(target, source) for source, target in forward]
    before = lax.ppermute(to_high, axis, forward)
    behind = lax.ppermute(to_low, axis, backward)
    return before, behind


def on_device(
    charge_blocks, block_tile, block_count, near_kernel, mid_kernel, top_weights, top_widths
):
    at_x = lax.axis_index("gx")
    at_y = lax.axis_index("gy")
    info = jnp.stack(
        [block_count[0], ((at_x * SIZE_Y + at_y) % 4) * CAP, at_x, at_y]
    ).astype(jnp.int32)
    outgoing = send(block_tile.reshape(32, 128), info, charge_blocks)
    arrived = lax.all_to_all(
        outgoing.reshape(DEVICES, 1, ROWS * 128),
        ("gx", "gy"),
        split_axis=0,
        concat_axis=0,
        tiled=True,
    ).reshape(DEVICES * ROWS, 128)

    z_fine, z_fine_back = z_matrices(256, 1)
    z_mid, z_mid_back = z_matrices(128, 2)
    y_forward, y_back = y_matrices()
    zf, yf = stacked_rows(z_fine), stacked_cols(y_forward)
    zi, yi = stacked_rows(z_fine_back), stacked_cols(y_back)
    mzf, mzi = stacked_rows(z_mid), stacked_rows(z_mid_back)
    near_taps = taps(near_kernel, 1, zf, yf, outgoing)
    mid_taps = taps(mid_kernel, 2, mzf, yf, outgoing)

    fine, mid, low, high, top = collect(arrived, near_taps, mid_taps)
    before, behind = swap(low, high, "gy")
    tops = lax.all_to_all(
        top.reshape(SIZE_X, TOP_ROWS, 128), "gx", split_axis=0, concat_axis=0, tiled=True
    )
    tops = tops.reshape(SIZE_X * TOP_ROWS, 128)
    partial = call(
        top_kernel,
        array(64, 640),
        [VM, SM, SM, SM],
        [pltpu.VMEM((256, 128), F32), pltpu.VMEM((256, 128), F32)],
    )(tops, top_weights, top_widths, info)
    partial = lax.all_to_all(
        partial.reshape(SIZE_Y, 8, 640), "gy", split_axis=0, concat_axis=0, tiled=True
    ).reshape(64, 640)
    halo, wide, low, high = merge(fine, mid, before, behind)
    before, behind = swap(low, high, "gx")
    own = call(
        own_kernel,
        array(CX * 64, 128),
        [HB, HB, VM, VM],
        buffers(fine, halo) + [pltpu.SemaphoreType.DMA((16,))],
    )(fine, halo, zf, yf)
    tables = (wide, near_taps, mid_taps)
    near, mid_near = call(
        levels_kernel,
        (array(CX * CY, NZ), array(9 * 16, 256)),
        [VM] * 9 + [HB] * 3,
        [
            pltpu.VMEM((40 * 64, 128), F32),
            pltpu.VMEM((32 * 64, 128), F32),
            pltpu.VMEM((24 * 64, 128), F32),
            pltpu.VMEM((16 * 64, 128), F32),
            *buffers(*tables),
            pltpu.SemaphoreType.DMA((3,)),
        ],
    )(own, before, behind, zf, yf, mzf, zi, yi, mzi, *tables)
    grow_z = grow_matrix(2 * 64, 65)
    grow_z[:, 0] += grow_z[:, 64]
    grow_fine_z = grow_matrix(2 * 128, 129)
    grow_fine_z[:, 0] += grow_fine_z[:, 128]
    tables = (
        plain(twice(grow_z[:, :64].T)),
        plain(padded(grow_matrix(13, 7), 16, 128)),
        plain(grow_fine_z[:, :128].T),
        plain(np.kron(np.eye(8), padded(grow_matrix(CY, 13), CY, 16))),
    )
    out = call(
        finish_kernel, array(CX * CY, NZ), [VM] * 7, [pltpu.VMEM((24 * CY, NZ), F32)]
    )(near, mid_near, partial, *tables)
    return out.reshape(CX, CY, NZ)


def solution(mesh):
    placed = (P(("gx", "gy"), None), P(("gx", "gy")), P(("gx", "gy")), P(), P(), P(), P())
    return jax.shard_map(
        on_device, mesh=mesh, in_specs=placed, out_specs=P("gx", "gy", None), check_vma=False
    )
```

```python
import functools

import jax
import jax.numpy as jnp
import numpy as np
from jax import lax
from jax.experimental import pallas as pl
from jax.experimental.pallas import tpu as pltpu
from jax.sharding import PartitionSpec as P


CX = 32
CY = 24
NZ = 256
CAP = 32
DEVICES = 128
ROWS = CAP + 1
SIZE_X = 16
SIZE_Y = 8
DEAD = 2047
SEND = 376
TOP_ROWS = 40
YD = 32
F32 = jnp.float32
BF16 = jnp.bfloat16
VM = pl.BlockSpec(memory_space=pltpu.VMEM)
SM = pl.BlockSpec(memory_space=pltpu.SMEM)
HB = pl.BlockSpec(memory_space=pltpu.HBM)


def call(body, out, ins, scratch=(), limit=10, flops=0, moved=0, outs=VM):
    many = isinstance(out, tuple)
    outs = outs if isinstance(outs, tuple) else (outs,) * (len(out) if many else 1)
    shapes = tuple(
        pltpu.HBM(shape.shape, shape.dtype) if spec is HB else shape
        for shape, spec in zip(out if many else (out,), outs)
    )
    kernel = pl.pallas_call(
        body,
        out_shape=shapes if many else shapes[0],
        in_specs=ins,
        out_specs=outs if many else outs[0],
        scratch_shapes=list(scratch),
        compiler_params=pltpu.CompilerParams(vmem_limit_bytes=limit << 20),
        cost_estimate=pl.CostEstimate(flops=flops, bytes_accessed=moved, transcendentals=0),
    )

    def run(*args):
        placed = [
            pltpu.with_memory_space_constraint(jnp.asarray(arg), pltpu.HBM) if spec is HB else arg
            for arg, spec in zip(args, ins)
        ]
        return kernel(*placed)

    return run


def started(pairs, sems, first=0):
    copies = []
    for n, (source, target) in enumerate(pairs):
        copy = pltpu.make_async_copy(source, target, sems.at[first + n])
        copy.start()
        copies.append(copy)
    return copies


def buffers(*tables):
    return [pltpu.VMEM(table.shape, table.dtype) for table in tables]


def array(*shape):
    return jax.ShapeDtypeStruct(shape, F32)


def mm(a, b):
    return jnp.dot(a, b, preferred_element_type=F32)


def halves(value):
    top = value.astype(BF16)
    return top, (value - top.astype(F32)).astype(BF16)


def np_halves(matrix):
    matrix = np.asarray(matrix, np.float32)
    top = matrix.astype(BF16)
    return top, (matrix - top.astype(np.float32)).astype(BF16)


def send_kernel(
    tile_ref, info_ref, data_ref, out_ref,
    data_s, out_s, hit_s, count_s, place_s, source_s, source_smem, sems,
):
    (data_copy,) = started([(data_ref, data_s)], sems)
    tile = tile_ref[...]
    column = tile >> 1
    high_part = column >> 6
    grid_x = (high_part * 43691) >> 17
    grid_y = column - grid_x * (CY * SIZE_Y)
    owner_y = ((grid_y >> 3) * 43) >> 7
    owner = (grid_x >> 5) * SIZE_Y + owner_y
    cell = (tile & 1) * (CX * CY) + (grid_x & (CX - 1)) * CY + (grid_y - owner_y * CY)
    slot = lax.broadcasted_iota(jnp.int32, tile.shape, 0) * 128 + lax.broadcasted_iota(
        jnp.int32, tile.shape, 1
    )
    code = jnp.where(slot < info_ref[0], cell, DEAD)
    rows = lax.broadcasted_iota(jnp.int32, (128, 128), 0)
    before = lax.broadcasted_iota(jnp.int32, (128, 256), 0)
    after = lax.broadcasted_iota(jnp.int32, (128, 256), 1)
    prefix = jnp.where((before < after) | (after >= 128), 1.0, 0.0).astype(BF16)
    for c in range(32):
        hit = jnp.where(rows == owner[c : c + 1], 1.0, 0.0)
        hit_s[:, c * 128 : (c + 1) * 128] = hit.astype(BF16)
    for g in range(8):
        chunks = [hit_s[:, c * 128 : (c + 1) * 128] for c in range(g * 4, g * 4 + 4)]
        count_s[g * 512 : (g + 1) * 512, :] = mm(jnp.concatenate(chunks, axis=0), prefix)
    base = jnp.zeros((128, 128), F32)
    lane = lax.broadcasted_iota(jnp.int32, (1, 128), 1)
    for c in range(32):
        counted = count_s[c * 128 : (c + 1) * 128, :128] + base
        base = base + count_s[c * 128 : (c + 1) * 128, 128:]
        hit = rows == owner[c : c + 1]
        rank = jnp.sum(jnp.where(hit, counted, 0.0), axis=0, keepdims=True)
        place = rows[:CAP] == rank.astype(jnp.int32)
        ids = code[c : c + 1]
        values = (ids >> 4, ids & 15, c * 2 + (lane >> 6), lane & 63)
        both = [jnp.where(place, value.astype(F32), 0.0) for value in values]
        place_s[:, c * 128 : (c + 1) * 128] = jnp.concatenate(both, axis=0).astype(BF16)
    found = lax.dot_general(
        hit_s[...], place_s[...], (((1,), (1,)), ((), ())), preferred_element_type=F32
    )
    source = found * 64.0 + pltpu.roll(found, 128 - CAP, 1)
    source_s[...] = pltpu.roll(source, 64, 1).astype(jnp.int32)
    (source_copy,) = started([(source_s, source_smem)], sems, 1)
    lane = lax.broadcasted_iota(jnp.int32, (128, 128), 1)
    ids = jnp.where(lane < CAP, found * 16.0 + pltpu.roll(found, 128 - CAP, 1), 0.0)
    ids = pltpu.roll(ids, info_ref[1], 1)
    for d in range(DEVICES):
        at = d * ROWS + CAP
        out_s[at : at + 1, :] = ids[d : d + 1]
    source_copy.wait()
    data_copy.wait()
    copies = []
    for part in range(4):

        def body(n, carry):
            for q in range(4):
                d = part * 32 + n * 4 + q
                for r in range(CAP):
                    out_s[pl.ds(d * ROWS + r, 1), :] = data_s[pl.ds(source_smem[d, r], 1), :]
            return carry

        lax.fori_loop(0, 8, body, 0)
        at = pl.ds(part * 32 * ROWS, 32 * ROWS)
        copies += started([(out_s.at[at], out_ref.at[at])], sems, 2 + part)
    for copy in copies:
        copy.wait()


def send(tile, info, data):
    return call(
        send_kernel,
        array(DEVICES * ROWS, 128),
        [VM, SM, HB],
        [
            pltpu.VMEM((4096, 128), F32),
            pltpu.VMEM((DEVICES * ROWS, 128), F32),
            pltpu.VMEM((128, 4096), BF16),
            pltpu.VMEM((4096, 256), F32),
            pltpu.VMEM((128, 4096), BF16),
            pltpu.VMEM((128, 128), jnp.int32),
            pltpu.SMEM((128, 128), jnp.int32),
            pltpu.SemaphoreType.DMA((6,)),
        ],
        outs=HB,
        limit=20,
    )(tile, info, data)


def thin_pair(count):
    matrix = np.zeros((count // 2 + 1, count))
    for i in range(count // 2 + 1):
        for source, weight in ((2 * i - 1, 0.5), (2 * i, 1.0), (2 * i + 1, 0.5)):
            if 0 <= source < count:
                matrix[i, source] = weight
    return matrix


def thin_cycle(length):
    matrix = np.zeros((length, length // 2))
    for i in range(length // 2):
        matrix[2 * i, i] += 1.0
        matrix[(2 * i - 1) % length, i] += 0.5
        matrix[(2 * i + 1) % length, i] += 0.5
    return matrix


def grow_matrix(count, source):
    matrix = np.zeros((count, source))
    for i in range(count):
        if i % 2 == 0:
            matrix[i, i // 2] = 1.0
        else:
            matrix[i, i // 2] = 0.5
            matrix[i, i // 2 + 1] = 0.5
    return matrix


def padded(matrix, rows, columns):
    out = np.zeros((rows, columns))
    out[: matrix.shape[0], : matrix.shape[1]] = matrix
    return out


def twice(matrix):
    return np.kron(np.eye(2), matrix)


def plain(matrix):
    return np.asarray(matrix, np.float32).astype(BF16)


def top_rows_matrix():
    rows_x = padded(thin_pair(17), 9, 17)
    rows_y = padded(thin_pair(13), 8, 16)
    rows_y[7] = 0.0
    matrix = np.zeros((2 * TOP_ROWS, 17 * 16))
    for i in range(9):
        for j in range(8):
            line = (j // 2) * 8 + i if i < 8 else 32 + j // 2
            matrix[(j % 2) * TOP_ROWS + line] = np.kron(rows_x[i], rows_y[j])
    return matrix


def exact_left(matrix, value):
    matrix = matrix[...]
    top, rest = halves(value)
    return mm(matrix, top) + mm(matrix, rest)


def exact_right(value, matrix):
    matrix = matrix[...]
    top, rest = halves(value)
    return mm(top, matrix) + mm(rest, matrix)


def collect_kernel(in_ref, *refs):
    tables = refs[:4]
    outs = refs[-18:-13]
    data_s, ids_s, slab_s = refs[-13:-10]
    thin_z_ref, thin_y_ref, top_rows_ref, top_z_ref = refs[-10:-6]
    fine_ref, mid_ref, low_ref, high_ref, top_ref, sems = refs[-6:]
    table_copies = started(list(zip(tables, refs[-10:-6])), sems)
    for c in range(DEVICES // 4):
        total = None
        for j in range(4):
            base = (c * 4 + j) * ROWS
            top, rest = halves(in_ref[base : base + CAP, :])
            start = (c * 4 + j) * CAP
            data_s[start : start + CAP, :128] = top
            data_s[start : start + CAP, 128:] = rest
            line = in_ref[base + CAP : base + CAP + 1, :]
            total = line if total is None else total + line
        ids_s[c : c + 1, :] = total.astype(jnp.int32)
    rows = lax.broadcasted_iota(jnp.int32, (256, 128), 0).astype(F32).astype(BF16)
    one, zero = jnp.ones((256, 128), BF16), jnp.zeros((256, 128), BF16)

    def block(b, carry):
        first = pl.multiple_of(b * 256, 256)
        acc = jnp.zeros((256, 256), F32)
        for k in range(16):
            parts = []
            for q in range(2):
                ids = jnp.clip(ids_s[2 * k + q : 2 * k + q + 1, :] - first, -1, 256)
                line = jnp.broadcast_to(ids.astype(F32), (16, 128)).astype(BF16)
                parts.append(jnp.where(rows == jnp.concatenate([line] * 16, axis=0), one, zero))
            acc = acc + mm(jnp.concatenate(parts, axis=1), data_s[k * 256 : (k + 1) * 256, :])
        fine_ref[pl.ds(first, 256), :] = acc[:, :128] + acc[:, 128:]
        return carry

    lax.fori_loop(0, 6, block, 0)
    out_copies = started([(fine_ref, outs[0])], sems, 4)
    for i in range(17):
        total = None
        for x, weight in ((2 * i, 1.0), (2 * i - 1, 0.5), (2 * i + 1, 0.5)):
            if 0 <= x < CX:
                term = jnp.concatenate(
                    [
                        fine_ref[h * CX * CY + x * CY : h * CX * CY + (x + 1) * CY, :]
                        for h in range(2)
                    ],
                    axis=1,
                )
                term = term if weight == 1.0 else weight * term
                total = term if total is None else total + term
        slab_s[i * CY : (i + 1) * CY, :] = total
    slab_s[17 * CY :, :] = jnp.zeros((7 * CY, NZ), F32)
    for copy in table_copies:
        copy.wait()
    for g in range(3):
        part = exact_right(slab_s[g * 192 : (g + 1) * 192, :], thin_z_ref)
        mid_ref[g * 128 : (g + 1) * 128, :] = exact_left(thin_y_ref, part)
    for h in range(2):
        for c in range(4):
            at = slice((h * 4 + c) * CX, (h * 4 + c + 1) * CX)
            low_ref[at, :] = fine_ref[pl.ds(h * CX * CY + c, CX, stride=CY), :]
            high_ref[at, :] = fine_ref[pl.ds(h * CX * CY + CY - 4 + c, CX, stride=CY), :]
    for j in range(5):
        at = slice(256 + j * 24, 256 + (j + 1) * 24)
        low_ref[at, :] = mid_ref[pl.ds(j, 24, stride=16), :]
        high_ref[at, :] = mid_ref[pl.ds(8 + j, 24, stride=16), :]
    out_copies += started([(mid_ref, outs[1]), (low_ref, outs[2]), (high_ref, outs[3])], sems, 5)
    stacked = exact_left(top_rows_ref, mid_ref[: 17 * 16, :])
    pair = jnp.concatenate([stacked[:TOP_ROWS], stacked[TOP_ROWS:]], axis=1)
    top_charge = exact_right(pair, top_z_ref)
    for s in range(SIZE_X):
        top_ref[s * TOP_ROWS : (s + 1) * TOP_ROWS, :] = top_charge
    out_copies += started([(top_ref, outs[4])], sems, 8)
    for copy in out_copies:
        copy.wait()


def collect(arrived, *after):
    tables = (
        plain(thin_cycle(NZ)),
        plain(np.kron(np.eye(8), padded(thin_pair(CY), 16, CY))),
        plain(top_rows_matrix()),
        plain(twice(thin_cycle(128))),
    )
    out = (
        array(2 * CX * CY, 128),
        array(24 * 16, 128),
        array(SEND, 128),
        array(SEND, 128),
        array(SIZE_X * TOP_ROWS, 128),
    )
    return call(
        collect_kernel,
        out,
        [VM] + [HB] * (4 + len(after)),
        [
            pltpu.VMEM((DEVICES * CAP, 256), BF16),
            pltpu.VMEM((DEVICES // 4, 128), jnp.int32),
            pltpu.VMEM((24 * CY, NZ), F32),
            *buffers(*tables),
            *buffers(*out),
            pltpu.SemaphoreType.DMA((9,)),
        ],
        outs=HB,
        limit=20,
    )(arrived, *tables, *after)


def merge_kernel(
    fine_hbm, mid_hbm, before_ref, behind_ref, halo_hbm, wide_hbm, low_hbm, high_hbm,
    fine_s, mid_ref, halo_ref, wide_ref, low_ref, high_ref, sems,
):
    pairs = [(mid_hbm, mid_ref)]
    for h in range(2):
        for first, at in ((0, 0), (CX - 4, 4)):
            start = (h * CX + first) * CY
            pairs.append(
                (fine_hbm.at[pl.ds(start, 4 * CY)], fine_s.at[pl.ds((h * 8 + at) * CY, 4 * CY)])
            )
    mid_copy, *fine_copies = started(pairs, sems)
    for h in range(2):
        for c in range(4):
            at = slice((h * 4 + c) * CX, (h * 4 + c + 1) * CX)
            start = h * CX * 8 + c
            halo_ref[pl.ds(start, CX, stride=8), :] = behind_ref[at, :]
            halo_ref[pl.ds(start + 4, CX, stride=8), :] = before_ref[at, :]
    out_copies = started([(halo_ref, halo_hbm)], sems, 5)
    mid_copy.wait()
    for i in range(24):
        wide_ref[i * YD : i * YD + 16, :] = mid_ref[i * 16 : (i + 1) * 16, :]
        wide_ref[i * YD + 16 : (i + 1) * YD, :] = jnp.zeros((16, 128), F32)
    for j in range(5):
        at = slice(256 + j * 24, 256 + (j + 1) * 24)
        behind = behind_ref[at, :]
        if j == 0:
            behind = behind + wide_ref[pl.ds(12, 24, stride=YD), :]
        wide_ref[pl.ds(12 + j, 24, stride=YD), :] = behind
        before = before_ref[at, :]
        row = 28 + j if j < 4 else 0
        if j == 4:
            before = before + wide_ref[pl.ds(0, 24, stride=YD), :]
        wide_ref[pl.ds(row, 24, stride=YD), :] = before
    out_copies += started([(wide_ref, wide_hbm)], sems, 6)
    for copy in fine_copies:
        copy.wait()
    for ref, first, at_fine, mid_first in ((low_ref, 0, 0, 0), (high_ref, CX - 4, 4, 12)):
        for h in range(2):
            for x in range(4):
                at = h * 128 + x * YD
                source = (h * 8 + at_fine + x) * CY
                ref[at : at + CY, :] = fine_s[source : source + CY, :]
                source = (h * CX + first + x) * 8
                ref[at + CY : at + YD, :] = halo_ref[source : source + 8, :]
        for i in range(5):
            base = (mid_first + i) * YD
            at = 256 + i * 24
            ref[at : at + 16, :] = wide_ref[base : base + 16, :]
            ref[at + 16 : at + 24, :] = (
                wide_ref[base + 16 : base + 24, :] + wide_ref[base + 24 : base + 32, :]
            )
    out_copies += started([(low_ref, low_hbm), (high_ref, high_hbm)], sems, 7)
    for copy in out_copies:
        copy.wait()


def merge(fine, mid, before, behind):
    out = (array(2 * CX * 8, 128), array(24 * YD, 128), array(SEND, 128), array(SEND, 128))
    return call(
        merge_kernel,
        out,
        [HB, HB, VM, VM],
        [
            pltpu.VMEM((16 * CY, 128), F32),
            pltpu.VMEM((24 * 16, 128), F32),
            *buffers(*out),
            pltpu.SemaphoreType.DMA((9,)),
        ],
        outs=HB,
    )(fine, mid, before, behind)


def z_matrices(period, copies):
    half = period // 2
    z = np.arange(period)[:, None]
    f = np.arange(half)[None, :]
    angle = 2 * np.pi * ((z * f) % period) / period
    cosine, sine = np.cos(angle), -np.sin(angle)
    sine[:, 0] = (-1.0) ** np.arange(period)
    scale = np.full((half, 1), 2.0 / period)
    scale[0] = 1.0 / period
    forward = np.zeros((256, 256))
    inverse = np.zeros((256, 256))
    for c in range(copies):
        rows = slice(c * period, (c + 1) * period)
        real = slice(c * half, (c + 1) * half)
        imag = slice(128 + c * half, 128 + (c + 1) * half)
        forward[rows, real] = cosine
        forward[rows, imag] = sine
        inverse[real, rows] = scale * cosine.T
        inverse[imag, rows] = scale * sine.T
    return forward, inverse


def y_matrices():
    order = np.concatenate([np.arange(17), np.arange(31, 16, -1)])
    y = np.arange(YD)
    angle = 2 * np.pi * ((order[:, None] * y[None, :]) % YD) / YD
    cosine, sine = np.cos(angle), np.sin(angle)
    forward = np.block([[cosine, sine], [-sine, cosine]])
    inverse = np.block([[cosine.T, -sine.T], [sine.T, cosine.T]]) / YD
    return np.kron(np.eye(4), forward), np.kron(np.eye(4), inverse)


def stacked_rows(matrix):
    top, rest = np_halves(matrix)
    return np.concatenate([top, rest], axis=0)


def stacked_cols(matrix):
    top, rest = np_halves(matrix)
    return np.concatenate([top, rest], axis=1)


def right_product(value, matrix_ref):
    top, rest = halves(value)
    return (
        mm(top, matrix_ref[:256, :]) + mm(top, matrix_ref[256:, :]) + mm(rest, matrix_ref[:256, :])
    )


def left_product(matrix_ref, value):
    top, rest = halves(value)
    return (
        mm(matrix_ref[:, :256], top) + mm(matrix_ref[:, 256:], top) + mm(matrix_ref[:, :256], rest)
    )


def special_mask(copies, rows):
    lane = lax.broadcasted_iota(jnp.int32, (rows, 128), 1)
    row = lax.broadcasted_iota(jnp.int32, (rows, 128), 0)
    return (lane & (128 // copies - 1)) == 0, row


def forward_chunk(value, z_ref, y_ref, copies):
    z_freq = right_product(value, z_ref)
    stacks = []
    for h in range(2):
        pieces = []
        for q in range(4):
            slab = z_freq[(h * 4 + q) * YD : (h * 4 + q + 1) * YD]
            pieces += [slab[:, :128], slab[:, 128:]]
        stacks.append(jnp.concatenate(pieces, axis=0))
    freq = left_product(y_ref, jnp.concatenate(stacks, axis=1))
    lane_special, row = special_mask(copies, 16)
    special = lane_special & (row != 0)
    slabs = []
    for h in range(2):
        for q in range(4):
            slab = freq[q * 64 : (q + 1) * 64, h * 128 : (h + 1) * 128]
            ar, br, ai, bi = slab[:16], slab[16:32], slab[32:48], slab[48:]
            slabs.append(
                jnp.concatenate(
                    [
                        jnp.where(special, 0.5 * (ar + br), ar),
                        jnp.where(special, 0.5 * (ai + bi), br),
                        jnp.where(special, 0.5 * (ai - bi), ai),
                        jnp.where(special, 0.5 * (br - ar), bi),
                    ],
                    axis=0,
                )
            )
    return slabs


def inverse_chunk(slabs, z_ref, y_ref):
    stacks = [jnp.concatenate(slabs[h * 4 : h * 4 + 4], axis=0) for h in range(2)]
    space = left_product(y_ref, jnp.concatenate(stacks, axis=1))
    rows = []
    for h in range(2):
        for q in range(4):
            slab = space[q * 64 : (q + 1) * 64, h * 128 : (h + 1) * 128]
            rows.append(jnp.concatenate([slab[:YD], slab[YD:]], axis=1))
    return right_product(jnp.concatenate(rows, axis=0), z_ref)


def taps_kernel(copies, in_ref, z_ref, y_ref, after_ref, out_ref):
    lane_special, row = special_mask(copies, YD)
    special = lane_special & ((row == 0) | (row == 16))
    for p in range(2):
        slabs = forward_chunk(in_ref[p * 256 : (p + 1) * 256, :], z_ref, y_ref, copies)
        for j in range(8):
            dx = p * 8 + j
            if dx > 8:
                break
            real, imag = slabs[j][:YD], slabs[j][YD:]
            values = (real, jnp.where(special, imag, real), jnp.where(special, 0.0, imag))
            for part in range(3):
                at = (part * 9 + dx) * YD
                out_ref[at : at + YD, :] = values[part]


def taps(kernel, copies, z_matrix, y_matrix, after):
    flipped = kernel[:, ::-1, ::-1]
    tall = jnp.concatenate(
        [flipped[:, 4:], jnp.zeros((9, YD - 9, 9), F32), flipped[:, :4]], axis=1
    )
    period = 256 // copies
    wide = jnp.concatenate(
        [tall[:, :, 4:], jnp.zeros((9, YD, period - 9), F32), tall[:, :, :4]], axis=2
    )
    wide = jnp.concatenate([wide] * copies, axis=2)
    wide = jnp.concatenate([wide, jnp.zeros((7, YD, 256), F32)], axis=0)
    return call(
        functools.partial(taps_kernel, copies), array(27 * YD, 128), [VM] * 3 + [HB]
    )(wide.reshape(16 * YD, 256), z_matrix, y_matrix, after)


def own_kernel(fine_hbm, halo_hbm, z_ref, y_ref, out_ref, fine_s, halo_s, sems):
    for copy in started([(fine_hbm, fine_s), (halo_hbm, halo_s)], sems):
        copy.wait()
    for p in range(CX // 8):
        columns = []
        for h in range(2):
            rows = []
            for j in range(8):
                n = h * CX + p * 8 + j
                rows += [fine_s[n * CY : (n + 1) * CY, :], halo_s[n * 8 : (n + 1) * 8, :]]
            columns.append(jnp.concatenate(rows, axis=0))
        slabs = forward_chunk(jnp.concatenate(columns, axis=1), z_ref, y_ref, 1)
        for j in range(8):
            out_ref[(p * 8 + j) * 64 : (p * 8 + j + 1) * 64, :] = slabs[j]


def convolve(copies, first, count, taps_ref, freq_s, conv_s):
    lane_special, row = special_mask(copies, 8)
    for v in range(2):
        sums = [[None] * 4 for _ in range(count)]
        for dx in range(9):
            coefs = []
            for half in range(2):
                at = dx * YD + half * 16 + v * 8
                coefs.append([taps_ref[at + part * 288 : at + part * 288 + 8, :] for part in range(3)])
            for j in range(count):
                old = sums[j]
                for half in range(2):
                    at = (first + j + dx) * 64 + v * 8 + half * 16
                    re = freq_s[at : at + 8, :]
                    im = freq_s[at + 32 : at + 40, :]
                    a, t, b = coefs[half]
                    new_re = a * re - b * im
                    new_im = b * re + t * im
                    old[2 * half] = new_re if dx == 0 else old[2 * half] + new_re
                    old[2 * half + 1] = new_im if dx == 0 else old[2 * half + 1] + new_im
        special = lane_special & (row != 0) if v == 0 else lane_special
        for j in range(count):
            ar, ai, br, bi = sums[j]
            at = (first + j) * 64 + v * 8
            conv_s[at : at + 8, :] = jnp.where(special, ar - bi, ar)
            conv_s[at + 16 : at + 24, :] = jnp.where(special, ar + bi, br)
            conv_s[at + 32 : at + 40, :] = jnp.where(special, ai + br, ai)
            conv_s[at + 48 : at + 56, :] = jnp.where(special, br - ai, bi)


def wide_slab(ref, index):
    at = 256 + index * 24
    last = ref[at + 16 : at + 24, :]
    row = lax.broadcasted_iota(jnp.int32, (8, 128), 0)
    return jnp.concatenate(
        [ref[at : at + 16, :], jnp.where(row < 4, last, 0.0), jnp.where(row < 4, 0.0, last)], axis=0
    )


def levels_kernel(
    own_ref, before_ref, behind_ref, *refs
):
    zf_ref, yf_ref = refs[:2]
    near_ref, mid_ref, grow_ref, freq_s, conv_s, mid_freq_s, mid_conv_s = refs[10:17]
    wide_ref, mzf_ref, near_taps, mid_taps, zi_ref, yi_ref, mzi_ref, sems = refs[17:]
    copies = started(list(zip(refs[2:10], (*refs[17:24], grow_ref))), sems)
    freq_s[4 * 64 : 36 * 64, :] = own_ref[...]
    edges = [
        jnp.concatenate([ref[:128, :], ref[128:256, :]], axis=1) for ref in (before_ref, behind_ref)
    ]
    slabs = forward_chunk(jnp.concatenate(edges, axis=0), zf_ref, yf_ref, 1)
    for j in range(8):
        at = j if j < 4 else 32 + j
        freq_s[at * 64 : (at + 1) * 64, :] = slabs[j]
    zero = jnp.zeros((YD, 128), F32)
    copies[0].wait()
    copies[1].wait()
    for p in range(3):
        pairs = []
        for j in range(8):
            pair = []
            for n in (p * 8 + j, p * 8 + j + 9):
                if n > 24 or (n == p * 8 + j and n > 16):
                    slab = zero
                elif n < 4:
                    slab = wide_slab(before_ref, n)
                elif n > 20:
                    slab = wide_slab(behind_ref, n - 20)
                else:
                    slab = wide_ref[(n - 4) * YD : (n - 3) * YD, :]
                    if n == 4:
                        slab = slab + wide_slab(before_ref, 4)
                    if n == 20:
                        slab = slab + wide_slab(behind_ref, 0)
                pair.append(slab)
            pairs.append(jnp.concatenate(pair, axis=1))
        slabs = forward_chunk(jnp.concatenate(pairs, axis=0), mzf_ref, yf_ref, 2)
        for j in range(8):
            at = p * 8 + j
            mid_freq_s[at * 64 : (at + 1) * 64, :] = slabs[j]
    for copy in copies[2:]:
        copy.wait()
    for p in range(4):
        convolve(1, p * 8, 8, near_taps, freq_s, conv_s)
        slabs = [conv_s[(p * 8 + j) * 64 : (p * 8 + j + 1) * 64, :] for j in range(8)]
        space = inverse_chunk(slabs, zi_ref, yi_ref)
        for j in range(8):
            x = p * 8 + j
            near_ref[x * CY : (x + 1) * CY, :] = space[j * YD : j * YD + CY]
    mid_conv_s[9 * 64 :, :] = jnp.zeros((7 * 64, 128), F32)
    for first, count in ((0, 5), (5, 4)):
        convolve(2, first, count, mid_taps, mid_freq_s, mid_conv_s)
    for p in range(2):
        slabs = [mid_conv_s[(p * 8 + j) * 64 : (p * 8 + j + 1) * 64, :] for j in range(8)]
        space = inverse_chunk(slabs, mzi_ref, yi_ref)
        for j in range(8):
            i = p * 8 + j
            if i < 9:
                mid_ref[i * 16 : (i + 1) * 16, :] = space[j * YD : j * YD + 16]


def gauss(index, period, width):
    distance = jnp.minimum(index, period - index).astype(F32)
    return jnp.exp(-(distance * distance) / (width * width))


def gauss_kernel(weights_ref, widths_ref, info_ref, after_ref, x_ref, y_ref, z_ref):
    first_x = info_ref[2] * 8
    first_y = info_ref[3] * 6
    row = lax.broadcasted_iota(jnp.int32, (16, 256), 0)
    column = lax.broadcasted_iota(jnp.int32, (16, 256), 1)
    source = jnp.where(column < 128, column, (column - 128) * 8 + 8)
    offset = (first_x + row - source) & 127
    for k in range(4):
        value = jnp.where(column < 144, gauss(offset, 128, widths_ref[k]), 0.0)
        for n, part in enumerate(halves(value)):
            x_ref[n * 64 + k * 16 : n * 64 + (k + 1) * 16, :] = part
    row = lax.broadcasted_iota(jnp.int32, (128, 128), 0)
    column = lax.broadcasted_iota(jnp.int32, (128, 128), 1)
    for k in range(4):
        value = gauss((row - column) & 63, 64, widths_ref[k]) * weights_ref[k]
        value = jnp.where((row >> 6) == (column >> 6), value, 0.0)
        for n, part in enumerate(halves(value)):
            z_ref[(n * 4 + k) * 128 : (n * 4 + k + 1) * 128, :] = part
    row = lax.broadcasted_iota(jnp.int32, (64, 128), 0)
    column = lax.broadcasted_iota(jnp.int32, (64, 128), 1)
    target = (row >> 3) * 6 + (row & 7)
    source = first_y + (column & 3) * 2 + ((column >> 4) & 1)
    offset = target - source
    offset = jnp.where(offset < 0, offset + 48, offset)
    offset = jnp.where(offset >= 48, offset - 48, offset)
    chosen = (column >> 2) & 3
    value = jnp.zeros((64, 128), F32)
    for k in range(4):
        value = jnp.where(chosen == k, gauss(offset, 48, widths_ref[k]), value)
    for n, part in enumerate(halves(jnp.where(column < 32, value, 0.0))):
        y_ref[n * 64 : (n + 1) * 64, :] = part


def top_kernel(in_ref, x_ref, y_ref, z_ref, out_ref, plane_s, depth_s):
    left = (x_ref[:64, :], x_ref[64:, :])
    for jp in range(4):
        tiles = [in_ref[s * TOP_ROWS + jp * 8 : s * TOP_ROWS + jp * 8 + 8, :] for s in range(16)]
        tiles.append(in_ref[pl.ds(32 + jp, SIZE_X, stride=TOP_ROWS), :])
        tiles.append(jnp.zeros((112, 128), F32))
        right = halves(jnp.concatenate(tiles, axis=0))
        plane = mm(left[0], right[0]) + mm(left[0], right[1]) + mm(left[1], right[0])
        for k in range(4):
            plane_s[(k * 4 + jp) * 16 : (k * 4 + jp + 1) * 16, :] = plane[k * 16 : (k + 1) * 16]
    for k in range(4):
        weight = [z_ref[(n * 4 + k) * 128 : (n * 4 + k + 1) * 128, :] for n in range(2)]
        value = halves(plane_s[k * 64 : (k + 1) * 64, :])
        depth_s[k * 64 : (k + 1) * 64, :] = (
            mm(value[0], weight[0]) + mm(value[0], weight[1]) + mm(value[1], weight[0])
        )
    lane = lax.broadcasted_iota(jnp.int32, (16, 128), 1)
    tiles = []
    for ip in range(5):
        first = depth_s[pl.ds(2 * ip, 16, stride=16), :]
        second = depth_s[pl.ds(2 * ip + 1, 16, stride=16), :]
        even = jnp.where(lane < 64, first, pltpu.roll(second, 64, 1))
        odd = jnp.where(lane < 64, pltpu.roll(first, 64, 1), second)
        tiles.append(jnp.concatenate([even, odd, jnp.zeros((96, 128), F32)], axis=0))
    right = halves(jnp.concatenate(tiles, axis=1))
    left = (y_ref[:64, :], y_ref[64:, :])
    out_ref[...] = mm(left[0], right[0]) + mm(left[0], right[1]) + mm(left[1], right[0])


def finish_kernel(
    near_ref, mid_ref, top_ref, *refs
):
    grow_ref, out_ref, grown_s = refs
    grow_top, grow_z = grow_ref[:128, :], grow_ref[128:256, :]
    grow_fine, grow_y = grow_ref[256:, :128], grow_ref[256:272, 128:]
    total = top_ref[:8, :]
    for s in range(1, SIZE_Y):
        total = total + top_ref[s * 8 : (s + 1) * 8, :]
    lanes = []
    for ip in range(5):
        lanes.append(exact_right(total[:, ip * 128 : (ip + 1) * 128], grow_top))
    deep = jnp.concatenate(lanes, axis=1)
    tiles = []
    for i in range(17):
        tile = deep[:, (i // 2) * 128 : (i // 2 + 1) * 128]
        if i % 2:
            tile = 0.5 * (tile + deep[:, (i // 2 + 1) * 128 : (i // 2 + 2) * 128])
        tiles.append(tile)
    flat = jnp.concatenate(tiles, axis=1)
    flat = jnp.concatenate([flat, jnp.zeros((120, 17 * 128), F32)], axis=0)
    tall = exact_left(grow_y, flat)
    slabs = []
    for i in range(24):
        if i > 16:
            slabs.append(jnp.zeros((16, 128), F32))
            continue
        h = i // 9
        slabs.append(
            tall[:, i * 128 : (i + 1) * 128]
            + mid_ref[(i - 9 * h) * 16 : (i - 9 * h + 1) * 16, h * 128 : (h + 1) * 128]
        )
    for g in range(3):
        part = exact_right(jnp.concatenate(slabs[g * 8 : (g + 1) * 8], axis=0), grow_z)
        grown_s[g * 192 : (g + 1) * 192, :] = exact_left(grow_fine, part)
    for x in range(CX):
        at = slice(x * CY, (x + 1) * CY)
        i = x // 2
        value = grown_s[i * CY : (i + 1) * CY, :]
        if x % 2:
            value = 0.5 * (value + grown_s[(i + 1) * CY : (i + 2) * CY, :])
        out_ref[at, :] = near_ref[at, :] + value


def swap(to_low, to_high, axis):
    count = lax.axis_size(axis)
    forward = [(i, (i + 1) % count) for i in range(count)]
    backward = [(target, source) for source, target in forward]
    before = lax.ppermute(to_high, axis, forward)
    behind = lax.ppermute(to_low, axis, backward)
    return before, behind


def on_device(
    charge_blocks, block_tile, block_count, near_kernel, mid_kernel, top_weights, top_widths
):
    at_x = lax.axis_index("gx")
    at_y = lax.axis_index("gy")
    info = jnp.stack(
        [block_count[0], ((at_x * SIZE_Y + at_y) % 4) * CAP, at_x, at_y]
    ).astype(jnp.int32)
    outgoing = send(block_tile.reshape(32, 128), info, charge_blocks)
    arrived = lax.all_to_all(
        outgoing.reshape(DEVICES, 1, ROWS * 128),
        ("gx", "gy"),
        split_axis=0,
        concat_axis=0,
        tiled=True,
    ).reshape(DEVICES * ROWS, 128)

    z_fine, z_fine_back = z_matrices(256, 1)
    z_mid, z_mid_back = z_matrices(128, 2)
    y_forward, y_back = y_matrices()
    zf, yf = stacked_rows(z_fine), stacked_cols(y_forward)
    zi, yi = stacked_rows(z_fine_back), stacked_cols(y_back)
    mzf, mzi = stacked_rows(z_mid), stacked_rows(z_mid_back)
    near_taps = taps(near_kernel, 1, zf, yf, outgoing)
    mid_taps = taps(mid_kernel, 2, mzf, yf, outgoing)

    bells = call(
        gauss_kernel,
        tuple(jax.ShapeDtypeStruct(n, BF16) for n in ((128, 256), (128, 128), (1024, 128))),
        [SM, SM, SM, HB],
    )(top_weights, top_widths, info, outgoing)

    fine, mid, low, high, top = collect(arrived, near_taps, mid_taps, bells[0])
    before, behind = swap(low, high, "gy")
    tops = lax.all_to_all(
        top.reshape(SIZE_X, TOP_ROWS, 128), "gx", split_axis=0, concat_axis=0, tiled=True
    )
    tops = tops.reshape(SIZE_X * TOP_ROWS, 128)
    partial = call(
        top_kernel,
        array(64, 640),
        [VM] * 4,
        [pltpu.VMEM((256, 128), F32), pltpu.VMEM((256, 128), F32)],
    )(tops, *bells)
    partial = lax.all_to_all(
        partial.reshape(SIZE_Y, 8, 640), "gy", split_axis=0, concat_axis=0, tiled=True
    ).reshape(64, 640)
    halo, wide, low, high = merge(fine, mid, before, behind)
    before, behind = swap(low, high, "gx")
    own = call(
        own_kernel,
        array(CX * 64, 128),
        [HB, HB, VM, VM],
        buffers(fine, halo) + [pltpu.SemaphoreType.DMA((2,))],
    )(fine, halo, zf, yf)
    grow_z = grow_matrix(2 * 64, 65)
    grow_z[:, 0] += grow_z[:, 64]
    grow_fine_z = grow_matrix(2 * 128, 129)
    grow_fine_z[:, 0] += grow_fine_z[:, 128]
    grow_y = np.zeros((192, 256))
    grow_y[:, :128] = np.kron(np.eye(8), padded(grow_matrix(CY, 13), CY, 16))
    grow_y[:16, 128:135] = padded(grow_matrix(13, 7), 16, 7)
    grow = plain(np.concatenate([twice(grow_z[:, :64].T), grow_fine_z[:, :128].T, grow_y]))
    tables = (wide, mzf, near_taps, mid_taps, zi, yi, mzi)
    near, mid_near, grow = call(
        levels_kernel,
        (array(CX * CY, NZ), array(9 * 16, 256), jax.ShapeDtypeStruct(grow.shape, BF16)),
        [VM] * 5 + [HB] * 8,
        [
            pltpu.VMEM((40 * 64, 128), F32),
            pltpu.VMEM((32 * 64, 128), F32),
            pltpu.VMEM((24 * 64, 128), F32),
            pltpu.VMEM((16 * 64, 128), F32),
            *buffers(*tables),
            pltpu.SemaphoreType.DMA((8,)),
        ],
        limit=14,
    )(own, before, behind, zf, yf, *tables, grow)
    out = call(
        finish_kernel, array(CX * CY, NZ), [VM] * 4, [pltpu.VMEM((24 * CY, NZ), F32)]
    )(near, mid_near, partial, grow)
    return out.reshape(CX, CY, NZ)


def solution(mesh):
    placed = (P(("gx", "gy"), None), P(("gx", "gy")), P(("gx", "gy")), P(), P(), P(), P())
    return jax.shard_map(
        on_device, mesh=mesh, in_specs=placed, out_specs=P("gx", "gy", None), check_vma=False
    )
```

```python
import functools

import jax
import jax.numpy as jnp
import numpy as np
from jax import lax
from jax.experimental import pallas as pl
from jax.experimental.pallas import tpu as pltpu
from jax.sharding import PartitionSpec as P


CX = 32
CY = 24
NZ = 256
CAP = 32
DEVICES = 128
ROWS = CAP + 1
SIZE_X = 16
SIZE_Y = 8
DEAD = 2047
SEND = 376
TOP_ROWS = 40
YD = 32
F32 = jnp.float32
BF16 = jnp.bfloat16
VM = pl.BlockSpec(memory_space=pltpu.VMEM)
SM = pl.BlockSpec(memory_space=pltpu.SMEM)
HB = pl.BlockSpec(memory_space=pltpu.HBM)


def call(body, out, ins, scratch=(), limit=10, flops=0, moved=0, outs=VM):
    many = isinstance(out, tuple)
    outs = outs if isinstance(outs, tuple) else (outs,) * (len(out) if many else 1)
    shapes = tuple(
        pltpu.HBM(shape.shape, shape.dtype) if spec is HB else shape
        for shape, spec in zip(out if many else (out,), outs)
    )
    kernel = pl.pallas_call(
        body,
        out_shape=shapes if many else shapes[0],
        in_specs=ins,
        out_specs=outs if many else outs[0],
        scratch_shapes=list(scratch),
        compiler_params=pltpu.CompilerParams(vmem_limit_bytes=limit << 20),
        cost_estimate=pl.CostEstimate(flops=flops, bytes_accessed=moved, transcendentals=0),
    )

    def run(*args):
        placed = [
            pltpu.with_memory_space_constraint(jnp.asarray(arg), pltpu.HBM) if spec is HB else arg
            for arg, spec in zip(args, ins)
        ]
        return kernel(*placed)

    return run


def started(pairs, sems, first=0):
    copies = []
    for n, (source, target) in enumerate(pairs):
        copy = pltpu.make_async_copy(source, target, sems.at[first + n])
        copy.start()
        copies.append(copy)
    return copies


def buffers(*tables):
    return [pltpu.VMEM(table.shape, table.dtype) for table in tables]


def array(*shape):
    return jax.ShapeDtypeStruct(shape, F32)


def mm(a, b):
    return jnp.dot(a, b, preferred_element_type=F32)


def halves(value):
    top = value.astype(BF16)
    return top, (value - top.astype(F32)).astype(BF16)


def np_halves(matrix):
    matrix = np.asarray(matrix, np.float32)
    top = matrix.astype(BF16)
    return top, (matrix - top.astype(np.float32)).astype(BF16)


def send_kernel(
    tile_ref, info_ref, data_ref, out_ref,
    data_s, out_s, hit_s, count_s, place_s, source_s, source_smem, sems,
):
    (data_copy,) = started([(data_ref, data_s)], sems)
    tile = tile_ref[...]
    column = tile >> 1
    high_part = column >> 6
    grid_x = (high_part * 43691) >> 17
    grid_y = column - grid_x * (CY * SIZE_Y)
    owner_y = ((grid_y >> 3) * 43) >> 7
    owner = (grid_x >> 5) * SIZE_Y + owner_y
    cell = (tile & 1) * (CX * CY) + (grid_x & (CX - 1)) * CY + (grid_y - owner_y * CY)
    slot = lax.broadcasted_iota(jnp.int32, tile.shape, 0) * 128 + lax.broadcasted_iota(
        jnp.int32, tile.shape, 1
    )
    code = jnp.where(slot < info_ref[0], cell, DEAD)
    rows = lax.broadcasted_iota(jnp.int32, (128, 128), 0)
    before = lax.broadcasted_iota(jnp.int32, (128, 256), 0)
    after = lax.broadcasted_iota(jnp.int32, (128, 256), 1)
    prefix = jnp.where((before < after) | (after >= 128), 1.0, 0.0).astype(BF16)
    for c in range(32):
        hit = jnp.where(rows == owner[c : c + 1], 1.0, 0.0)
        hit_s[:, c * 128 : (c + 1) * 128] = hit.astype(BF16)
    for g in range(8):
        chunks = [hit_s[:, c * 128 : (c + 1) * 128] for c in range(g * 4, g * 4 + 4)]
        count_s[g * 512 : (g + 1) * 512, :] = mm(jnp.concatenate(chunks, axis=0), prefix)
    base = jnp.zeros((128, 128), F32)
    lane = lax.broadcasted_iota(jnp.int32, (1, 128), 1)
    for c in range(32):
        counted = count_s[c * 128 : (c + 1) * 128, :128] + base
        base = base + count_s[c * 128 : (c + 1) * 128, 128:]
        hit = rows == owner[c : c + 1]
        rank = jnp.sum(jnp.where(hit, counted, 0.0), axis=0, keepdims=True)
        place = rows[:CAP] == rank.astype(jnp.int32)
        ids = code[c : c + 1]
        values = (ids >> 4, ids & 15, c * 2 + (lane >> 6), lane & 63)
        both = [jnp.where(place, value.astype(F32), 0.0) for value in values]
        place_s[:, c * 128 : (c + 1) * 128] = jnp.concatenate(both, axis=0).astype(BF16)
    found = lax.dot_general(
        hit_s[...], place_s[...], (((1,), (1,)), ((), ())), preferred_element_type=F32
    )
    source = found * 64.0 + pltpu.roll(found, 128 - CAP, 1)
    source_s[...] = pltpu.roll(source, 64, 1).astype(jnp.int32)
    (source_copy,) = started([(source_s, source_smem)], sems, 1)
    lane = lax.broadcasted_iota(jnp.int32, (128, 128), 1)
    ids = jnp.where(lane < CAP, found * 16.0 + pltpu.roll(found, 128 - CAP, 1), 0.0)
    ids = pltpu.roll(ids, info_ref[1], 1)
    for d in range(DEVICES):
        at = d * ROWS + CAP
        out_s[at : at + 1, :] = ids[d : d + 1]
    source_copy.wait()
    data_copy.wait()
    copies = []
    for part in range(4):

        def body(n, carry):
            for q in range(4):
                d = part * 32 + n * 4 + q
                for r in range(CAP):
                    out_s[pl.ds(d * ROWS + r, 1), :] = data_s[pl.ds(source_smem[d, r], 1), :]
            return carry

        lax.fori_loop(0, 8, body, 0)
        at = pl.ds(part * 32 * ROWS, 32 * ROWS)
        copies += started([(out_s.at[at], out_ref.at[at])], sems, 2 + part)
    for copy in copies:
        copy.wait()


def send(tile, info, data):
    return call(
        send_kernel,
        array(DEVICES * ROWS, 128),
        [VM, SM, HB],
        [
            pltpu.VMEM((4096, 128), F32),
            pltpu.VMEM((DEVICES * ROWS, 128), F32),
            pltpu.VMEM((128, 4096), BF16),
            pltpu.VMEM((4096, 256), F32),
            pltpu.VMEM((128, 4096), BF16),
            pltpu.VMEM((128, 128), jnp.int32),
            pltpu.SMEM((128, 128), jnp.int32),
            pltpu.SemaphoreType.DMA((6,)),
        ],
        outs=HB,
        limit=20,
    )(tile, info, data)


def thin_pair(count):
    matrix = np.zeros((count // 2 + 1, count))
    for i in range(count // 2 + 1):
        for source, weight in ((2 * i - 1, 0.5), (2 * i, 1.0), (2 * i + 1, 0.5)):
            if 0 <= source < count:
                matrix[i, source] = weight
    return matrix


def thin_cycle(length):
    matrix = np.zeros((length, length // 2))
    for i in range(length // 2):
        matrix[2 * i, i] += 1.0
        matrix[(2 * i - 1) % length, i] += 0.5
        matrix[(2 * i + 1) % length, i] += 0.5
    return matrix


def grow_matrix(count, source):
    matrix = np.zeros((count, source))
    for i in range(count):
        if i % 2 == 0:
            matrix[i, i // 2] = 1.0
        else:
            matrix[i, i // 2] = 0.5
            matrix[i, i // 2 + 1] = 0.5
    return matrix


def padded(matrix, rows, columns):
    out = np.zeros((rows, columns))
    out[: matrix.shape[0], : matrix.shape[1]] = matrix
    return out


def twice(matrix):
    return np.kron(np.eye(2), matrix)


def plain(matrix):
    return np.asarray(matrix, np.float32).astype(BF16)


def top_rows_matrix():
    rows_x = padded(thin_pair(17), 9, 17)
    rows_y = padded(thin_pair(13), 8, 16)
    rows_y[7] = 0.0
    matrix = np.zeros((2 * TOP_ROWS, 17 * 16))
    for i in range(9):
        for j in range(8):
            line = (j // 2) * 8 + i if i < 8 else 32 + j // 2
            matrix[(j % 2) * TOP_ROWS + line] = np.kron(rows_x[i], rows_y[j])
    return matrix


def exact_left(matrix, value):
    matrix = matrix[...]
    top, rest = halves(value)
    return mm(matrix, top) + mm(matrix, rest)


def exact_right(value, matrix):
    matrix = matrix[...]
    top, rest = halves(value)
    return mm(top, matrix) + mm(rest, matrix)


def collect_kernel(in_ref, *refs):
    tables = refs[:4]
    outs = refs[-18:-13]
    data_s, ids_s, slab_s = refs[-13:-10]
    thin_z_ref, thin_y_ref, top_rows_ref, top_z_ref = refs[-10:-6]
    fine_ref, mid_ref, low_ref, high_ref, top_ref, sems = refs[-6:]
    table_copies = started(list(zip(tables, refs[-10:-6])), sems)
    for c in range(DEVICES // 4):
        total = None
        for j in range(4):
            base = (c * 4 + j) * ROWS
            top, rest = halves(in_ref[base : base + CAP, :])
            start = (c * 4 + j) * CAP
            data_s[start : start + CAP, :128] = top
            data_s[start : start + CAP, 128:] = rest
            line = in_ref[base + CAP : base + CAP + 1, :]
            total = line if total is None else total + line
        ids_s[c : c + 1, :] = total.astype(jnp.int32)
    rows = lax.broadcasted_iota(jnp.int32, (256, 128), 0).astype(F32).astype(BF16)
    one, zero = jnp.ones((256, 128), BF16), jnp.zeros((256, 128), BF16)

    def block(b, carry):
        first = pl.multiple_of(b * 512, 512)
        acc = [jnp.zeros((256, 256), F32)] * 2
        for k in range(16):
            for m in range(2):
                parts = []
                for q in range(2):
                    ids = ids_s[2 * k + q : 2 * k + q + 1, :] - (first + m * 256)
                    line = jnp.clip(ids, -1, 256).astype(F32)
                    line = jnp.broadcast_to(line, (16, 128)).astype(BF16)
                    parts.append(jnp.where(rows == jnp.concatenate([line] * 16, axis=0), one, zero))
                hit = jnp.concatenate(parts, axis=1)
                acc[m] = acc[m] + mm(hit, data_s[k * 256 : (k + 1) * 256, :])
        for m in range(2):
            value = acc[m][:, :128] + acc[m][:, 128:]
            fine_ref[pl.ds(pl.multiple_of(first + m * 256, 256), 256), :] = value
        return carry

    lax.fori_loop(0, 3, block, 0)
    out_copies = started([(fine_ref, outs[0])], sems, 4)
    for i in range(17):
        total = None
        for x, weight in ((2 * i, 1.0), (2 * i - 1, 0.5), (2 * i + 1, 0.5)):
            if 0 <= x < CX:
                term = jnp.concatenate(
                    [
                        fine_ref[h * CX * CY + x * CY : h * CX * CY + (x + 1) * CY, :]
                        for h in range(2)
                    ],
                    axis=1,
                )
                term = term if weight == 1.0 else weight * term
                total = term if total is None else total + term
        slab_s[i * CY : (i + 1) * CY, :] = total
    slab_s[17 * CY :, :] = jnp.zeros((7 * CY, NZ), F32)
    for copy in table_copies:
        copy.wait()
    for g in range(3):
        part = exact_right(slab_s[g * 192 : (g + 1) * 192, :], thin_z_ref)
        mid_ref[g * 128 : (g + 1) * 128, :] = exact_left(thin_y_ref, part)
    for h in range(2):
        for c in range(4):
            at = slice((h * 4 + c) * CX, (h * 4 + c + 1) * CX)
            low_ref[at, :] = fine_ref[pl.ds(h * CX * CY + c, CX, stride=CY), :]
            high_ref[at, :] = fine_ref[pl.ds(h * CX * CY + CY - 4 + c, CX, stride=CY), :]
    for j in range(5):
        at = slice(256 + j * 24, 256 + (j + 1) * 24)
        low_ref[at, :] = mid_ref[pl.ds(j, 24, stride=16), :]
        high_ref[at, :] = mid_ref[pl.ds(8 + j, 24, stride=16), :]
    out_copies += started([(mid_ref, outs[1]), (low_ref, outs[2]), (high_ref, outs[3])], sems, 5)
    stacked = exact_left(top_rows_ref, mid_ref[: 17 * 16, :])
    pair = jnp.concatenate([stacked[:TOP_ROWS], stacked[TOP_ROWS:]], axis=1)
    top_charge = exact_right(pair, top_z_ref)
    for s in range(SIZE_X):
        top_ref[s * TOP_ROWS : (s + 1) * TOP_ROWS, :] = top_charge
    out_copies += started([(top_ref, outs[4])], sems, 8)
    for copy in out_copies:
        copy.wait()


def collect(arrived, *after):
    tables = (
        plain(thin_cycle(NZ)),
        plain(np.kron(np.eye(8), padded(thin_pair(CY), 16, CY))),
        plain(top_rows_matrix()),
        plain(twice(thin_cycle(128))),
    )
    out = (
        array(2 * CX * CY, 128),
        array(24 * 16, 128),
        array(SEND, 128),
        array(SEND, 128),
        array(SIZE_X * TOP_ROWS, 128),
    )
    return call(
        collect_kernel,
        out,
        [VM] + [HB] * (4 + len(after)),
        [
            pltpu.VMEM((DEVICES * CAP, 256), BF16),
            pltpu.VMEM((DEVICES // 4, 128), jnp.int32),
            pltpu.VMEM((24 * CY, NZ), F32),
            *buffers(*tables),
            *buffers(*out),
            pltpu.SemaphoreType.DMA((9,)),
        ],
        outs=HB,
        limit=20,
    )(arrived, *tables, *after)


def merge_kernel(
    fine_hbm, mid_hbm, before_ref, behind_ref, fine_s, halo_ref, wide_hbm, low_hbm, high_hbm,
    mid_ref, wide_ref, low_ref, high_ref, sems,
):
    mid_copy, fine_copy = started([(mid_hbm, mid_ref), (fine_hbm, fine_s)], sems)
    for h in range(2):
        for c in range(4):
            at = slice((h * 4 + c) * CX, (h * 4 + c + 1) * CX)
            start = h * CX * 8 + c
            halo_ref[pl.ds(start, CX, stride=8), :] = behind_ref[at, :]
            halo_ref[pl.ds(start + 4, CX, stride=8), :] = before_ref[at, :]
    mid_copy.wait()
    for i in range(24):
        wide_ref[i * YD : i * YD + 16, :] = mid_ref[i * 16 : (i + 1) * 16, :]
        wide_ref[i * YD + 16 : (i + 1) * YD, :] = jnp.zeros((16, 128), F32)
    for j in range(5):
        at = slice(256 + j * 24, 256 + (j + 1) * 24)
        behind = behind_ref[at, :]
        if j == 0:
            behind = behind + wide_ref[pl.ds(12, 24, stride=YD), :]
        wide_ref[pl.ds(12 + j, 24, stride=YD), :] = behind
        before = before_ref[at, :]
        row = 28 + j if j < 4 else 0
        if j == 4:
            before = before + wide_ref[pl.ds(0, 24, stride=YD), :]
        wide_ref[pl.ds(row, 24, stride=YD), :] = before
    out_copies = started([(wide_ref, wide_hbm)], sems, 2)
    fine_copy.wait()
    for ref, first, mid_first in ((low_ref, 0, 0), (high_ref, CX - 4, 12)):
        for h in range(2):
            for x in range(4):
                at = h * 128 + x * YD
                source = (h * CX + first + x) * CY
                ref[at : at + CY, :] = fine_s[source : source + CY, :]
                source = (h * CX + first + x) * 8
                ref[at + CY : at + YD, :] = halo_ref[source : source + 8, :]
        for i in range(5):
            base = (mid_first + i) * YD
            at = 256 + i * 24
            ref[at : at + 16, :] = wide_ref[base : base + 16, :]
            ref[at + 16 : at + 24, :] = (
                wide_ref[base + 16 : base + 24, :] + wide_ref[base + 24 : base + 32, :]
            )
    out_copies += started([(low_ref, low_hbm), (high_ref, high_hbm)], sems, 3)
    for copy in out_copies:
        copy.wait()


def merge(fine, mid, before, behind):
    out = (
        array(2 * CX * CY, 128),
        array(2 * CX * 8, 128),
        array(24 * YD, 128),
        array(SEND, 128),
        array(SEND, 128),
    )
    return call(
        merge_kernel,
        out,
        [HB, HB, VM, VM],
        [
            pltpu.VMEM((24 * 16, 128), F32),
            *buffers(*out[2:]),
            pltpu.SemaphoreType.DMA((5,)),
        ],
        outs=(VM, VM, HB, HB, HB),
    )(fine, mid, before, behind)


def z_matrices(period, copies):
    half = period // 2
    z = np.arange(period)[:, None]
    f = np.arange(half)[None, :]
    angle = 2 * np.pi * ((z * f) % period) / period
    cosine, sine = np.cos(angle), -np.sin(angle)
    sine[:, 0] = (-1.0) ** np.arange(period)
    scale = np.full((half, 1), 2.0 / period)
    scale[0] = 1.0 / period
    forward = np.zeros((256, 256))
    inverse = np.zeros((256, 256))
    for c in range(copies):
        rows = slice(c * period, (c + 1) * period)
        real = slice(c * half, (c + 1) * half)
        imag = slice(128 + c * half, 128 + (c + 1) * half)
        forward[rows, real] = cosine
        forward[rows, imag] = sine
        inverse[real, rows] = scale * cosine.T
        inverse[imag, rows] = scale * sine.T
    return forward, inverse


def y_matrices():
    order = np.concatenate([np.arange(17), np.arange(31, 16, -1)])
    y = np.arange(YD)
    angle = 2 * np.pi * ((order[:, None] * y[None, :]) % YD) / YD
    cosine, sine = np.cos(angle), np.sin(angle)
    forward = np.block([[cosine, sine], [-sine, cosine]])
    inverse = np.block([[cosine.T, -sine.T], [sine.T, cosine.T]]) / YD
    return np.kron(np.eye(4), forward), np.kron(np.eye(4), inverse)


def stacked_rows(matrix):
    top, rest = np_halves(matrix)
    return np.concatenate([top, rest], axis=0)


def stacked_cols(matrix):
    top, rest = np_halves(matrix)
    return np.concatenate([top, rest], axis=1)


def right_product(value, matrix_ref):
    top, rest = halves(value)
    return (
        mm(top, matrix_ref[:256, :]) + mm(top, matrix_ref[256:, :]) + mm(rest, matrix_ref[:256, :])
    )


def left_product(matrix_ref, value):
    top, rest = halves(value)
    return (
        mm(matrix_ref[:, :256], top) + mm(matrix_ref[:, 256:], top) + mm(matrix_ref[:, :256], rest)
    )


def special_mask(copies, rows):
    lane = lax.broadcasted_iota(jnp.int32, (rows, 128), 1)
    row = lax.broadcasted_iota(jnp.int32, (rows, 128), 0)
    return (lane & (128 // copies - 1)) == 0, row


def forward_chunk(value, z_ref, y_ref, copies):
    z_freq = right_product(value, z_ref)
    stacks = []
    for h in range(2):
        pieces = []
        for q in range(4):
            slab = z_freq[(h * 4 + q) * YD : (h * 4 + q + 1) * YD]
            pieces += [slab[:, :128], slab[:, 128:]]
        stacks.append(jnp.concatenate(pieces, axis=0))
    freq = left_product(y_ref, jnp.concatenate(stacks, axis=1))
    lane_special, row = special_mask(copies, 16)
    special = lane_special & (row != 0)
    slabs = []
    for h in range(2):
        for q in range(4):
            slab = freq[q * 64 : (q + 1) * 64, h * 128 : (h + 1) * 128]
            ar, br, ai, bi = slab[:16], slab[16:32], slab[32:48], slab[48:]
            slabs.append(
                jnp.concatenate(
                    [
                        jnp.where(special, 0.5 * (ar + br), ar),
                        jnp.where(special, 0.5 * (ai + bi), br),
                        jnp.where(special, 0.5 * (ai - bi), ai),
                        jnp.where(special, 0.5 * (br - ar), bi),
                    ],
                    axis=0,
                )
            )
    return slabs


def inverse_chunk(slabs, z_ref, y_ref):
    stacks = [jnp.concatenate(slabs[h * 4 : h * 4 + 4], axis=0) for h in range(2)]
    space = left_product(y_ref, jnp.concatenate(stacks, axis=1))
    rows = []
    for h in range(2):
        for q in range(4):
            slab = space[q * 64 : (q + 1) * 64, h * 128 : (h + 1) * 128]
            rows.append(jnp.concatenate([slab[:YD], slab[YD:]], axis=1))
    return right_product(jnp.concatenate(rows, axis=0), z_ref)


def taps_kernel(copies, in_ref, z_ref, y_ref, after_ref, out_ref):
    for p in range(2):
        slabs = forward_chunk(in_ref[p * 256 : (p + 1) * 256, :], z_ref, y_ref, copies)
        for j in range(8):
            dx = p * 8 + j
            if dx > 8:
                break
            real, imag = slabs[j][:YD], slabs[j][YD:]
            values = (real, imag, real + imag)
            for part in range(3):
                at = (part * 9 + dx) * YD
                out_ref[at : at + YD, :] = values[part]


def taps(kernel, copies, z_matrix, y_matrix, after):
    flipped = kernel[:, ::-1, ::-1]
    tall = jnp.concatenate(
        [flipped[:, 4:], jnp.zeros((9, YD - 9, 9), F32), flipped[:, :4]], axis=1
    )
    period = 256 // copies
    wide = jnp.concatenate(
        [tall[:, :, 4:], jnp.zeros((9, YD, period - 9), F32), tall[:, :, :4]], axis=2
    )
    wide = jnp.concatenate([wide] * copies, axis=2)
    wide = jnp.concatenate([wide, jnp.zeros((7, YD, 256), F32)], axis=0)
    return call(
        functools.partial(taps_kernel, copies), array(27 * YD, 128), [VM] * 3 + [HB]
    )(wide.reshape(16 * YD, 256), z_matrix, y_matrix, after)


def own_kernel(fine_s, halo_s, z_ref, y_ref, out_ref):
    for p in range(CX // 8):
        columns = []
        for h in range(2):
            rows = []
            for j in range(8):
                n = h * CX + p * 8 + j
                rows += [fine_s[n * CY : (n + 1) * CY, :], halo_s[n * 8 : (n + 1) * 8, :]]
            columns.append(jnp.concatenate(rows, axis=0))
        slabs = forward_chunk(jnp.concatenate(columns, axis=1), z_ref, y_ref, 1)
        for j in range(8):
            out_ref[(p * 8 + j) * 64 : (p * 8 + j + 1) * 64, :] = slabs[j]


def convolve(copies, first, count, taps_ref, freq_s, conv_s):
    lane_special, row = special_mask(copies, 8)
    whole = lane_special & (row == 0)
    for v in range(2):
        sums = [[None] * 6 for _ in range(count)]
        for dx in range(9):
            coefs = []
            for half in range(2):
                at = dx * YD + half * 16 + v * 8
                coefs.append([taps_ref[at + part * 288 : at + part * 288 + 8, :] for part in range(3)])
            for j in range(count):
                for half in range(2):
                    at = (first + j + dx) * 96 + v * 8 + half * 16
                    for part in range(3):
                        term = coefs[half][part] * freq_s[at + part * 32 : at + part * 32 + 8, :]
                        n = 3 * half + part
                        sums[j][n] = term if dx == 0 else sums[j][n] + term
        for j in range(count):
            values = []
            for half in range(2):
                re, im, both = sums[j][3 * half : 3 * half + 3]
                real, imag = re - im, both - re - im
                if v == 0:
                    real, imag = jnp.where(whole, re, real), jnp.where(whole, im, imag)
                values += [real, imag]
            ar, ai, br, bi = values
            special = lane_special & (row != 0) if v == 0 else lane_special
            at = (first + j) * 64 + v * 8
            conv_s[at : at + 8, :] = jnp.where(special, ar - bi, ar)
            conv_s[at + 16 : at + 24, :] = jnp.where(special, ar + bi, br)
            conv_s[at + 32 : at + 40, :] = jnp.where(special, ai + br, ai)
            conv_s[at + 48 : at + 56, :] = jnp.where(special, br - ai, bi)


def with_sum(slab):
    return jnp.concatenate([slab, slab[:YD] + slab[YD:]], axis=0)


def wide_slab(ref, index):
    at = 256 + index * 24
    last = ref[at + 16 : at + 24, :]
    row = lax.broadcasted_iota(jnp.int32, (8, 128), 0)
    return jnp.concatenate(
        [ref[at : at + 16, :], jnp.where(row < 4, last, 0.0), jnp.where(row < 4, 0.0, last)], axis=0
    )


def levels_kernel(
    own_ref, before_ref, behind_ref, *refs
):
    zf_ref, yf_ref = refs[:2]
    near_ref, mid_ref, grow_ref, freq_s, conv_s, mid_freq_s, mid_conv_s = refs[10:17]
    wide_ref, mzf_ref, near_taps, mid_taps, zi_ref, yi_ref, mzi_ref, sems = refs[17:]
    copies = started(list(zip(refs[2:10], (*refs[17:24], grow_ref))), sems)
    for x in range(CX):
        freq_s[(x + 4) * 96 : (x + 5) * 96, :] = with_sum(own_ref[x * 64 : (x + 1) * 64, :])
    edges = [
        jnp.concatenate([ref[:128, :], ref[128:256, :]], axis=1) for ref in (before_ref, behind_ref)
    ]
    slabs = forward_chunk(jnp.concatenate(edges, axis=0), zf_ref, yf_ref, 1)
    for j in range(8):
        at = j if j < 4 else 32 + j
        freq_s[at * 96 : (at + 1) * 96, :] = with_sum(slabs[j])
    zero = jnp.zeros((YD, 128), F32)
    copies[0].wait()
    copies[1].wait()
    for p in range(3):
        pairs = []
        for j in range(8):
            pair = []
            for n in (p * 8 + j, p * 8 + j + 9):
                if n > 24 or (n == p * 8 + j and n > 16):
                    slab = zero
                elif n < 4:
                    slab = wide_slab(before_ref, n)
                elif n > 20:
                    slab = wide_slab(behind_ref, n - 20)
                else:
                    slab = wide_ref[(n - 4) * YD : (n - 3) * YD, :]
                    if n == 4:
                        slab = slab + wide_slab(before_ref, 4)
                    if n == 20:
                        slab = slab + wide_slab(behind_ref, 0)
                pair.append(slab)
            pairs.append(jnp.concatenate(pair, axis=1))
        slabs = forward_chunk(jnp.concatenate(pairs, axis=0), mzf_ref, yf_ref, 2)
        for j in range(8):
            at = p * 8 + j
            mid_freq_s[at * 96 : (at + 1) * 96, :] = with_sum(slabs[j])
    for copy in copies[2:]:
        copy.wait()
    for p in range(4):
        convolve(1, p * 8, 8, near_taps, freq_s, conv_s)
        slabs = [conv_s[(p * 8 + j) * 64 : (p * 8 + j + 1) * 64, :] for j in range(8)]
        space = inverse_chunk(slabs, zi_ref, yi_ref)
        for j in range(8):
            x = p * 8 + j
            near_ref[x * CY : (x + 1) * CY, :] = space[j * YD : j * YD + CY]
    mid_conv_s[9 * 64 :, :] = jnp.zeros((7 * 64, 128), F32)
    for first, count in ((0, 5), (5, 4)):
        convolve(2, first, count, mid_taps, mid_freq_s, mid_conv_s)
    for p in range(2):
        slabs = [mid_conv_s[(p * 8 + j) * 64 : (p * 8 + j + 1) * 64, :] for j in range(8)]
        space = inverse_chunk(slabs, mzi_ref, yi_ref)
        for j in range(8):
            i = p * 8 + j
            if i < 9:
                mid_ref[i * 16 : (i + 1) * 16, :] = space[j * YD : j * YD + 16]


def gauss(index, period, width):
    distance = jnp.minimum(index, period - index).astype(F32)
    return jnp.exp(-(distance * distance) / (width * width))


def gauss_kernel(weights_ref, widths_ref, info_ref, after_ref, x_ref, y_ref, z_ref):
    first_x = info_ref[2] * 8
    first_y = info_ref[3] * 6
    row = lax.broadcasted_iota(jnp.int32, (16, 256), 0)
    column = lax.broadcasted_iota(jnp.int32, (16, 256), 1)
    source = jnp.where(column < 128, column, (column - 128) * 8 + 8)
    offset = (first_x + row - source) & 127
    for k in range(4):
        value = jnp.where(column < 144, gauss(offset, 128, widths_ref[k]), 0.0)
        for n, part in enumerate(halves(value)):
            x_ref[n * 64 + k * 16 : n * 64 + (k + 1) * 16, :] = part
    row = lax.broadcasted_iota(jnp.int32, (128, 128), 0)
    column = lax.broadcasted_iota(jnp.int32, (128, 128), 1)
    for k in range(4):
        value = gauss((row - column) & 63, 64, widths_ref[k]) * weights_ref[k]
        value = jnp.where((row >> 6) == (column >> 6), value, 0.0)
        for n, part in enumerate(halves(value)):
            z_ref[(n * 4 + k) * 128 : (n * 4 + k + 1) * 128, :] = part
    row = lax.broadcasted_iota(jnp.int32, (64, 128), 0)
    column = lax.broadcasted_iota(jnp.int32, (64, 128), 1)
    target = (row >> 3) * 6 + (row & 7)
    source = first_y + (column & 3) * 2 + ((column >> 4) & 1)
    offset = target - source
    offset = jnp.where(offset < 0, offset + 48, offset)
    offset = jnp.where(offset >= 48, offset - 48, offset)
    chosen = (column >> 2) & 3
    value = jnp.zeros((64, 128), F32)
    for k in range(4):
        value = jnp.where(chosen == k, gauss(offset, 48, widths_ref[k]), value)
    for n, part in enumerate(halves(jnp.where(column < 32, value, 0.0))):
        y_ref[n * 64 : (n + 1) * 64, :] = part


def top_kernel(in_ref, x_ref, y_ref, z_ref, out_ref, plane_s, depth_s):
    left = (x_ref[:64, :], x_ref[64:, :])
    for jp in range(4):
        tiles = [in_ref[s * TOP_ROWS + jp * 8 : s * TOP_ROWS + jp * 8 + 8, :] for s in range(16)]
        tiles.append(in_ref[pl.ds(32 + jp, SIZE_X, stride=TOP_ROWS), :])
        tiles.append(jnp.zeros((112, 128), F32))
        right = halves(jnp.concatenate(tiles, axis=0))
        plane = mm(left[0], right[0]) + mm(left[0], right[1]) + mm(left[1], right[0])
        for k in range(4):
            plane_s[(k * 4 + jp) * 16 : (k * 4 + jp + 1) * 16, :] = plane[k * 16 : (k + 1) * 16]
    for k in range(4):
        weight = [z_ref[(n * 4 + k) * 128 : (n * 4 + k + 1) * 128, :] for n in range(2)]
        value = halves(plane_s[k * 64 : (k + 1) * 64, :])
        depth_s[k * 64 : (k + 1) * 64, :] = (
            mm(value[0], weight[0]) + mm(value[0], weight[1]) + mm(value[1], weight[0])
        )
    lane = lax.broadcasted_iota(jnp.int32, (16, 128), 1)
    tiles = []
    for ip in range(5):
        first = depth_s[pl.ds(2 * ip, 16, stride=16), :]
        second = depth_s[pl.ds(2 * ip + 1, 16, stride=16), :]
        even = jnp.where(lane < 64, first, pltpu.roll(second, 64, 1))
        odd = jnp.where(lane < 64, pltpu.roll(first, 64, 1), second)
        tiles.append(jnp.concatenate([even, odd, jnp.zeros((96, 128), F32)], axis=0))
    right = halves(jnp.concatenate(tiles, axis=1))
    left = (y_ref[:64, :], y_ref[64:, :])
    out_ref[...] = mm(left[0], right[0]) + mm(left[0], right[1]) + mm(left[1], right[0])


def finish_kernel(
    near_ref, mid_ref, top_ref, *refs
):
    grow_ref, out_ref, grown_s = refs
    grow_top, grow_z = grow_ref[:128, :], grow_ref[128:256, :]
    grow_fine, grow_y = grow_ref[256:, :128], grow_ref[256:272, 128:]
    total = top_ref[:8, :]
    for s in range(1, SIZE_Y):
        total = total + top_ref[s * 8 : (s + 1) * 8, :]
    lanes = []
    for ip in range(5):
        lanes.append(exact_right(total[:, ip * 128 : (ip + 1) * 128], grow_top))
    deep = jnp.concatenate(lanes, axis=1)
    tiles = []
    for i in range(17):
        tile = deep[:, (i // 2) * 128 : (i // 2 + 1) * 128]
        if i % 2:
            tile = 0.5 * (tile + deep[:, (i // 2 + 1) * 128 : (i // 2 + 2) * 128])
        tiles.append(tile)
    flat = jnp.concatenate(tiles, axis=1)
    flat = jnp.concatenate([flat, jnp.zeros((120, 17 * 128), F32)], axis=0)
    tall = exact_left(grow_y, flat)
    slabs = []
    for i in range(24):
        if i > 16:
            slabs.append(jnp.zeros((16, 128), F32))
            continue
        h = i // 9
        slabs.append(
            tall[:, i * 128 : (i + 1) * 128]
            + mid_ref[(i - 9 * h) * 16 : (i - 9 * h + 1) * 16, h * 128 : (h + 1) * 128]
        )
    for g in range(3):
        part = exact_right(jnp.concatenate(slabs[g * 8 : (g + 1) * 8], axis=0), grow_z)
        grown_s[g * 192 : (g + 1) * 192, :] = exact_left(grow_fine, part)
    for x in range(CX):
        at = slice(x * CY, (x + 1) * CY)
        i = x // 2
        value = grown_s[i * CY : (i + 1) * CY, :]
        if x % 2:
            value = 0.5 * (value + grown_s[(i + 1) * CY : (i + 2) * CY, :])
        out_ref[at, :] = near_ref[at, :] + value


def swap(to_low, to_high, axis):
    count = lax.axis_size(axis)
    forward = [(i, (i + 1) % count) for i in range(count)]
    backward = [(target, source) for source, target in forward]
    before = lax.ppermute(to_high, axis, forward)
    behind = lax.ppermute(to_low, axis, backward)
    return before, behind


def on_device(
    charge_blocks, block_tile, block_count, near_kernel, mid_kernel, top_weights, top_widths
):
    at_x = lax.axis_index("gx")
    at_y = lax.axis_index("gy")
    info = jnp.stack(
        [block_count[0], ((at_x * SIZE_Y + at_y) % 4) * CAP, at_x, at_y]
    ).astype(jnp.int32)
    outgoing = send(block_tile.reshape(32, 128), info, charge_blocks)
    arrived = lax.all_to_all(
        outgoing.reshape(DEVICES, 1, ROWS * 128),
        ("gx", "gy"),
        split_axis=0,
        concat_axis=0,
        tiled=True,
    ).reshape(DEVICES * ROWS, 128)

    z_fine, z_fine_back = z_matrices(256, 1)
    z_mid, z_mid_back = z_matrices(128, 2)
    y_forward, y_back = y_matrices()
    zf, yf = stacked_rows(z_fine), stacked_cols(y_forward)
    zi, yi = stacked_rows(z_fine_back), stacked_cols(y_back)
    mzf, mzi = stacked_rows(z_mid), stacked_rows(z_mid_back)
    near_taps = taps(near_kernel, 1, zf, yf, outgoing)
    mid_taps = taps(mid_kernel, 2, mzf, yf, outgoing)

    bells = call(
        gauss_kernel,
        tuple(jax.ShapeDtypeStruct(n, BF16) for n in ((128, 256), (128, 128), (1024, 128))),
        [SM, SM, SM, HB],
    )(top_weights, top_widths, info, outgoing)

    fine, mid, low, high, top = collect(arrived, near_taps, mid_taps, bells[0])
    before, behind = swap(low, high, "gy")
    tops = lax.all_to_all(
        top.reshape(SIZE_X, TOP_ROWS, 128), "gx", split_axis=0, concat_axis=0, tiled=True
    )
    tops = tops.reshape(SIZE_X * TOP_ROWS, 128)
    partial = call(
        top_kernel,
        array(64, 640),
        [VM] * 4,
        [pltpu.VMEM((256, 128), F32), pltpu.VMEM((256, 128), F32)],
    )(tops, *bells)
    partial = lax.all_to_all(
        partial.reshape(SIZE_Y, 8, 640), "gy", split_axis=0, concat_axis=0, tiled=True
    ).reshape(64, 640)
    fine, halo, wide, low, high = merge(fine, mid, before, behind)
    before, behind = swap(low, high, "gx")
    own = call(own_kernel, array(CX * 64, 128), [VM] * 4)(fine, halo, zf, yf)
    grow_z = grow_matrix(2 * 64, 65)
    grow_z[:, 0] += grow_z[:, 64]
    grow_fine_z = grow_matrix(2 * 128, 129)
    grow_fine_z[:, 0] += grow_fine_z[:, 128]
    grow_y = np.zeros((192, 256))
    grow_y[:, :128] = np.kron(np.eye(8), padded(grow_matrix(CY, 13), CY, 16))
    grow_y[:16, 128:135] = padded(grow_matrix(13, 7), 16, 7)
    grow = plain(np.concatenate([twice(grow_z[:, :64].T), grow_fine_z[:, :128].T, grow_y]))
    tables = (wide, mzf, near_taps, mid_taps, zi, yi, mzi)
    near, mid_near, grow = call(
        levels_kernel,
        (array(CX * CY, NZ), array(9 * 16, 256), jax.ShapeDtypeStruct(grow.shape, BF16)),
        [VM] * 5 + [HB] * 8,
        [
            pltpu.VMEM((40 * 96, 128), F32),
            pltpu.VMEM((32 * 64, 128), F32),
            pltpu.VMEM((24 * 96, 128), F32),
            pltpu.VMEM((16 * 64, 128), F32),
            *buffers(*tables),
            pltpu.SemaphoreType.DMA((8,)),
        ],
        limit=14,
    )(own, before, behind, zf, yf, *tables, grow)
    out = call(
        finish_kernel, array(CX * CY, NZ), [VM] * 4, [pltpu.VMEM((24 * CY, NZ), F32)]
    )(near, mid_near, partial, grow)
    return out.reshape(CX, CY, NZ)


def solution(mesh):
    placed = (P(("gx", "gy"), None), P(("gx", "gy")), P(("gx", "gy")), P(), P(), P(), P())
    return jax.shard_map(
        on_device, mesh=mesh, in_specs=placed, out_specs=P("gx", "gy", None), check_vma=False
    )
```

```python
import functools

import jax
import jax.numpy as jnp
import numpy as np
from jax import lax
from jax.experimental import pallas as pl
from jax.experimental.pallas import tpu as pltpu
from jax.sharding import PartitionSpec as P


CX = 32
CY = 24
NZ = 256
CAP = 32
DEVICES = 128
ROWS = CAP + 1
SIZE_X = 16
SIZE_Y = 8
DEAD = 2047
SEND = 376
TOP_ROWS = 40
YD = 32
F32 = jnp.float32
BF16 = jnp.bfloat16
VM = pl.BlockSpec(memory_space=pltpu.VMEM)
SM = pl.BlockSpec(memory_space=pltpu.SMEM)
HB = pl.BlockSpec(memory_space=pltpu.HBM)


def call(body, out, ins, scratch=(), limit=10, flops=0, moved=0, outs=VM):
    many = isinstance(out, tuple)
    outs = outs if isinstance(outs, tuple) else (outs,) * (len(out) if many else 1)
    shapes = tuple(
        pltpu.HBM(shape.shape, shape.dtype) if spec is HB else shape
        for shape, spec in zip(out if many else (out,), outs)
    )
    kernel = pl.pallas_call(
        body,
        out_shape=shapes if many else shapes[0],
        in_specs=ins,
        out_specs=outs if many else outs[0],
        scratch_shapes=list(scratch),
        compiler_params=pltpu.CompilerParams(vmem_limit_bytes=limit << 20),
        cost_estimate=pl.CostEstimate(flops=flops, bytes_accessed=moved, transcendentals=0),
    )

    def run(*args):
        placed = [
            pltpu.with_memory_space_constraint(jnp.asarray(arg), pltpu.HBM) if spec is HB else arg
            for arg, spec in zip(args, ins)
        ]
        return kernel(*placed)

    return run


def started(pairs, sems, first=0):
    copies = []
    for n, (source, target) in enumerate(pairs):
        copy = pltpu.make_async_copy(source, target, sems.at[first + n])
        copy.start()
        copies.append(copy)
    return copies


def buffers(*tables):
    return [pltpu.VMEM(table.shape, table.dtype) for table in tables]


def array(*shape):
    return jax.ShapeDtypeStruct(shape, F32)


def mm(a, b):
    return jnp.dot(a, b, preferred_element_type=F32)


def halves(value):
    top = value.astype(BF16)
    return top, (value - top.astype(F32)).astype(BF16)


def np_halves(matrix):
    matrix = np.asarray(matrix, np.float32)
    top = matrix.astype(BF16)
    return top, (matrix - top.astype(np.float32)).astype(BF16)


def send_kernel(
    tile_ref, info_ref, data_ref, out_ref,
    data_s, out_s, hit_s, count_s, place_s, source_s, source_smem, sems,
):
    (data_copy,) = started([(data_ref, data_s)], sems)
    tile = tile_ref[...]
    column = tile >> 1
    high_part = column >> 6
    grid_x = (high_part * 43691) >> 17
    grid_y = column - grid_x * (CY * SIZE_Y)
    owner_y = ((grid_y >> 3) * 43) >> 7
    owner = (grid_x >> 5) * SIZE_Y + owner_y
    cell = (tile & 1) * (CX * CY) + (grid_x & (CX - 1)) * CY + (grid_y - owner_y * CY)
    slot = lax.broadcasted_iota(jnp.int32, tile.shape, 0) * 128 + lax.broadcasted_iota(
        jnp.int32, tile.shape, 1
    )
    code = jnp.where(slot < info_ref[0], cell, DEAD)
    rows = lax.broadcasted_iota(jnp.int32, (128, 128), 0)
    before = lax.broadcasted_iota(jnp.int32, (128, 256), 0)
    after = lax.broadcasted_iota(jnp.int32, (128, 256), 1)
    prefix = jnp.where((before < after) | (after >= 128), 1.0, 0.0).astype(BF16)
    for c in range(32):
        hit = jnp.where(rows == owner[c : c + 1], 1.0, 0.0)
        hit_s[:, c * 128 : (c + 1) * 128] = hit.astype(BF16)
    for g in range(8):
        chunks = [hit_s[:, c * 128 : (c + 1) * 128] for c in range(g * 4, g * 4 + 4)]
        count_s[g * 512 : (g + 1) * 512, :] = mm(jnp.concatenate(chunks, axis=0), prefix)
    base = jnp.zeros((128, 128), F32)
    lane = lax.broadcasted_iota(jnp.int32, (1, 128), 1)
    for c in range(32):
        counted = count_s[c * 128 : (c + 1) * 128, :128] + base
        base = base + count_s[c * 128 : (c + 1) * 128, 128:]
        hit = rows == owner[c : c + 1]
        rank = jnp.sum(jnp.where(hit, counted, 0.0), axis=0, keepdims=True)
        place = rows[:CAP] == rank.astype(jnp.int32)
        ids = code[c : c + 1]
        values = (ids >> 4, ids & 15, c * 2 + (lane >> 6), lane & 63)
        both = [jnp.where(place, value.astype(F32), 0.0) for value in values]
        place_s[:, c * 128 : (c + 1) * 128] = jnp.concatenate(both, axis=0).astype(BF16)
    found = lax.dot_general(
        hit_s[...], place_s[...], (((1,), (1,)), ((), ())), preferred_element_type=F32
    )
    source = found * 64.0 + pltpu.roll(found, 128 - CAP, 1)
    source_s[...] = pltpu.roll(source, 64, 1).astype(jnp.int32)
    quarters = [pl.ds(part * 32, 32) for part in range(4)]
    source_copies = started([(source_s.at[at], source_smem.at[at]) for at in quarters], sems, 5)
    lane = lax.broadcasted_iota(jnp.int32, (128, 128), 1)
    ids = jnp.where(lane < CAP, found * 16.0 + pltpu.roll(found, 128 - CAP, 1), 0.0)
    ids = pltpu.roll(ids, info_ref[1], 1)
    for d in range(DEVICES):
        at = d * ROWS + CAP
        out_s[at : at + 1, :] = ids[d : d + 1]
    data_copy.wait()
    copies = []
    for part in range(4):
        source_copies[part].wait()

        def body(n, carry):
            for q in range(4):
                d = part * 32 + n * 4 + q
                for r in range(CAP):
                    out_s[pl.ds(d * ROWS + r, 1), :] = data_s[pl.ds(source_smem[d, r], 1), :]
            return carry

        lax.fori_loop(0, 8, body, 0)
        at = pl.ds(part * 32 * ROWS, 32 * ROWS)
        copies += started([(out_s.at[at], out_ref.at[at])], sems, 1 + part)
    for copy in copies:
        copy.wait()


def send(tile, info, data):
    return call(
        send_kernel,
        array(DEVICES * ROWS, 128),
        [VM, SM, HB],
        [
            pltpu.VMEM((4096, 128), F32),
            pltpu.VMEM((DEVICES * ROWS, 128), F32),
            pltpu.VMEM((128, 4096), BF16),
            pltpu.VMEM((4096, 256), F32),
            pltpu.VMEM((128, 4096), BF16),
            pltpu.VMEM((128, 128), jnp.int32),
            pltpu.SMEM((128, 128), jnp.int32),
            pltpu.SemaphoreType.DMA((9,)),
        ],
        outs=HB,
        limit=20,
    )(tile, info, data)


def thin_pair(count):
    matrix = np.zeros((count // 2 + 1, count))
    for i in range(count // 2 + 1):
        for source, weight in ((2 * i - 1, 0.5), (2 * i, 1.0), (2 * i + 1, 0.5)):
            if 0 <= source < count:
                matrix[i, source] = weight
    return matrix


def thin_cycle(length):
    matrix = np.zeros((length, length // 2))
    for i in range(length // 2):
        matrix[2 * i, i] += 1.0
        matrix[(2 * i - 1) % length, i] += 0.5
        matrix[(2 * i + 1) % length, i] += 0.5
    return matrix


def grow_matrix(count, source):
    matrix = np.zeros((count, source))
    for i in range(count):
        if i % 2 == 0:
            matrix[i, i // 2] = 1.0
        else:
            matrix[i, i // 2] = 0.5
            matrix[i, i // 2 + 1] = 0.5
    return matrix


def padded(matrix, rows, columns):
    out = np.zeros((rows, columns))
    out[: matrix.shape[0], : matrix.shape[1]] = matrix
    return out


def twice(matrix):
    return np.kron(np.eye(2), matrix)


def plain(matrix):
    return np.asarray(matrix, np.float32).astype(BF16)


def top_rows_matrix():
    rows_x = padded(thin_pair(17), 9, 17)
    rows_y = padded(thin_pair(13), 8, 16)
    rows_y[7] = 0.0
    matrix = np.zeros((2 * TOP_ROWS, 17 * 16))
    for i in range(9):
        for j in range(8):
            line = (j // 2) * 8 + i if i < 8 else 32 + j // 2
            matrix[(j % 2) * TOP_ROWS + line] = np.kron(rows_x[i], rows_y[j])
    return matrix


def exact_left(matrix, value):
    matrix = matrix[...]
    top, rest = halves(value)
    return mm(matrix, top) + mm(matrix, rest)


def exact_right(value, matrix):
    matrix = matrix[...]
    top, rest = halves(value)
    return mm(top, matrix) + mm(rest, matrix)


def collect_kernel(in_ref, *refs):
    tables = refs[:4]
    outs = refs[-18:-13]
    data_s, ids_s, slab_s = refs[-13:-10]
    thin_z_ref, thin_y_ref, top_rows_ref, top_z_ref = refs[-10:-6]
    fine_ref, mid_ref, low_ref, high_ref, top_ref, sems = refs[-6:]
    table_copies = started(list(zip(tables, refs[-10:-6])), sems)

    def unpack(c):
        total = None
        for j in range(4):
            base = (c * 4 + j) * ROWS
            top, rest = halves(in_ref[base : base + CAP, :])
            start = (c * 4 + j) * CAP
            data_s[start : start + CAP, :128] = top
            data_s[start : start + CAP, 128:] = rest
            line = in_ref[base + CAP : base + CAP + 1, :]
            total = line if total is None else total + line
        ids_s[c : c + 1, :] = total.astype(jnp.int32)

    rows = lax.broadcasted_iota(jnp.int32, (256, 128), 0).astype(F32).astype(BF16)
    one, zero = jnp.ones((256, 128), BF16), jnp.zeros((256, 128), BF16)

    def block(b, carry):
        first = b * 512 if isinstance(b, int) else pl.multiple_of(b * 512, 512)
        acc = [jnp.zeros((256, 256), F32)] * 2
        for k in range(16):
            if isinstance(b, int):
                unpack(2 * k)
                unpack(2 * k + 1)
            for m in range(2):
                parts = []
                for q in range(2):
                    ids = ids_s[2 * k + q : 2 * k + q + 1, :] - (first + m * 256)
                    line = jnp.clip(ids, -1, 256).astype(F32)
                    line = jnp.broadcast_to(line, (16, 128)).astype(BF16)
                    parts.append(jnp.where(rows == jnp.concatenate([line] * 16, axis=0), one, zero))
                hit = jnp.concatenate(parts, axis=1)
                acc[m] = acc[m] + mm(hit, data_s[k * 256 : (k + 1) * 256, :])
        for m in range(2):
            value = acc[m][:, :128] + acc[m][:, 128:]
            at = first + m * 256
            fine_ref[pl.ds(at if isinstance(b, int) else pl.multiple_of(at, 256), 256), :] = value
        return carry

    block(0, 0)
    lax.fori_loop(1, 3, block, 0)
    out_copies = started([(fine_ref, outs[0])], sems, 4)
    for i in range(17):
        total = None
        for x, weight in ((2 * i, 1.0), (2 * i - 1, 0.5), (2 * i + 1, 0.5)):
            if 0 <= x < CX:
                term = jnp.concatenate(
                    [
                        fine_ref[h * CX * CY + x * CY : h * CX * CY + (x + 1) * CY, :]
                        for h in range(2)
                    ],
                    axis=1,
                )
                term = term if weight == 1.0 else weight * term
                total = term if total is None else total + term
        slab_s[i * CY : (i + 1) * CY, :] = total
    slab_s[17 * CY :, :] = jnp.zeros((7 * CY, NZ), F32)
    for copy in table_copies:
        copy.wait()
    for g in range(3):
        part = exact_right(slab_s[g * 192 : (g + 1) * 192, :], thin_z_ref)
        mid_ref[g * 128 : (g + 1) * 128, :] = exact_left(thin_y_ref, part)
    for h in range(2):
        for c in range(4):
            at = slice((h * 4 + c) * CX, (h * 4 + c + 1) * CX)
            low_ref[at, :] = fine_ref[pl.ds(h * CX * CY + c, CX, stride=CY), :]
            high_ref[at, :] = fine_ref[pl.ds(h * CX * CY + CY - 4 + c, CX, stride=CY), :]
    for j in range(5):
        at = slice(256 + j * 24, 256 + (j + 1) * 24)
        low_ref[at, :] = mid_ref[pl.ds(j, 24, stride=16), :]
        high_ref[at, :] = mid_ref[pl.ds(8 + j, 24, stride=16), :]
    out_copies += started([(mid_ref, outs[1]), (low_ref, outs[2]), (high_ref, outs[3])], sems, 5)
    stacked = exact_left(top_rows_ref, mid_ref[: 17 * 16, :])
    pair = jnp.concatenate([stacked[:TOP_ROWS], stacked[TOP_ROWS:]], axis=1)
    top_charge = exact_right(pair, top_z_ref)
    for s in range(SIZE_X):
        top_ref[s * TOP_ROWS : (s + 1) * TOP_ROWS, :] = top_charge
    out_copies += started([(top_ref, outs[4])], sems, 8)
    for copy in out_copies:
        copy.wait()


def collect(arrived, *after):
    tables = (
        plain(thin_cycle(NZ)),
        plain(np.kron(np.eye(8), padded(thin_pair(CY), 16, CY))),
        plain(top_rows_matrix()),
        plain(twice(thin_cycle(128))),
    )
    out = (
        array(2 * CX * CY, 128),
        array(24 * 16, 128),
        array(SEND, 128),
        array(SEND, 128),
        array(SIZE_X * TOP_ROWS, 128),
    )
    return call(
        collect_kernel,
        out,
        [VM] + [HB] * (4 + len(after)),
        [
            pltpu.VMEM((DEVICES * CAP, 256), BF16),
            pltpu.VMEM((DEVICES // 4, 128), jnp.int32),
            pltpu.VMEM((24 * CY, NZ), F32),
            *buffers(*tables),
            *buffers(*out),
            pltpu.SemaphoreType.DMA((9,)),
        ],
        outs=HB,
        limit=20,
    )(arrived, *tables, *after)


def merge_kernel(
    fine_hbm, mid_hbm, before_ref, behind_ref, fine_s, halo_ref, wide_hbm, low_hbm, high_hbm,
    mid_ref, wide_ref, low_ref, high_ref, sems,
):
    mid_copy, fine_copy = started([(mid_hbm, mid_ref), (fine_hbm, fine_s)], sems)
    for h in range(2):
        for c in range(4):
            at = slice((h * 4 + c) * CX, (h * 4 + c + 1) * CX)
            start = h * CX * 8 + c
            halo_ref[pl.ds(start, CX, stride=8), :] = behind_ref[at, :]
            halo_ref[pl.ds(start + 4, CX, stride=8), :] = before_ref[at, :]
    mid_copy.wait()
    for i in range(24):
        wide_ref[i * YD : i * YD + 16, :] = mid_ref[i * 16 : (i + 1) * 16, :]
        wide_ref[i * YD + 16 : (i + 1) * YD, :] = jnp.zeros((16, 128), F32)
    for j in range(5):
        at = slice(256 + j * 24, 256 + (j + 1) * 24)
        behind = behind_ref[at, :]
        if j == 0:
            behind = behind + wide_ref[pl.ds(12, 24, stride=YD), :]
        wide_ref[pl.ds(12 + j, 24, stride=YD), :] = behind
        before = before_ref[at, :]
        row = 28 + j if j < 4 else 0
        if j == 4:
            before = before + wide_ref[pl.ds(0, 24, stride=YD), :]
        wide_ref[pl.ds(row, 24, stride=YD), :] = before
    out_copies = started([(wide_ref, wide_hbm)], sems, 2)
    fine_copy.wait()
    for ref, first, mid_first in ((low_ref, 0, 0), (high_ref, CX - 4, 12)):
        for h in range(2):
            for x in range(4):
                at = h * 128 + x * YD
                source = (h * CX + first + x) * CY
                ref[at : at + CY, :] = fine_s[source : source + CY, :]
                source = (h * CX + first + x) * 8
                ref[at + CY : at + YD, :] = halo_ref[source : source + 8, :]
        for i in range(5):
            base = (mid_first + i) * YD
            at = 256 + i * 24
            ref[at : at + 16, :] = wide_ref[base : base + 16, :]
            ref[at + 16 : at + 24, :] = (
                wide_ref[base + 16 : base + 24, :] + wide_ref[base + 24 : base + 32, :]
            )
    out_copies += started([(low_ref, low_hbm), (high_ref, high_hbm)], sems, 3)
    for copy in out_copies:
        copy.wait()


def merge(fine, mid, before, behind):
    out = (
        array(2 * CX * CY, 128),
        array(2 * CX * 8, 128),
        array(24 * YD, 128),
        array(SEND, 128),
        array(SEND, 128),
    )
    return call(
        merge_kernel,
        out,
        [HB, HB, VM, VM],
        [
            pltpu.VMEM((24 * 16, 128), F32),
            *buffers(*out[2:]),
            pltpu.SemaphoreType.DMA((5,)),
        ],
        outs=(VM, VM, HB, HB, HB),
    )(fine, mid, before, behind)


def z_matrices(period, copies):
    half = period // 2
    z = np.arange(period)[:, None]
    f = np.arange(half)[None, :]
    angle = 2 * np.pi * ((z * f) % period) / period
    cosine, sine = np.cos(angle), -np.sin(angle)
    sine[:, 0] = (-1.0) ** np.arange(period)
    scale = np.full((half, 1), 2.0 / period)
    scale[0] = 1.0 / period
    forward = np.zeros((256, 256))
    inverse = np.zeros((256, 256))
    for c in range(copies):
        rows = slice(c * period, (c + 1) * period)
        real = slice(c * half, (c + 1) * half)
        imag = slice(128 + c * half, 128 + (c + 1) * half)
        forward[rows, real] = cosine
        forward[rows, imag] = sine
        inverse[real, rows] = scale * cosine.T
        inverse[imag, rows] = scale * sine.T
    return forward, inverse


def y_matrices():
    order = np.concatenate([np.arange(17), np.arange(31, 16, -1)])
    y = np.arange(YD)
    angle = 2 * np.pi * ((order[:, None] * y[None, :]) % YD) / YD
    cosine, sine = np.cos(angle), np.sin(angle)
    forward = np.block([[cosine, sine], [-sine, cosine]])
    inverse = np.block([[cosine.T, -sine.T], [sine.T, cosine.T]]) / YD
    return np.kron(np.eye(4), forward), np.kron(np.eye(4), inverse)


def stacked_rows(matrix):
    top, rest = np_halves(matrix)
    return np.concatenate([top, rest], axis=0)


def stacked_cols(matrix):
    top, rest = np_halves(matrix)
    return np.concatenate([top, rest], axis=1)


def right_product(value, matrix_ref):
    top, rest = halves(value)
    return (
        mm(top, matrix_ref[:256, :]) + mm(top, matrix_ref[256:, :]) + mm(rest, matrix_ref[:256, :])
    )


def left_product(matrix_ref, value):
    top, rest = halves(value)
    return (
        mm(matrix_ref[:, :256], top) + mm(matrix_ref[:, 256:], top) + mm(matrix_ref[:, :256], rest)
    )


def special_mask(copies, rows):
    lane = lax.broadcasted_iota(jnp.int32, (rows, 128), 1)
    row = lax.broadcasted_iota(jnp.int32, (rows, 128), 0)
    return (lane & (128 // copies - 1)) == 0, row


def forward_chunk(value, z_ref, y_ref, copies):
    z_freq = right_product(value, z_ref)
    stacks = []
    for h in range(2):
        pieces = []
        for q in range(4):
            slab = z_freq[(h * 4 + q) * YD : (h * 4 + q + 1) * YD]
            pieces += [slab[:, :128], slab[:, 128:]]
        stacks.append(jnp.concatenate(pieces, axis=0))
    freq = left_product(y_ref, jnp.concatenate(stacks, axis=1))
    lane_special, row = special_mask(copies, 16)
    special = lane_special & (row != 0)
    slabs = []
    for h in range(2):
        for q in range(4):
            slab = freq[q * 64 : (q + 1) * 64, h * 128 : (h + 1) * 128]
            ar, br, ai, bi = slab[:16], slab[16:32], slab[32:48], slab[48:]
            slabs.append(
                jnp.concatenate(
                    [
                        jnp.where(special, 0.5 * (ar + br), ar),
                        jnp.where(special, 0.5 * (ai + bi), br),
                        jnp.where(special, 0.5 * (ai - bi), ai),
                        jnp.where(special, 0.5 * (br - ar), bi),
                    ],
                    axis=0,
                )
            )
    return slabs


def inverse_chunk(slabs, z_ref, y_ref):
    stacks = [jnp.concatenate(slabs[h * 4 : h * 4 + 4], axis=0) for h in range(2)]
    space = left_product(y_ref, jnp.concatenate(stacks, axis=1))
    rows = []
    for h in range(2):
        for q in range(4):
            slab = space[q * 64 : (q + 1) * 64, h * 128 : (h + 1) * 128]
            rows.append(jnp.concatenate([slab[:YD], slab[YD:]], axis=1))
    return right_product(jnp.concatenate(rows, axis=0), z_ref)


def taps_kernel(copies, in_ref, z_ref, y_ref, after_ref, out_ref):
    for p in range(2):
        slabs = forward_chunk(in_ref[p * 256 : (p + 1) * 256, :], z_ref, y_ref, copies)
        for j in range(8):
            dx = p * 8 + j
            if dx > 8:
                break
            real, imag = slabs[j][:YD], slabs[j][YD:]
            values = (real, imag, real + imag)
            for part in range(3):
                at = (part * 9 + dx) * YD
                out_ref[at : at + YD, :] = values[part]


def taps(kernel, copies, z_matrix, y_matrix, after):
    flipped = kernel[:, ::-1, ::-1]
    tall = jnp.concatenate(
        [flipped[:, 4:], jnp.zeros((9, YD - 9, 9), F32), flipped[:, :4]], axis=1
    )
    period = 256 // copies
    wide = jnp.concatenate(
        [tall[:, :, 4:], jnp.zeros((9, YD, period - 9), F32), tall[:, :, :4]], axis=2
    )
    wide = jnp.concatenate([wide] * copies, axis=2)
    wide = jnp.concatenate([wide, jnp.zeros((7, YD, 256), F32)], axis=0)
    return call(
        functools.partial(taps_kernel, copies), array(27 * YD, 128), [VM] * 3 + [HB]
    )(wide.reshape(16 * YD, 256), z_matrix, y_matrix, after)


def own_kernel(fine_s, halo_s, z_ref, y_ref, out_ref):
    for p in range(CX // 8):
        columns = []
        for h in range(2):
            rows = []
            for j in range(8):
                n = h * CX + p * 8 + j
                rows += [fine_s[n * CY : (n + 1) * CY, :], halo_s[n * 8 : (n + 1) * 8, :]]
            columns.append(jnp.concatenate(rows, axis=0))
        slabs = forward_chunk(jnp.concatenate(columns, axis=1), z_ref, y_ref, 1)
        for j in range(8):
            out_ref[(p * 8 + j) * 64 : (p * 8 + j + 1) * 64, :] = slabs[j]


def convolve(copies, first, count, taps_ref, freq_s, conv_s):
    lane_special, row = special_mask(copies, 8)
    whole = lane_special & (row == 0)
    for v in range(2):
        sums = [[None] * 6 for _ in range(count)]
        for dx in range(9):
            coefs = []
            for half in range(2):
                at = dx * YD + half * 16 + v * 8
                coefs.append([taps_ref[at + part * 288 : at + part * 288 + 8, :] for part in range(3)])
            for j in range(count):
                for half in range(2):
                    at = (first + j + dx) * 96 + v * 8 + half * 16
                    for part in range(3):
                        term = coefs[half][part] * freq_s[at + part * 32 : at + part * 32 + 8, :]
                        n = 3 * half + part
                        sums[j][n] = term if dx == 0 else sums[j][n] + term
        for j in range(count):
            values = []
            for half in range(2):
                re, im, both = sums[j][3 * half : 3 * half + 3]
                real, imag = re - im, both - re - im
                if v == 0:
                    real, imag = jnp.where(whole, re, real), jnp.where(whole, im, imag)
                values += [real, imag]
            ar, ai, br, bi = values
            special = lane_special & (row != 0) if v == 0 else lane_special
            at = (first + j) * 64 + v * 8
            conv_s[at : at + 8, :] = jnp.where(special, ar - bi, ar)
            conv_s[at + 16 : at + 24, :] = jnp.where(special, ar + bi, br)
            conv_s[at + 32 : at + 40, :] = jnp.where(special, ai + br, ai)
            conv_s[at + 48 : at + 56, :] = jnp.where(special, br - ai, bi)


def with_sum(slab):
    return jnp.concatenate([slab, slab[:YD] + slab[YD:]], axis=0)


def wide_slab(ref, index):
    at = 256 + index * 24
    last = ref[at + 16 : at + 24, :]
    row = lax.broadcasted_iota(jnp.int32, (8, 128), 0)
    return jnp.concatenate(
        [ref[at : at + 16, :], jnp.where(row < 4, last, 0.0), jnp.where(row < 4, 0.0, last)], axis=0
    )


def levels_kernel(
    own_ref, before_ref, behind_ref, *refs
):
    zf_ref, yf_ref = refs[:2]
    near_ref, mid_ref, grow_ref, freq_s, conv_s, mid_freq_s, mid_conv_s = refs[10:17]
    wide_ref, mzf_ref, near_taps, mid_taps, zi_ref, yi_ref, mzi_ref, sems = refs[17:]
    copies = started(list(zip(refs[2:10], (*refs[17:24], grow_ref))), sems)
    for x in range(CX):
        freq_s[(x + 4) * 96 : (x + 5) * 96, :] = with_sum(own_ref[x * 64 : (x + 1) * 64, :])
    edges = [
        jnp.concatenate([ref[:128, :], ref[128:256, :]], axis=1) for ref in (before_ref, behind_ref)
    ]
    slabs = forward_chunk(jnp.concatenate(edges, axis=0), zf_ref, yf_ref, 1)
    for j in range(8):
        at = j if j < 4 else 32 + j
        freq_s[at * 96 : (at + 1) * 96, :] = with_sum(slabs[j])
    zero = jnp.zeros((YD, 128), F32)
    copies[0].wait()
    copies[1].wait()
    for p in range(3):
        pairs = []
        for j in range(8):
            pair = []
            for n in (p * 8 + j, p * 8 + j + 9):
                if n > 24 or (n == p * 8 + j and n > 16):
                    slab = zero
                elif n < 4:
                    slab = wide_slab(before_ref, n)
                elif n > 20:
                    slab = wide_slab(behind_ref, n - 20)
                else:
                    slab = wide_ref[(n - 4) * YD : (n - 3) * YD, :]
                    if n == 4:
                        slab = slab + wide_slab(before_ref, 4)
                    if n == 20:
                        slab = slab + wide_slab(behind_ref, 0)
                pair.append(slab)
            pairs.append(jnp.concatenate(pair, axis=1))
        slabs = forward_chunk(jnp.concatenate(pairs, axis=0), mzf_ref, yf_ref, 2)
        for j in range(8):
            at = p * 8 + j
            mid_freq_s[at * 96 : (at + 1) * 96, :] = with_sum(slabs[j])
    for copy in copies[2:]:
        copy.wait()
    for p in range(4):
        convolve(1, p * 8, 8, near_taps, freq_s, conv_s)
        slabs = [conv_s[(p * 8 + j) * 64 : (p * 8 + j + 1) * 64, :] for j in range(8)]
        space = inverse_chunk(slabs, zi_ref, yi_ref)
        for j in range(8):
            x = p * 8 + j
            near_ref[x * CY : (x + 1) * CY, :] = space[j * YD : j * YD + CY]
    mid_conv_s[9 * 64 :, :] = jnp.zeros((7 * 64, 128), F32)
    for first, count in ((0, 5), (5, 4)):
        convolve(2, first, count, mid_taps, mid_freq_s, mid_conv_s)
    for p in range(2):
        slabs = [mid_conv_s[(p * 8 + j) * 64 : (p * 8 + j + 1) * 64, :] for j in range(8)]
        space = inverse_chunk(slabs, mzi_ref, yi_ref)
        for j in range(8):
            i = p * 8 + j
            if i < 9:
                mid_ref[i * 16 : (i + 1) * 16, :] = space[j * YD : j * YD + 16]


def gauss(index, period, width):
    distance = jnp.minimum(index, period - index).astype(F32)
    return jnp.exp(-(distance * distance) / (width * width))


def gauss_kernel(weights_ref, widths_ref, info_ref, after_ref, x_ref, y_ref, z_ref):
    first_x = info_ref[2] * 8
    first_y = info_ref[3] * 6
    row = lax.broadcasted_iota(jnp.int32, (16, 256), 0)
    column = lax.broadcasted_iota(jnp.int32, (16, 256), 1)
    source = jnp.where(column < 128, column, (column - 128) * 8 + 8)
    offset = (first_x + row - source) & 127
    for k in range(4):
        value = jnp.where(column < 144, gauss(offset, 128, widths_ref[k]), 0.0)
        for n, part in enumerate(halves(value)):
            x_ref[n * 64 + k * 16 : n * 64 + (k + 1) * 16, :] = part
    row = lax.broadcasted_iota(jnp.int32, (128, 128), 0)
    column = lax.broadcasted_iota(jnp.int32, (128, 128), 1)
    for k in range(4):
        value = gauss((row - column) & 63, 64, widths_ref[k]) * weights_ref[k]
        value = jnp.where((row >> 6) == (column >> 6), value, 0.0)
        for n, part in enumerate(halves(value)):
            z_ref[(n * 4 + k) * 128 : (n * 4 + k + 1) * 128, :] = part
    row = lax.broadcasted_iota(jnp.int32, (64, 128), 0)
    column = lax.broadcasted_iota(jnp.int32, (64, 128), 1)
    target = (row >> 3) * 6 + (row & 7)
    source = first_y + (column & 3) * 2 + ((column >> 4) & 1)
    offset = target - source
    offset = jnp.where(offset < 0, offset + 48, offset)
    offset = jnp.where(offset >= 48, offset - 48, offset)
    chosen = (column >> 2) & 3
    value = jnp.zeros((64, 128), F32)
    for k in range(4):
        value = jnp.where(chosen == k, gauss(offset, 48, widths_ref[k]), value)
    for n, part in enumerate(halves(jnp.where(column < 32, value, 0.0))):
        y_ref[n * 64 : (n + 1) * 64, :] = part


def top_kernel(in_ref, x_ref, y_ref, z_ref, out_ref, plane_s, depth_s):
    left = (x_ref[:64, :], x_ref[64:, :])
    for jp in range(4):
        tiles = [in_ref[s * TOP_ROWS + jp * 8 : s * TOP_ROWS + jp * 8 + 8, :] for s in range(16)]
        tiles.append(in_ref[pl.ds(32 + jp, SIZE_X, stride=TOP_ROWS), :])
        tiles.append(jnp.zeros((112, 128), F32))
        right = halves(jnp.concatenate(tiles, axis=0))
        plane = mm(left[0], right[0]) + mm(left[0], right[1]) + mm(left[1], right[0])
        for k in range(4):
            plane_s[(k * 4 + jp) * 16 : (k * 4 + jp + 1) * 16, :] = plane[k * 16 : (k + 1) * 16]
    for k in range(4):
        weight = [z_ref[(n * 4 + k) * 128 : (n * 4 + k + 1) * 128, :] for n in range(2)]
        value = halves(plane_s[k * 64 : (k + 1) * 64, :])
        depth_s[k * 64 : (k + 1) * 64, :] = (
            mm(value[0], weight[0]) + mm(value[0], weight[1]) + mm(value[1], weight[0])
        )
    lane = lax.broadcasted_iota(jnp.int32, (16, 128), 1)
    tiles = []
    for ip in range(5):
        first = depth_s[pl.ds(2 * ip, 16, stride=16), :]
        second = depth_s[pl.ds(2 * ip + 1, 16, stride=16), :]
        even = jnp.where(lane < 64, first, pltpu.roll(second, 64, 1))
        odd = jnp.where(lane < 64, pltpu.roll(first, 64, 1), second)
        tiles.append(jnp.concatenate([even, odd, jnp.zeros((96, 128), F32)], axis=0))
    right = halves(jnp.concatenate(tiles, axis=1))
    left = (y_ref[:64, :], y_ref[64:, :])
    out_ref[...] = mm(left[0], right[0]) + mm(left[0], right[1]) + mm(left[1], right[0])


def finish_kernel(
    near_ref, mid_ref, top_ref, *refs
):
    grow_ref, out_hbm, grown_s, out_ref, sems = refs
    grow_top, grow_z = grow_ref[:128, :], grow_ref[128:256, :]
    grow_fine, grow_y = grow_ref[256:, :128], grow_ref[256:272, 128:]
    total = top_ref[:8, :]
    for s in range(1, SIZE_Y):
        total = total + top_ref[s * 8 : (s + 1) * 8, :]
    lanes = []
    for ip in range(5):
        lanes.append(exact_right(total[:, ip * 128 : (ip + 1) * 128], grow_top))
    deep = jnp.concatenate(lanes, axis=1)
    tiles = []
    for i in range(17):
        tile = deep[:, (i // 2) * 128 : (i // 2 + 1) * 128]
        if i % 2:
            tile = 0.5 * (tile + deep[:, (i // 2 + 1) * 128 : (i // 2 + 2) * 128])
        tiles.append(tile)
    flat = jnp.concatenate(tiles, axis=1)
    flat = jnp.concatenate([flat, jnp.zeros((120, 17 * 128), F32)], axis=0)
    tall = exact_left(grow_y, flat)
    slabs = []
    for i in range(24):
        if i > 16:
            slabs.append(jnp.zeros((16, 128), F32))
            continue
        h = i // 9
        slabs.append(
            tall[:, i * 128 : (i + 1) * 128]
            + mid_ref[(i - 9 * h) * 16 : (i - 9 * h + 1) * 16, h * 128 : (h + 1) * 128]
        )
    for g in range(3):
        part = exact_right(jnp.concatenate(slabs[g * 8 : (g + 1) * 8], axis=0), grow_z)
        grown_s[g * 192 : (g + 1) * 192, :] = exact_left(grow_fine, part)
    copies = []
    for x in range(CX):
        at = slice(x * CY, (x + 1) * CY)
        i = x // 2
        value = grown_s[i * CY : (i + 1) * CY, :]
        if x % 2:
            value = 0.5 * (value + grown_s[(i + 1) * CY : (i + 2) * CY, :])
        out_ref[at, :] = near_ref[at, :] + value
        if x % 8 == 7:
            at = pl.ds((x - 7) * CY, 8 * CY)
            copies += started([(out_ref.at[at], out_hbm.at[at])], sems, x // 8)
    for copy in copies:
        copy.wait()


def swap(to_low, to_high, axis):
    count = lax.axis_size(axis)
    forward = [(i, (i + 1) % count) for i in range(count)]
    backward = [(target, source) for source, target in forward]
    before = lax.ppermute(to_high, axis, forward)
    behind = lax.ppermute(to_low, axis, backward)
    return before, behind


def on_device(
    charge_blocks, block_tile, block_count, near_kernel, mid_kernel, top_weights, top_widths
):
    at_x = lax.axis_index("gx")
    at_y = lax.axis_index("gy")
    info = jnp.stack(
        [block_count[0], ((at_x * SIZE_Y + at_y) % 4) * CAP, at_x, at_y]
    ).astype(jnp.int32)
    outgoing = send(block_tile.reshape(32, 128), info, charge_blocks)
    arrived = lax.all_to_all(
        outgoing.reshape(DEVICES, 1, ROWS * 128),
        ("gx", "gy"),
        split_axis=0,
        concat_axis=0,
        tiled=True,
    ).reshape(DEVICES * ROWS, 128)

    z_fine, z_fine_back = z_matrices(256, 1)
    z_mid, z_mid_back = z_matrices(128, 2)
    y_forward, y_back = y_matrices()
    zf, yf = stacked_rows(z_fine), stacked_cols(y_forward)
    zi, yi = stacked_rows(z_fine_back), stacked_cols(y_back)
    mzf, mzi = stacked_rows(z_mid), stacked_rows(z_mid_back)
    near_taps = taps(near_kernel, 1, zf, yf, outgoing)
    mid_taps = taps(mid_kernel, 2, mzf, yf, outgoing)

    bells = call(
        gauss_kernel,
        tuple(jax.ShapeDtypeStruct(n, BF16) for n in ((128, 256), (128, 128), (1024, 128))),
        [SM, SM, SM, HB],
    )(top_weights, top_widths, info, outgoing)

    fine, mid, low, high, top = collect(arrived, near_taps, mid_taps, bells[0])
    before, behind = swap(low, high, "gy")
    tops = lax.all_to_all(
        top.reshape(SIZE_X, TOP_ROWS, 128), "gx", split_axis=0, concat_axis=0, tiled=True
    )
    tops = tops.reshape(SIZE_X * TOP_ROWS, 128)
    partial = call(
        top_kernel,
        array(64, 640),
        [VM] * 4,
        [pltpu.VMEM((256, 128), F32), pltpu.VMEM((256, 128), F32)],
    )(tops, *bells)
    partial = lax.all_to_all(
        partial.reshape(SIZE_Y, 8, 640), "gy", split_axis=0, concat_axis=0, tiled=True
    ).reshape(64, 640)
    fine, halo, wide, low, high = merge(fine, mid, before, behind)
    before, behind = swap(low, high, "gx")
    own = call(own_kernel, array(CX * 64, 128), [VM] * 4)(fine, halo, zf, yf)
    grow_z = grow_matrix(2 * 64, 65)
    grow_z[:, 0] += grow_z[:, 64]
    grow_fine_z = grow_matrix(2 * 128, 129)
    grow_fine_z[:, 0] += grow_fine_z[:, 128]
    grow_y = np.zeros((192, 256))
    grow_y[:, :128] = np.kron(np.eye(8), padded(grow_matrix(CY, 13), CY, 16))
    grow_y[:16, 128:135] = padded(grow_matrix(13, 7), 16, 7)
    grow = plain(np.concatenate([twice(grow_z[:, :64].T), grow_fine_z[:, :128].T, grow_y]))
    tables = (wide, mzf, near_taps, mid_taps, zi, yi, mzi)
    near, mid_near, grow = call(
        levels_kernel,
        (array(CX * CY, NZ), array(9 * 16, 256), jax.ShapeDtypeStruct(grow.shape, BF16)),
        [VM] * 5 + [HB] * 8,
        [
            pltpu.VMEM((40 * 96, 128), F32),
            pltpu.VMEM((32 * 64, 128), F32),
            pltpu.VMEM((24 * 96, 128), F32),
            pltpu.VMEM((16 * 64, 128), F32),
            *buffers(*tables),
            pltpu.SemaphoreType.DMA((8,)),
        ],
        limit=14,
    )(own, before, behind, zf, yf, *tables, grow)
    out = call(
        finish_kernel,
        array(CX * CY, NZ),
        [VM] * 4,
        [
            pltpu.VMEM((24 * CY, NZ), F32),
            pltpu.VMEM((CX * CY, NZ), F32),
            pltpu.SemaphoreType.DMA((4,)),
        ],
        outs=HB,
    )(near, mid_near, partial, grow)
    return out.reshape(CX, CY, NZ)


def solution(mesh):
    placed = (P(("gx", "gy"), None), P(("gx", "gy")), P(("gx", "gy")), P(), P(), P(), P())
    return jax.shard_map(
        on_device, mesh=mesh, in_specs=placed, out_specs=P("gx", "gy", None), check_vma=False
    )
```

```python
import functools

import jax
import jax.numpy as jnp
import numpy as np
from jax import lax
from jax.experimental import pallas as pl
from jax.experimental.pallas import tpu as pltpu
from jax.sharding import PartitionSpec as P


CX = 32
CY = 24
NZ = 256
CAP = 32
DEVICES = 128
ROWS = CAP + 1
SIZE_X = 16
SIZE_Y = 8
DEAD = 2047
SEND = 376
TOP_ROWS = 40
YD = 32
F32 = jnp.float32
BF16 = jnp.bfloat16
VM = pl.BlockSpec(memory_space=pltpu.VMEM)
SM = pl.BlockSpec(memory_space=pltpu.SMEM)
HB = pl.BlockSpec(memory_space=pltpu.HBM)


def call(body, out, ins, scratch=(), limit=10, flops=0, moved=0, outs=VM):
    many = isinstance(out, tuple)
    outs = outs if isinstance(outs, tuple) else (outs,) * (len(out) if many else 1)
    shapes = tuple(
        pltpu.HBM(shape.shape, shape.dtype) if spec is HB else shape
        for shape, spec in zip(out if many else (out,), outs)
    )
    kernel = pl.pallas_call(
        body,
        out_shape=shapes if many else shapes[0],
        in_specs=ins,
        out_specs=outs if many else outs[0],
        scratch_shapes=list(scratch),
        compiler_params=pltpu.CompilerParams(vmem_limit_bytes=limit << 20),
        cost_estimate=pl.CostEstimate(flops=flops, bytes_accessed=moved, transcendentals=0),
    )

    def run(*args):
        placed = [
            pltpu.with_memory_space_constraint(jnp.asarray(arg), pltpu.HBM) if spec is HB else arg
            for arg, spec in zip(args, ins)
        ]
        return kernel(*placed)

    return run


def started(pairs, sems, first=0):
    copies = []
    for n, (source, target) in enumerate(pairs):
        copy = pltpu.make_async_copy(source, target, sems.at[first + n])
        copy.start()
        copies.append(copy)
    return copies


def buffers(*tables):
    return [pltpu.VMEM(table.shape, table.dtype) for table in tables]


def array(*shape):
    return jax.ShapeDtypeStruct(shape, F32)


def mm(a, b):
    return jnp.dot(a, b, preferred_element_type=F32)


def halves(value):
    top = value.astype(BF16)
    return top, (value - top.astype(F32)).astype(BF16)


def np_halves(matrix):
    matrix = np.asarray(matrix, np.float32)
    top = matrix.astype(BF16)
    return top, (matrix - top.astype(np.float32)).astype(BF16)


def send_kernel(
    tile_ref, info_ref, data_ref, out_ref,
    data_s, out_s, hit_s, count_s, place_s, source_s, source_smem, sems,
):
    (data_copy,) = started([(data_ref, data_s)], sems)
    tile = tile_ref[...]
    column = tile >> 1
    high_part = column >> 6
    grid_x = (high_part * 43691) >> 17
    grid_y = column - grid_x * (CY * SIZE_Y)
    owner_y = ((grid_y >> 3) * 43) >> 7
    owner = (grid_x >> 5) * SIZE_Y + owner_y
    cell = (tile & 1) * (CX * CY) + (grid_x & (CX - 1)) * CY + (grid_y - owner_y * CY)
    slot = lax.broadcasted_iota(jnp.int32, tile.shape, 0) * 128 + lax.broadcasted_iota(
        jnp.int32, tile.shape, 1
    )
    code = jnp.where(slot < info_ref[0], cell, DEAD)
    rows = lax.broadcasted_iota(jnp.int32, (128, 128), 0)
    before = lax.broadcasted_iota(jnp.int32, (128, 256), 0)
    after = lax.broadcasted_iota(jnp.int32, (128, 256), 1)
    prefix = jnp.where((before < after) | (after >= 128), 1.0, 0.0).astype(BF16)
    for c in range(32):
        hit = jnp.where(rows == owner[c : c + 1], 1.0, 0.0)
        hit_s[:, c * 128 : (c + 1) * 128] = hit.astype(BF16)
    for g in range(8):
        chunks = [hit_s[:, c * 128 : (c + 1) * 128] for c in range(g * 4, g * 4 + 4)]
        count_s[g * 512 : (g + 1) * 512, :] = mm(jnp.concatenate(chunks, axis=0), prefix)
    base = jnp.zeros((128, 128), F32)
    lane = lax.broadcasted_iota(jnp.int32, (1, 128), 1)
    for c in range(32):
        counted = count_s[c * 128 : (c + 1) * 128, :128] + base
        base = base + count_s[c * 128 : (c + 1) * 128, 128:]
        hit = rows == owner[c : c + 1]
        rank = jnp.sum(jnp.where(hit, counted, 0.0), axis=0, keepdims=True)
        place = rows[:CAP] == rank.astype(jnp.int32)
        ids = code[c : c + 1]
        values = (ids >> 4, ids & 15, c * 2 + (lane >> 6), lane & 63)
        both = [jnp.where(place, value.astype(F32), 0.0) for value in values]
        place_s[:, c * 128 : (c + 1) * 128] = jnp.concatenate(both, axis=0).astype(BF16)
    found = lax.dot_general(
        hit_s[...], place_s[...], (((1,), (1,)), ((), ())), preferred_element_type=F32
    )
    source = found * 64.0 + pltpu.roll(found, 128 - CAP, 1)
    source_s[...] = pltpu.roll(source, 64, 1).astype(jnp.int32)
    quarters = [pl.ds(part * 32, 32) for part in range(4)]
    source_copies = started([(source_s.at[at], source_smem.at[at]) for at in quarters], sems, 5)
    lane = lax.broadcasted_iota(jnp.int32, (128, 128), 1)
    ids = jnp.where(lane < CAP, found * 16.0 + pltpu.roll(found, 128 - CAP, 1), 0.0)
    ids = pltpu.roll(ids, info_ref[1], 1)
    for d in range(DEVICES):
        at = d * ROWS + CAP
        out_s[at : at + 1, :] = ids[d : d + 1]
    data_copy.wait()
    copies = []
    for part in range(4):
        source_copies[part].wait()

        def body(n, carry):
            for q in range(4):
                d = part * 32 + n * 4 + q
                for r in range(CAP):
                    out_s[pl.ds(d * ROWS + r, 1), :] = data_s[pl.ds(source_smem[d, r], 1), :]
            return carry

        lax.fori_loop(0, 8, body, 0)
        at = pl.ds(part * 32 * ROWS, 32 * ROWS)
        copies += started([(out_s.at[at], out_ref.at[at])], sems, 1 + part)
    for copy in copies:
        copy.wait()


def send(tile, info, data):
    return call(
        send_kernel,
        array(DEVICES * ROWS, 128),
        [VM, SM, HB],
        [
            pltpu.VMEM((4096, 128), F32),
            pltpu.VMEM((DEVICES * ROWS, 128), F32),
            pltpu.VMEM((128, 4096), BF16),
            pltpu.VMEM((4096, 256), F32),
            pltpu.VMEM((128, 4096), BF16),
            pltpu.VMEM((128, 128), jnp.int32),
            pltpu.SMEM((128, 128), jnp.int32),
            pltpu.SemaphoreType.DMA((9,)),
        ],
        outs=HB,
        limit=20,
    )(tile, info, data)


def thin_pair(count):
    matrix = np.zeros((count // 2 + 1, count))
    for i in range(count // 2 + 1):
        for source, weight in ((2 * i - 1, 0.5), (2 * i, 1.0), (2 * i + 1, 0.5)):
            if 0 <= source < count:
                matrix[i, source] = weight
    return matrix


def thin_cycle(length):
    matrix = np.zeros((length, length // 2))
    for i in range(length // 2):
        matrix[2 * i, i] += 1.0
        matrix[(2 * i - 1) % length, i] += 0.5
        matrix[(2 * i + 1) % length, i] += 0.5
    return matrix


def grow_matrix(count, source):
    matrix = np.zeros((count, source))
    for i in range(count):
        if i % 2 == 0:
            matrix[i, i // 2] = 1.0
        else:
            matrix[i, i // 2] = 0.5
            matrix[i, i // 2 + 1] = 0.5
    return matrix


def padded(matrix, rows, columns):
    out = np.zeros((rows, columns))
    out[: matrix.shape[0], : matrix.shape[1]] = matrix
    return out


def twice(matrix):
    return np.kron(np.eye(2), matrix)


def plain(matrix):
    return np.asarray(matrix, np.float32).astype(BF16)


def top_rows_matrix():
    rows_x = padded(thin_pair(17), 9, 17)
    rows_y = padded(thin_pair(13), 8, 16)
    rows_y[7] = 0.0
    matrix = np.zeros((2 * TOP_ROWS, 17 * 16))
    for i in range(9):
        for j in range(8):
            line = (j // 2) * 8 + i if i < 8 else 32 + j // 2
            matrix[(j % 2) * TOP_ROWS + line] = np.kron(rows_x[i], rows_y[j])
    return matrix


def exact_left(matrix, value):
    matrix = matrix[...]
    top, rest = halves(value)
    return mm(matrix, top) + mm(matrix, rest)


def exact_right(value, matrix):
    matrix = matrix[...]
    top, rest = halves(value)
    return mm(top, matrix) + mm(rest, matrix)


def collect_kernel(in_ref, *refs):
    tables = refs[:4]
    outs = refs[-15:-13]
    low_ref, high_ref, top_ref = refs[-13:-10]
    data_s, ids_s, slab_s = refs[-10:-7]
    thin_z_ref, thin_y_ref, top_rows_ref, top_z_ref = refs[-7:-3]
    fine_ref, mid_ref, sems = refs[-3:]
    table_copies = started(list(zip(tables, refs[-7:-3])), sems)

    def unpack(c):
        total = None
        for j in range(4):
            base = (c * 4 + j) * ROWS
            top, rest = halves(in_ref[base : base + CAP, :])
            start = (c * 4 + j) * CAP
            data_s[start : start + CAP, :128] = top
            data_s[start : start + CAP, 128:] = rest
            line = in_ref[base + CAP : base + CAP + 1, :]
            total = line if total is None else total + line
        ids_s[c : c + 1, :] = total.astype(jnp.int32)

    rows = lax.broadcasted_iota(jnp.int32, (256, 128), 0).astype(F32).astype(BF16)
    one, zero = jnp.ones((256, 128), BF16), jnp.zeros((256, 128), BF16)

    def block(b, carry):
        first = b * 512 if isinstance(b, int) else pl.multiple_of(b * 512, 512)
        acc = [jnp.zeros((256, 256), F32)] * 2
        for k in range(16):
            if isinstance(b, int):
                unpack(2 * k)
                unpack(2 * k + 1)
            for m in range(2):
                parts = []
                for q in range(2):
                    ids = ids_s[2 * k + q : 2 * k + q + 1, :] - (first + m * 256)
                    line = jnp.clip(ids, -1, 256).astype(F32)
                    line = jnp.broadcast_to(line, (16, 128)).astype(BF16)
                    parts.append(jnp.where(rows == jnp.concatenate([line] * 16, axis=0), one, zero))
                hit = jnp.concatenate(parts, axis=1)
                acc[m] = acc[m] + mm(hit, data_s[k * 256 : (k + 1) * 256, :])
        for m in range(2):
            value = acc[m][:, :128] + acc[m][:, 128:]
            at = first + m * 256
            fine_ref[pl.ds(at if isinstance(b, int) else pl.multiple_of(at, 256), 256), :] = value
        return carry

    block(0, 0)
    lax.fori_loop(1, 3, block, 0)
    out_copies = started([(fine_ref, outs[0])], sems, 4)
    for i in range(17):
        total = None
        for x, weight in ((2 * i, 1.0), (2 * i - 1, 0.5), (2 * i + 1, 0.5)):
            if 0 <= x < CX:
                term = jnp.concatenate(
                    [
                        fine_ref[h * CX * CY + x * CY : h * CX * CY + (x + 1) * CY, :]
                        for h in range(2)
                    ],
                    axis=1,
                )
                term = term if weight == 1.0 else weight * term
                total = term if total is None else total + term
        slab_s[i * CY : (i + 1) * CY, :] = total
    slab_s[17 * CY :, :] = jnp.zeros((7 * CY, NZ), F32)
    for copy in table_copies:
        copy.wait()
    for g in range(3):
        part = exact_right(slab_s[g * 192 : (g + 1) * 192, :], thin_z_ref)
        mid_ref[g * 128 : (g + 1) * 128, :] = exact_left(thin_y_ref, part)
    out_copies += started([(mid_ref, outs[1])], sems, 5)
    for h in range(2):
        for c in range(4):
            at = slice((h * 4 + c) * CX, (h * 4 + c + 1) * CX)
            low_ref[at, :] = fine_ref[pl.ds(h * CX * CY + c, CX, stride=CY), :]
            high_ref[at, :] = fine_ref[pl.ds(h * CX * CY + CY - 4 + c, CX, stride=CY), :]
    for j in range(5):
        at = slice(256 + j * 24, 256 + (j + 1) * 24)
        low_ref[at, :] = mid_ref[pl.ds(j, 24, stride=16), :]
        high_ref[at, :] = mid_ref[pl.ds(8 + j, 24, stride=16), :]
    stacked = exact_left(top_rows_ref, mid_ref[: 17 * 16, :])
    pair = jnp.concatenate([stacked[:TOP_ROWS], stacked[TOP_ROWS:]], axis=1)
    top_charge = exact_right(pair, top_z_ref)
    for s in range(SIZE_X):
        top_ref[s * TOP_ROWS : (s + 1) * TOP_ROWS, :] = top_charge
    for copy in out_copies:
        copy.wait()


def collect(arrived, *after):
    tables = (
        plain(thin_cycle(NZ)),
        plain(np.kron(np.eye(8), padded(thin_pair(CY), 16, CY))),
        plain(top_rows_matrix()),
        plain(twice(thin_cycle(128))),
    )
    out = (
        array(2 * CX * CY, 128),
        array(24 * 16, 128),
        array(SEND, 128),
        array(SEND, 128),
        array(SIZE_X * TOP_ROWS, 128),
    )
    return call(
        collect_kernel,
        out,
        [VM] + [HB] * (4 + len(after)),
        [
            pltpu.VMEM((DEVICES * CAP, 256), BF16),
            pltpu.VMEM((DEVICES // 4, 128), jnp.int32),
            pltpu.VMEM((24 * CY, NZ), F32),
            *buffers(*tables),
            *buffers(*out[:2]),
            pltpu.SemaphoreType.DMA((6,)),
        ],
        outs=(HB, HB, VM, VM, VM),
        limit=20,
    )(arrived, *tables, *after)


def merge_kernel(
    fine_hbm, mid_hbm, before_ref, behind_ref, fine_s, halo_ref, wide_hbm, low_ref, high_ref,
    mid_ref, wide_ref, sems,
):
    mid_copy, fine_copy = started([(mid_hbm, mid_ref), (fine_hbm, fine_s)], sems)
    for h in range(2):
        for c in range(4):
            at = slice((h * 4 + c) * CX, (h * 4 + c + 1) * CX)
            start = h * CX * 8 + c
            halo_ref[pl.ds(start, CX, stride=8), :] = behind_ref[at, :]
            halo_ref[pl.ds(start + 4, CX, stride=8), :] = before_ref[at, :]
    mid_copy.wait()
    for i in range(24):
        wide_ref[i * YD : i * YD + 16, :] = mid_ref[i * 16 : (i + 1) * 16, :]
        wide_ref[i * YD + 16 : (i + 1) * YD, :] = jnp.zeros((16, 128), F32)
    for j in range(5):
        at = slice(256 + j * 24, 256 + (j + 1) * 24)
        behind = behind_ref[at, :]
        if j == 0:
            behind = behind + wide_ref[pl.ds(12, 24, stride=YD), :]
        wide_ref[pl.ds(12 + j, 24, stride=YD), :] = behind
        before = before_ref[at, :]
        row = 28 + j if j < 4 else 0
        if j == 4:
            before = before + wide_ref[pl.ds(0, 24, stride=YD), :]
        wide_ref[pl.ds(row, 24, stride=YD), :] = before
    out_copies = started([(wide_ref, wide_hbm)], sems, 2)
    fine_copy.wait()
    for ref, first, mid_first in ((low_ref, 0, 0), (high_ref, CX - 4, 12)):
        for h in range(2):
            for x in range(4):
                at = h * 128 + x * YD
                source = (h * CX + first + x) * CY
                ref[at : at + CY, :] = fine_s[source : source + CY, :]
                source = (h * CX + first + x) * 8
                ref[at + CY : at + YD, :] = halo_ref[source : source + 8, :]
        for i in range(5):
            base = (mid_first + i) * YD
            at = 256 + i * 24
            ref[at : at + 16, :] = wide_ref[base : base + 16, :]
            ref[at + 16 : at + 24, :] = (
                wide_ref[base + 16 : base + 24, :] + wide_ref[base + 24 : base + 32, :]
            )
    for copy in out_copies:
        copy.wait()


def merge(fine, mid, before, behind):
    out = (
        array(2 * CX * CY, 128),
        array(2 * CX * 8, 128),
        array(24 * YD, 128),
        array(SEND, 128),
        array(SEND, 128),
    )
    return call(
        merge_kernel,
        out,
        [HB, HB, VM, VM],
        [
            pltpu.VMEM((24 * 16, 128), F32),
            *buffers(out[2]),
            pltpu.SemaphoreType.DMA((3,)),
        ],
        outs=(VM, VM, HB, VM, VM),
    )(fine, mid, before, behind)


def z_matrices(period, copies):
    half = period // 2
    z = np.arange(period)[:, None]
    f = np.arange(half)[None, :]
    angle = 2 * np.pi * ((z * f) % period) / period
    cosine, sine = np.cos(angle), -np.sin(angle)
    sine[:, 0] = (-1.0) ** np.arange(period)
    scale = np.full((half, 1), 2.0 / period)
    scale[0] = 1.0 / period
    forward = np.zeros((256, 256))
    inverse = np.zeros((256, 256))
    for c in range(copies):
        rows = slice(c * period, (c + 1) * period)
        real = slice(c * half, (c + 1) * half)
        imag = slice(128 + c * half, 128 + (c + 1) * half)
        forward[rows, real] = cosine
        forward[rows, imag] = sine
        inverse[real, rows] = scale * cosine.T
        inverse[imag, rows] = scale * sine.T
    return forward, inverse


def y_matrices():
    order = np.concatenate([np.arange(17), np.arange(31, 16, -1)])
    y = np.arange(YD)
    angle = 2 * np.pi * ((order[:, None] * y[None, :]) % YD) / YD
    cosine, sine = np.cos(angle), np.sin(angle)
    forward = np.block([[cosine, sine], [-sine, cosine]])
    inverse = np.block([[cosine.T, -sine.T], [sine.T, cosine.T]]) / YD
    return np.kron(np.eye(4), forward), np.kron(np.eye(4), inverse)


def stacked_rows(matrix):
    top, rest = np_halves(matrix)
    return np.concatenate([top, rest], axis=0)


def stacked_cols(matrix):
    top, rest = np_halves(matrix)
    return np.concatenate([top, rest], axis=1)


def right_product(value, matrix_ref):
    top, rest = halves(value)
    return (
        mm(top, matrix_ref[:256, :]) + mm(top, matrix_ref[256:, :]) + mm(rest, matrix_ref[:256, :])
    )


def left_product(matrix_ref, value):
    top, rest = halves(value)
    return (
        mm(matrix_ref[:, :256], top) + mm(matrix_ref[:, 256:], top) + mm(matrix_ref[:, :256], rest)
    )


def special_mask(copies, rows):
    lane = lax.broadcasted_iota(jnp.int32, (rows, 128), 1)
    row = lax.broadcasted_iota(jnp.int32, (rows, 128), 0)
    return (lane & (128 // copies - 1)) == 0, row


def forward_chunk(value, z_ref, y_ref, copies):
    z_freq = right_product(value, z_ref)
    stacks = []
    for h in range(2):
        pieces = []
        for q in range(4):
            slab = z_freq[(h * 4 + q) * YD : (h * 4 + q + 1) * YD]
            pieces += [slab[:, :128], slab[:, 128:]]
        stacks.append(jnp.concatenate(pieces, axis=0))
    freq = left_product(y_ref, jnp.concatenate(stacks, axis=1))
    lane_special, row = special_mask(copies, 16)
    special = lane_special & (row != 0)
    slabs = []
    for h in range(2):
        for q in range(4):
            slab = freq[q * 64 : (q + 1) * 64, h * 128 : (h + 1) * 128]
            ar, br, ai, bi = slab[:16], slab[16:32], slab[32:48], slab[48:]
            slabs.append(
                jnp.concatenate(
                    [
                        jnp.where(special, 0.5 * (ar + br), ar),
                        jnp.where(special, 0.5 * (ai + bi), br),
                        jnp.where(special, 0.5 * (ai - bi), ai),
                        jnp.where(special, 0.5 * (br - ar), bi),
                    ],
                    axis=0,
                )
            )
    return slabs


def inverse_chunk(slabs, z_ref, y_ref):
    stacks = [jnp.concatenate(slabs[h * 4 : h * 4 + 4], axis=0) for h in range(2)]
    space = left_product(y_ref, jnp.concatenate(stacks, axis=1))
    rows = []
    for h in range(2):
        for q in range(4):
            slab = space[q * 64 : (q + 1) * 64, h * 128 : (h + 1) * 128]
            rows.append(jnp.concatenate([slab[:YD], slab[YD:]], axis=1))
    return right_product(jnp.concatenate(rows, axis=0), z_ref)


def taps_kernel(copies, in_ref, z_ref, y_ref, after_ref, out_ref):
    for p in range(2):
        slabs = forward_chunk(in_ref[p * 256 : (p + 1) * 256, :], z_ref, y_ref, copies)
        for j in range(8):
            dx = p * 8 + j
            if dx > 8:
                break
            real, imag = slabs[j][:YD], slabs[j][YD:]
            values = (real, imag, real + imag)
            for part in range(3):
                at = (part * 9 + dx) * YD
                out_ref[at : at + YD, :] = values[part]


def taps(kernel, copies, z_matrix, y_matrix, after):
    flipped = kernel[:, ::-1, ::-1]
    tall = jnp.concatenate(
        [flipped[:, 4:], jnp.zeros((9, YD - 9, 9), F32), flipped[:, :4]], axis=1
    )
    period = 256 // copies
    wide = jnp.concatenate(
        [tall[:, :, 4:], jnp.zeros((9, YD, period - 9), F32), tall[:, :, :4]], axis=2
    )
    wide = jnp.concatenate([wide] * copies, axis=2)
    wide = jnp.concatenate([wide, jnp.zeros((7, YD, 256), F32)], axis=0)
    return call(
        functools.partial(taps_kernel, copies), array(27 * YD, 128), [VM] * 3 + [HB]
    )(wide.reshape(16 * YD, 256), z_matrix, y_matrix, after)


def own_kernel(fine_s, halo_s, z_ref, y_ref, out_ref):
    for p in range(CX // 8):
        columns = []
        for h in range(2):
            rows = []
            for j in range(8):
                n = h * CX + p * 8 + j
                rows += [fine_s[n * CY : (n + 1) * CY, :], halo_s[n * 8 : (n + 1) * 8, :]]
            columns.append(jnp.concatenate(rows, axis=0))
        slabs = forward_chunk(jnp.concatenate(columns, axis=1), z_ref, y_ref, 1)
        for j in range(8):
            out_ref[(p * 8 + j) * 64 : (p * 8 + j + 1) * 64, :] = slabs[j]


def convolve(copies, first, count, taps_ref, freq_s, conv_s):
    lane_special, row = special_mask(copies, 8)
    whole = lane_special & (row == 0)
    for v in range(2):
        sums = [[None] * 6 for _ in range(count)]
        for dx in range(9):
            coefs = []
            for half in range(2):
                at = dx * YD + half * 16 + v * 8
                coefs.append([taps_ref[at + part * 288 : at + part * 288 + 8, :] for part in range(3)])
            for j in range(count):
                for half in range(2):
                    at = (first + j + dx) * 96 + v * 8 + half * 16
                    for part in range(3):
                        term = coefs[half][part] * freq_s[at + part * 32 : at + part * 32 + 8, :]
                        n = 3 * half + part
                        sums[j][n] = term if dx == 0 else sums[j][n] + term
        for j in range(count):
            values = []
            for half in range(2):
                re, im, both = sums[j][3 * half : 3 * half + 3]
                real, imag = re - im, both - re - im
                if v == 0:
                    real, imag = jnp.where(whole, re, real), jnp.where(whole, im, imag)
                values += [real, imag]
            ar, ai, br, bi = values
            special = lane_special & (row != 0) if v == 0 else lane_special
            at = (first + j) * 64 + v * 8
            conv_s[at : at + 8, :] = jnp.where(special, ar - bi, ar)
            conv_s[at + 16 : at + 24, :] = jnp.where(special, ar + bi, br)
            conv_s[at + 32 : at + 40, :] = jnp.where(special, ai + br, ai)
            conv_s[at + 48 : at + 56, :] = jnp.where(special, br - ai, bi)


def with_sum(slab):
    return jnp.concatenate([slab, slab[:YD] + slab[YD:]], axis=0)


def wide_slab(ref, index):
    at = 256 + index * 24
    last = ref[at + 16 : at + 24, :]
    row = lax.broadcasted_iota(jnp.int32, (8, 128), 0)
    return jnp.concatenate(
        [ref[at : at + 16, :], jnp.where(row < 4, last, 0.0), jnp.where(row < 4, 0.0, last)], axis=0
    )


def levels_kernel(
    own_ref, before_ref, behind_ref, *refs
):
    zf_ref, yf_ref = refs[:2]
    near_ref, mid_ref, grow_ref, freq_s, conv_s, mid_freq_s, mid_conv_s = refs[10:17]
    wide_ref, mzf_ref, near_taps, mid_taps, zi_ref, yi_ref, mzi_ref, sems = refs[17:]
    copies = started(list(zip(refs[2:10], (*refs[17:24], grow_ref))), sems)
    for x in range(CX):
        freq_s[(x + 4) * 96 : (x + 5) * 96, :] = with_sum(own_ref[x * 64 : (x + 1) * 64, :])
    edges = [
        jnp.concatenate([ref[:128, :], ref[128:256, :]], axis=1) for ref in (before_ref, behind_ref)
    ]
    slabs = forward_chunk(jnp.concatenate(edges, axis=0), zf_ref, yf_ref, 1)
    for j in range(8):
        at = j if j < 4 else 32 + j
        freq_s[at * 96 : (at + 1) * 96, :] = with_sum(slabs[j])
    zero = jnp.zeros((YD, 128), F32)
    copies[0].wait()
    copies[1].wait()
    for p in range(3):
        pairs = []
        for j in range(8):
            pair = []
            for n in (p * 8 + j, p * 8 + j + 9):
                if n > 24 or (n == p * 8 + j and n > 16):
                    slab = zero
                elif n < 4:
                    slab = wide_slab(before_ref, n)
                elif n > 20:
                    slab = wide_slab(behind_ref, n - 20)
                else:
                    slab = wide_ref[(n - 4) * YD : (n - 3) * YD, :]
                    if n == 4:
                        slab = slab + wide_slab(before_ref, 4)
                    if n == 20:
                        slab = slab + wide_slab(behind_ref, 0)
                pair.append(slab)
            pairs.append(jnp.concatenate(pair, axis=1))
        slabs = forward_chunk(jnp.concatenate(pairs, axis=0), mzf_ref, yf_ref, 2)
        for j in range(8):
            at = p * 8 + j
            mid_freq_s[at * 96 : (at + 1) * 96, :] = with_sum(slabs[j])
    for copy in copies[2:]:
        copy.wait()
    for p in range(4):
        convolve(1, p * 8, 8, near_taps, freq_s, conv_s)
        slabs = [conv_s[(p * 8 + j) * 64 : (p * 8 + j + 1) * 64, :] for j in range(8)]
        space = inverse_chunk(slabs, zi_ref, yi_ref)
        for j in range(8):
            x = p * 8 + j
            near_ref[x * CY : (x + 1) * CY, :] = space[j * YD : j * YD + CY]
    mid_conv_s[9 * 64 :, :] = jnp.zeros((7 * 64, 128), F32)
    for first, count in ((0, 5), (5, 4)):
        convolve(2, first, count, mid_taps, mid_freq_s, mid_conv_s)
    for p in range(2):
        slabs = [mid_conv_s[(p * 8 + j) * 64 : (p * 8 + j + 1) * 64, :] for j in range(8)]
        space = inverse_chunk(slabs, mzi_ref, yi_ref)
        for j in range(8):
            i = p * 8 + j
            if i < 9:
                mid_ref[i * 16 : (i + 1) * 16, :] = space[j * YD : j * YD + 16]


def gauss(index, period, width):
    distance = jnp.minimum(index, period - index).astype(F32)
    return jnp.exp(-(distance * distance) / (width * width))


def gauss_kernel(weights_ref, widths_ref, info_ref, after_ref, x_ref, y_ref, z_ref):
    first_x = info_ref[2] * 8
    first_y = info_ref[3] * 6
    row = lax.broadcasted_iota(jnp.int32, (16, 256), 0)
    column = lax.broadcasted_iota(jnp.int32, (16, 256), 1)
    source = jnp.where(column < 128, column, (column - 128) * 8 + 8)
    offset = (first_x + row - source) & 127
    for k in range(4):
        value = jnp.where(column < 144, gauss(offset, 128, widths_ref[k]), 0.0)
        for n, part in enumerate(halves(value)):
            x_ref[n * 64 + k * 16 : n * 64 + (k + 1) * 16, :] = part
    row = lax.broadcasted_iota(jnp.int32, (128, 128), 0)
    column = lax.broadcasted_iota(jnp.int32, (128, 128), 1)
    for k in range(4):
        value = gauss((row - column) & 63, 64, widths_ref[k]) * weights_ref[k]
        value = jnp.where((row >> 6) == (column >> 6), value, 0.0)
        for n, part in enumerate(halves(value)):
            z_ref[(n * 4 + k) * 128 : (n * 4 + k + 1) * 128, :] = part
    row = lax.broadcasted_iota(jnp.int32, (64, 128), 0)
    column = lax.broadcasted_iota(jnp.int32, (64, 128), 1)
    target = (row >> 3) * 6 + (row & 7)
    source = first_y + (column & 3) * 2 + ((column >> 4) & 1)
    offset = target - source
    offset = jnp.where(offset < 0, offset + 48, offset)
    offset = jnp.where(offset >= 48, offset - 48, offset)
    chosen = (column >> 2) & 3
    value = jnp.zeros((64, 128), F32)
    for k in range(4):
        value = jnp.where(chosen == k, gauss(offset, 48, widths_ref[k]), value)
    for n, part in enumerate(halves(jnp.where(column < 32, value, 0.0))):
        y_ref[n * 64 : (n + 1) * 64, :] = part


def top_kernel(in_ref, x_ref, y_ref, z_ref, out_ref, plane_s, depth_s):
    left = (x_ref[:64, :], x_ref[64:, :])
    columns = []
    for jp in range(4):
        tiles = [in_ref[s * TOP_ROWS + jp * 8 : s * TOP_ROWS + jp * 8 + 8, :] for s in range(16)]
        tiles.append(in_ref[pl.ds(32 + jp, SIZE_X, stride=TOP_ROWS), :])
        tiles.append(jnp.zeros((112, 128), F32))
        columns.append(jnp.concatenate(tiles, axis=0))
    right = halves(jnp.concatenate(columns, axis=1))
    plane = mm(left[0], right[0]) + mm(left[0], right[1]) + mm(left[1], right[0])
    for jp in range(4):
        for k in range(4):
            part = plane[k * 16 : (k + 1) * 16, jp * 128 : (jp + 1) * 128]
            plane_s[(k * 4 + jp) * 16 : (k * 4 + jp + 1) * 16, :] = part
    for k in range(4):
        weight = [z_ref[(n * 4 + k) * 128 : (n * 4 + k + 1) * 128, :] for n in range(2)]
        value = halves(plane_s[k * 64 : (k + 1) * 64, :])
        depth_s[k * 64 : (k + 1) * 64, :] = (
            mm(value[0], weight[0]) + mm(value[0], weight[1]) + mm(value[1], weight[0])
        )
    lane = lax.broadcasted_iota(jnp.int32, (16, 128), 1)
    tiles = []
    for ip in range(5):
        first = depth_s[pl.ds(2 * ip, 16, stride=16), :]
        second = depth_s[pl.ds(2 * ip + 1, 16, stride=16), :]
        even = jnp.where(lane < 64, first, pltpu.roll(second, 64, 1))
        odd = jnp.where(lane < 64, pltpu.roll(first, 64, 1), second)
        tiles.append(jnp.concatenate([even, odd, jnp.zeros((96, 128), F32)], axis=0))
    right = halves(jnp.concatenate(tiles, axis=1))
    left = (y_ref[:64, :], y_ref[64:, :])
    out_ref[...] = mm(left[0], right[0]) + mm(left[0], right[1]) + mm(left[1], right[0])


def finish_kernel(
    near_ref, mid_ref, top_ref, *refs
):
    grow_ref, out_hbm, grown_s, out_ref, sems = refs
    grow_top, grow_z = grow_ref[:128, :], grow_ref[128:256, :]
    grow_fine, grow_y = grow_ref[256:, :128], grow_ref[256:272, 128:]
    total = top_ref[:8, :]
    for s in range(1, SIZE_Y):
        total = total + top_ref[s * 8 : (s + 1) * 8, :]
    lanes = []
    for ip in range(5):
        lanes.append(exact_right(total[:, ip * 128 : (ip + 1) * 128], grow_top))
    deep = jnp.concatenate(lanes, axis=1)
    tiles = []
    for i in range(17):
        tile = deep[:, (i // 2) * 128 : (i // 2 + 1) * 128]
        if i % 2:
            tile = 0.5 * (tile + deep[:, (i // 2 + 1) * 128 : (i // 2 + 2) * 128])
        tiles.append(tile)
    flat = jnp.concatenate(tiles, axis=1)
    flat = jnp.concatenate([flat, jnp.zeros((120, 17 * 128), F32)], axis=0)
    tall = exact_left(grow_y, flat)
    slabs = []
    for i in range(24):
        if i > 16:
            slabs.append(jnp.zeros((16, 128), F32))
            continue
        h = i // 9
        slabs.append(
            tall[:, i * 128 : (i + 1) * 128]
            + mid_ref[(i - 9 * h) * 16 : (i - 9 * h + 1) * 16, h * 128 : (h + 1) * 128]
        )
    for g in range(3):
        part = exact_right(jnp.concatenate(slabs[g * 8 : (g + 1) * 8], axis=0), grow_z)
        grown_s[g * 192 : (g + 1) * 192, :] = exact_left(grow_fine, part)
    copies = []
    for x in range(CX):
        at = slice(x * CY, (x + 1) * CY)
        i = x // 2
        value = grown_s[i * CY : (i + 1) * CY, :]
        if x % 2:
            value = 0.5 * (value + grown_s[(i + 1) * CY : (i + 2) * CY, :])
        out_ref[at, :] = near_ref[at, :] + value
        if x % 8 == 7:
            at = pl.ds((x - 7) * CY, 8 * CY)
            copies += started([(out_ref.at[at], out_hbm.at[at])], sems, x // 8)
    for copy in copies:
        copy.wait()


def swap(to_low, to_high, axis):
    count = lax.axis_size(axis)
    forward = [(i, (i + 1) % count) for i in range(count)]
    backward = [(target, source) for source, target in forward]
    before = lax.ppermute(to_high, axis, forward)
    behind = lax.ppermute(to_low, axis, backward)
    return before, behind


def on_device(
    charge_blocks, block_tile, block_count, near_kernel, mid_kernel, top_weights, top_widths
):
    at_x = lax.axis_index("gx")
    at_y = lax.axis_index("gy")
    info = jnp.stack(
        [block_count[0], ((at_x * SIZE_Y + at_y) % 4) * CAP, at_x, at_y]
    ).astype(jnp.int32)
    outgoing = send(block_tile.reshape(32, 128), info, charge_blocks)
    arrived = lax.all_to_all(
        outgoing.reshape(DEVICES, 1, ROWS * 128),
        ("gx", "gy"),
        split_axis=0,
        concat_axis=0,
        tiled=True,
    ).reshape(DEVICES * ROWS, 128)

    z_fine, z_fine_back = z_matrices(256, 1)
    z_mid, z_mid_back = z_matrices(128, 2)
    y_forward, y_back = y_matrices()
    zf, yf = stacked_rows(z_fine), stacked_cols(y_forward)
    zi, yi = stacked_rows(z_fine_back), stacked_cols(y_back)
    mzf, mzi = stacked_rows(z_mid), stacked_rows(z_mid_back)
    near_taps = taps(near_kernel, 1, zf, yf, outgoing)
    mid_taps = taps(mid_kernel, 2, mzf, yf, outgoing)

    bells = call(
        gauss_kernel,
        tuple(jax.ShapeDtypeStruct(n, BF16) for n in ((128, 256), (128, 128), (1024, 128))),
        [SM, SM, SM, HB],
    )(top_weights, top_widths, info, outgoing)

    fine, mid, low, high, top = collect(arrived, near_taps, mid_taps, bells[0])
    before, behind = swap(low, high, "gy")
    tops = lax.all_to_all(
        top.reshape(SIZE_X, TOP_ROWS, 128), "gx", split_axis=0, concat_axis=0, tiled=True
    )
    tops = tops.reshape(SIZE_X * TOP_ROWS, 128)
    partial = call(
        top_kernel,
        array(64, 640),
        [VM] * 4,
        [pltpu.VMEM((256, 128), F32), pltpu.VMEM((256, 128), F32)],
    )(tops, *bells)
    partial = lax.all_to_all(
        partial.reshape(SIZE_Y, 8, 640), "gy", split_axis=0, concat_axis=0, tiled=True
    ).reshape(64, 640)
    fine, halo, wide, low, high = merge(fine, mid, before, behind)
    before, behind = swap(low, high, "gx")
    own = call(own_kernel, array(CX * 64, 128), [VM] * 4)(fine, halo, zf, yf)
    grow_z = grow_matrix(2 * 64, 65)
    grow_z[:, 0] += grow_z[:, 64]
    grow_fine_z = grow_matrix(2 * 128, 129)
    grow_fine_z[:, 0] += grow_fine_z[:, 128]
    grow_y = np.zeros((192, 256))
    grow_y[:, :128] = np.kron(np.eye(8), padded(grow_matrix(CY, 13), CY, 16))
    grow_y[:16, 128:135] = padded(grow_matrix(13, 7), 16, 7)
    grow = plain(np.concatenate([twice(grow_z[:, :64].T), grow_fine_z[:, :128].T, grow_y]))
    tables = (wide, mzf, near_taps, mid_taps, zi, yi, mzi)
    near, mid_near, grow = call(
        levels_kernel,
        (array(CX * CY, NZ), array(9 * 16, 256), jax.ShapeDtypeStruct(grow.shape, BF16)),
        [VM] * 5 + [HB] * 8,
        [
            pltpu.VMEM((40 * 96, 128), F32),
            pltpu.VMEM((32 * 64, 128), F32),
            pltpu.VMEM((24 * 96, 128), F32),
            pltpu.VMEM((16 * 64, 128), F32),
            *buffers(*tables),
            pltpu.SemaphoreType.DMA((8,)),
        ],
        limit=14,
    )(own, before, behind, zf, yf, *tables, grow)
    out = call(
        finish_kernel,
        array(CX * CY, NZ),
        [VM] * 4,
        [
            pltpu.VMEM((24 * CY, NZ), F32),
            pltpu.VMEM((CX * CY, NZ), F32),
            pltpu.SemaphoreType.DMA((4,)),
        ],
        outs=HB,
    )(near, mid_near, partial, grow)
    return out.reshape(CX, CY, NZ)


def solution(mesh):
    placed = (P(("gx", "gy"), None), P(("gx", "gy")), P(("gx", "gy")), P(), P(), P(), P())
    return jax.shard_map(
        on_device, mesh=mesh, in_specs=placed, out_specs=P("gx", "gy", None), check_vma=False
    )
```

```python
import functools

import jax
import jax.numpy as jnp
import numpy as np
from jax import lax
from jax.experimental import pallas as pl
from jax.experimental.pallas import tpu as pltpu
from jax.sharding import PartitionSpec as P


CX = 32
CY = 24
NZ = 256
CAP = 32
DEVICES = 128
ROWS = CAP + 1
SIZE_X = 16
SIZE_Y = 8
DEAD = 2047
SEND = 376
TOP_ROWS = 40
YD = 32
F32 = jnp.float32
BF16 = jnp.bfloat16
VM = pl.BlockSpec(memory_space=pltpu.VMEM)
SM = pl.BlockSpec(memory_space=pltpu.SMEM)
HB = pl.BlockSpec(memory_space=pltpu.HBM)


def call(body, out, ins, scratch=(), limit=10, flops=0, moved=0, outs=VM):
    many = isinstance(out, tuple)
    outs = outs if isinstance(outs, tuple) else (outs,) * (len(out) if many else 1)
    shapes = tuple(
        pltpu.HBM(shape.shape, shape.dtype) if spec is HB else shape
        for shape, spec in zip(out if many else (out,), outs)
    )
    kernel = pl.pallas_call(
        body,
        out_shape=shapes if many else shapes[0],
        in_specs=ins,
        out_specs=outs if many else outs[0],
        scratch_shapes=list(scratch),
        compiler_params=pltpu.CompilerParams(vmem_limit_bytes=limit << 20),
        cost_estimate=pl.CostEstimate(flops=flops, bytes_accessed=moved, transcendentals=0),
    )

    def run(*args):
        placed = [
            pltpu.with_memory_space_constraint(jnp.asarray(arg), pltpu.HBM) if spec is HB else arg
            for arg, spec in zip(args, ins)
        ]
        return kernel(*placed)

    return run


def started(pairs, sems, first=0):
    copies = []
    for n, (source, target) in enumerate(pairs):
        copy = pltpu.make_async_copy(source, target, sems.at[first + n])
        copy.start()
        copies.append(copy)
    return copies


def buffers(*tables):
    return [pltpu.VMEM(table.shape, table.dtype) for table in tables]


def array(*shape):
    return jax.ShapeDtypeStruct(shape, F32)


def mm(a, b):
    return jnp.dot(a, b, preferred_element_type=F32)


def halves(value):
    top = value.astype(BF16)
    return top, (value - top.astype(F32)).astype(BF16)


def np_halves(matrix):
    matrix = np.asarray(matrix, np.float32)
    top = matrix.astype(BF16)
    return top, (matrix - top.astype(np.float32)).astype(BF16)


def send_kernel(
    tile_ref, info_ref, data_ref, out_ref,
    data_s, out_s, hit_s, count_s, place_s, source_s, source_smem, sems,
):
    (data_copy,) = started([(data_ref, data_s)], sems)
    tile = tile_ref[...]
    column = tile >> 1
    high_part = column >> 6
    grid_x = (high_part * 43691) >> 17
    grid_y = column - grid_x * (CY * SIZE_Y)
    owner_y = ((grid_y >> 3) * 43) >> 7
    owner = (grid_x >> 5) * SIZE_Y + owner_y
    cell = (tile & 1) * (CX * CY) + (grid_x & (CX - 1)) * CY + (grid_y - owner_y * CY)
    slot = lax.broadcasted_iota(jnp.int32, tile.shape, 0) * 128 + lax.broadcasted_iota(
        jnp.int32, tile.shape, 1
    )
    code = jnp.where(slot < info_ref[0], cell, DEAD)
    rows = lax.broadcasted_iota(jnp.int32, (128, 128), 0)
    before = lax.broadcasted_iota(jnp.int32, (128, 256), 0)
    after = lax.broadcasted_iota(jnp.int32, (128, 256), 1)
    prefix = jnp.where((before < after) | (after >= 128), 1.0, 0.0).astype(BF16)
    for c in range(32):
        hit = jnp.where(rows == owner[c : c + 1], 1.0, 0.0)
        hit_s[:, c * 128 : (c + 1) * 128] = hit.astype(BF16)
    for g in range(8):
        chunks = [hit_s[:, c * 128 : (c + 1) * 128] for c in range(g * 4, g * 4 + 4)]
        count_s[g * 512 : (g + 1) * 512, :] = mm(jnp.concatenate(chunks, axis=0), prefix)
    base = jnp.zeros((128, 128), F32)
    lane = lax.broadcasted_iota(jnp.int32, (1, 128), 1)
    for c in range(32):
        counted = count_s[c * 128 : (c + 1) * 128, :128] + base
        base = base + count_s[c * 128 : (c + 1) * 128, 128:]
        hit = rows == owner[c : c + 1]
        rank = jnp.sum(jnp.where(hit, counted, 0.0), axis=0, keepdims=True)
        place = rows[:CAP] == rank.astype(jnp.int32)
        ids = code[c : c + 1]
        values = (ids >> 4, ids & 15, c * 2 + (lane >> 6), lane & 63)
        both = [jnp.where(place, value.astype(F32), 0.0) for value in values]
        place_s[:, c * 128 : (c + 1) * 128] = jnp.concatenate(both, axis=0).astype(BF16)
    found = lax.dot_general(
        hit_s[...], place_s[...], (((1,), (1,)), ((), ())), preferred_element_type=F32
    )
    source = found * 64.0 + pltpu.roll(found, 128 - CAP, 1)
    source_s[...] = pltpu.roll(source, 64, 1).astype(jnp.int32)
    quarters = [pl.ds(part * 32, 32) for part in range(4)]
    source_copies = started([(source_s.at[at], source_smem.at[at]) for at in quarters], sems, 5)
    lane = lax.broadcasted_iota(jnp.int32, (128, 128), 1)
    ids = jnp.where(lane < CAP, found * 16.0 + pltpu.roll(found, 128 - CAP, 1), 0.0)
    ids = pltpu.roll(ids, info_ref[1], 1)
    for d in range(DEVICES):
        at = d * ROWS + CAP
        out_s[at : at + 1, :] = ids[d : d + 1]
    data_copy.wait()
    copies = []
    for part in range(4):
        source_copies[part].wait()

        def body(n, carry):
            for q in range(4):
                d = part * 32 + n * 4 + q
                for r in range(CAP):
                    out_s[pl.ds(d * ROWS + r, 1), :] = data_s[pl.ds(source_smem[d, r], 1), :]
            return carry

        lax.fori_loop(0, 8, body, 0)
        at = pl.ds(part * 32 * ROWS, 32 * ROWS)
        copies += started([(out_s.at[at], out_ref.at[at])], sems, 1 + part)
    for copy in copies:
        copy.wait()


def send(tile, info, data):
    return call(
        send_kernel,
        array(DEVICES * ROWS, 128),
        [VM, SM, HB],
        [
            pltpu.VMEM((4096, 128), F32),
            pltpu.VMEM((DEVICES * ROWS, 128), F32),
            pltpu.VMEM((128, 4096), BF16),
            pltpu.VMEM((4096, 256), F32),
            pltpu.VMEM((128, 4096), BF16),
            pltpu.VMEM((128, 128), jnp.int32),
            pltpu.SMEM((128, 128), jnp.int32),
            pltpu.SemaphoreType.DMA((9,)),
        ],
        outs=HB,
        limit=20,
    )(tile, info, data)


def thin_pair(count):
    matrix = np.zeros((count // 2 + 1, count))
    for i in range(count // 2 + 1):
        for source, weight in ((2 * i - 1, 0.5), (2 * i, 1.0), (2 * i + 1, 0.5)):
            if 0 <= source < count:
                matrix[i, source] = weight
    return matrix


def thin_cycle(length):
    matrix = np.zeros((length, length // 2))
    for i in range(length // 2):
        matrix[2 * i, i] += 1.0
        matrix[(2 * i - 1) % length, i] += 0.5
        matrix[(2 * i + 1) % length, i] += 0.5
    return matrix


def grow_matrix(count, source):
    matrix = np.zeros((count, source))
    for i in range(count):
        if i % 2 == 0:
            matrix[i, i // 2] = 1.0
        else:
            matrix[i, i // 2] = 0.5
            matrix[i, i // 2 + 1] = 0.5
    return matrix


def padded(matrix, rows, columns):
    out = np.zeros((rows, columns))
    out[: matrix.shape[0], : matrix.shape[1]] = matrix
    return out


def twice(matrix):
    return np.kron(np.eye(2), matrix)


def plain(matrix):
    return np.asarray(matrix, np.float32).astype(BF16)


def top_rows_matrix():
    rows_x = padded(thin_pair(17), 9, 17)
    rows_y = padded(thin_pair(13), 8, 16)
    rows_y[7] = 0.0
    matrix = np.zeros((2 * TOP_ROWS, 17 * 16))
    for i in range(9):
        for j in range(8):
            line = (j // 2) * 8 + i if i < 8 else 32 + j // 2
            matrix[(j % 2) * TOP_ROWS + line] = np.kron(rows_x[i], rows_y[j])
    return matrix


def exact_left(matrix, value):
    matrix = matrix[...]
    top, rest = halves(value)
    return mm(matrix, top) + mm(matrix, rest)


def exact_right(value, matrix):
    matrix = matrix[...]
    top, rest = halves(value)
    return mm(top, matrix) + mm(rest, matrix)


def collect_kernel(in_ref, *refs):
    tables = refs[:4]
    *outs, low_ref, high_ref, top_out = refs[-16:-11]
    data_s, ids_s, slab_s = refs[-11:-8]
    thin_z_ref, thin_y_ref, top_rows_ref, top_z_ref = refs[-8:-4]
    fine_ref, mid_ref, top_ref, sems = refs[-4:]
    table_copies = started(list(zip(tables, refs[-8:-4])), sems)

    def unpack(c):
        total = None
        for j in range(4):
            base = (c * 4 + j) * ROWS
            top, rest = halves(in_ref[base : base + CAP, :])
            start = (c * 4 + j) * CAP
            data_s[start : start + CAP, :128] = top
            data_s[start : start + CAP, 128:] = rest
            line = in_ref[base + CAP : base + CAP + 1, :]
            total = line if total is None else total + line
        ids_s[c : c + 1, :] = total.astype(jnp.int32)

    rows = lax.broadcasted_iota(jnp.int32, (256, 128), 0).astype(F32).astype(BF16)
    one, zero = jnp.ones((256, 128), BF16), jnp.zeros((256, 128), BF16)

    def block(b, carry):
        first = b * 512 if isinstance(b, int) else pl.multiple_of(b * 512, 512)
        acc = [jnp.zeros((256, 256), F32)] * 2
        for k in range(16):
            if isinstance(b, int):
                unpack(2 * k)
                unpack(2 * k + 1)
            for m in range(2):
                parts = []
                for q in range(2):
                    ids = ids_s[2 * k + q : 2 * k + q + 1, :] - (first + m * 256)
                    line = jnp.clip(ids, -1, 256).astype(F32)
                    line = jnp.broadcast_to(line, (16, 128)).astype(BF16)
                    parts.append(jnp.where(rows == jnp.concatenate([line] * 16, axis=0), one, zero))
                hit = jnp.concatenate(parts, axis=1)
                acc[m] = acc[m] + mm(hit, data_s[k * 256 : (k + 1) * 256, :])
        for m in range(2):
            value = acc[m][:, :128] + acc[m][:, 128:]
            at = first + m * 256
            fine_ref[pl.ds(at if isinstance(b, int) else pl.multiple_of(at, 256), 256), :] = value
        return carry

    block(0, 0)
    lax.fori_loop(1, 3, block, 0)
    out_copies = started([(fine_ref, outs[0])], sems, 4)
    for i in range(17):
        total = None
        for x, weight in ((2 * i, 1.0), (2 * i - 1, 0.5), (2 * i + 1, 0.5)):
            if 0 <= x < CX:
                term = jnp.concatenate(
                    [
                        fine_ref[h * CX * CY + x * CY : h * CX * CY + (x + 1) * CY, :]
                        for h in range(2)
                    ],
                    axis=1,
                )
                term = term if weight == 1.0 else weight * term
                total = term if total is None else total + term
        slab_s[i * CY : (i + 1) * CY, :] = total
    slab_s[17 * CY :, :] = jnp.zeros((7 * CY, NZ), F32)
    for copy in table_copies:
        copy.wait()
    for g in range(3):
        part = exact_right(slab_s[g * 192 : (g + 1) * 192, :], thin_z_ref)
        mid_ref[g * 128 : (g + 1) * 128, :] = exact_left(thin_y_ref, part)
    out_copies += started([(mid_ref, outs[1])], sems, 5)
    stacked = exact_left(top_rows_ref, mid_ref[: 17 * 16, :])
    pair = jnp.concatenate([stacked[:TOP_ROWS], stacked[TOP_ROWS:]], axis=1)
    top_charge = exact_right(pair, top_z_ref)
    for s in range(SIZE_X):
        top_ref[s * TOP_ROWS : (s + 1) * TOP_ROWS, :] = top_charge
    out_copies += started([(top_ref, top_out)], sems, 6)
    for h in range(2):
        for c in range(4):
            at = slice((h * 4 + c) * CX, (h * 4 + c + 1) * CX)
            low_ref[at, :] = fine_ref[pl.ds(h * CX * CY + c, CX, stride=CY), :]
            high_ref[at, :] = fine_ref[pl.ds(h * CX * CY + CY - 4 + c, CX, stride=CY), :]
    for j in range(5):
        at = slice(256 + j * 24, 256 + (j + 1) * 24)
        low_ref[at, :] = mid_ref[pl.ds(j, 24, stride=16), :]
        high_ref[at, :] = mid_ref[pl.ds(8 + j, 24, stride=16), :]
    for copy in out_copies:
        copy.wait()


def collect(arrived, *after):
    tables = (
        plain(thin_cycle(NZ)),
        plain(np.kron(np.eye(8), padded(thin_pair(CY), 16, CY))),
        plain(top_rows_matrix()),
        plain(twice(thin_cycle(128))),
    )
    out = (
        array(2 * CX * CY, 128),
        array(24 * 16, 128),
        array(SEND, 128),
        array(SEND, 128),
        array(SIZE_X * TOP_ROWS, 128),
    )
    return call(
        collect_kernel,
        out,
        [VM] + [HB] * (4 + len(after)),
        [
            pltpu.VMEM((DEVICES * CAP, 256), BF16),
            pltpu.VMEM((DEVICES // 4, 128), jnp.int32),
            pltpu.VMEM((24 * CY, NZ), F32),
            *buffers(*tables),
            *buffers(out[0], out[1], out[4]),
            pltpu.SemaphoreType.DMA((7,)),
        ],
        outs=(HB, HB, VM, VM, HB),
        limit=20,
    )(arrived, *tables, *after)


def merge_kernel(
    fine_hbm, mid_hbm, before_ref, behind_ref, fine_s, halo_ref, wide_hbm, low_hbm, high_hbm,
    mid_ref, wide_ref, low_ref, high_ref, sems,
):
    mid_copy, fine_copy = started([(mid_hbm, mid_ref), (fine_hbm, fine_s)], sems)
    for h in range(2):
        for c in range(4):
            at = slice((h * 4 + c) * CX, (h * 4 + c + 1) * CX)
            start = h * CX * 8 + c
            halo_ref[pl.ds(start, CX, stride=8), :] = behind_ref[at, :]
            halo_ref[pl.ds(start + 4, CX, stride=8), :] = before_ref[at, :]
    mid_copy.wait()
    for i in range(24):
        wide_ref[i * YD : i * YD + 16, :] = mid_ref[i * 16 : (i + 1) * 16, :]
        wide_ref[i * YD + 16 : (i + 1) * YD, :] = jnp.zeros((16, 128), F32)
    for j in range(5):
        at = slice(256 + j * 24, 256 + (j + 1) * 24)
        behind = behind_ref[at, :]
        if j == 0:
            behind = behind + wide_ref[pl.ds(12, 24, stride=YD), :]
        wide_ref[pl.ds(12 + j, 24, stride=YD), :] = behind
        before = before_ref[at, :]
        row = 28 + j if j < 4 else 0
        if j == 4:
            before = before + wide_ref[pl.ds(0, 24, stride=YD), :]
        wide_ref[pl.ds(row, 24, stride=YD), :] = before
    out_copies = started([(wide_ref, wide_hbm)], sems, 2)
    fine_copy.wait()
    for ref, first, mid_first in ((low_ref, 0, 0), (high_ref, CX - 4, 12)):
        for h in range(2):
            for x in range(4):
                at = h * 128 + x * YD
                source = (h * CX + first + x) * CY
                ref[at : at + CY, :] = fine_s[source : source + CY, :]
                source = (h * CX + first + x) * 8
                ref[at + CY : at + YD, :] = halo_ref[source : source + 8, :]
        for i in range(5):
            base = (mid_first + i) * YD
            at = 256 + i * 24
            ref[at : at + 16, :] = wide_ref[base : base + 16, :]
            ref[at + 16 : at + 24, :] = (
                wide_ref[base + 16 : base + 24, :] + wide_ref[base + 24 : base + 32, :]
            )
    out_copies += started([(low_ref, low_hbm), (high_ref, high_hbm)], sems, 3)
    for copy in out_copies:
        copy.wait()


def merge(fine, mid, before, behind):
    out = (
        array(2 * CX * CY, 128),
        array(2 * CX * 8, 128),
        array(24 * YD, 128),
        array(SEND, 128),
        array(SEND, 128),
    )
    return call(
        merge_kernel,
        out,
        [HB, HB, VM, VM],
        [
            pltpu.VMEM((24 * 16, 128), F32),
            *buffers(*out[2:]),
            pltpu.SemaphoreType.DMA((5,)),
        ],
        outs=(VM, VM, HB, HB, HB),
    )(fine, mid, before, behind)


def z_matrices(period, copies):
    half = period // 2
    z = np.arange(period)[:, None]
    f = np.arange(half)[None, :]
    angle = 2 * np.pi * ((z * f) % period) / period
    cosine, sine = np.cos(angle), -np.sin(angle)
    sine[:, 0] = (-1.0) ** np.arange(period)
    scale = np.full((half, 1), 2.0 / period)
    scale[0] = 1.0 / period
    forward = np.zeros((256, 256))
    inverse = np.zeros((256, 256))
    for c in range(copies):
        rows = slice(c * period, (c + 1) * period)
        real = slice(c * half, (c + 1) * half)
        imag = slice(128 + c * half, 128 + (c + 1) * half)
        forward[rows, real] = cosine
        forward[rows, imag] = sine
        inverse[real, rows] = scale * cosine.T
        inverse[imag, rows] = scale * sine.T
    return forward, inverse


def y_matrices():
    order = np.concatenate([np.arange(17), np.arange(31, 16, -1)])
    y = np.arange(YD)
    angle = 2 * np.pi * ((order[:, None] * y[None, :]) % YD) / YD
    cosine, sine = np.cos(angle), np.sin(angle)
    forward = np.block([[cosine, sine], [-sine, cosine]])
    inverse = np.block([[cosine.T, -sine.T], [sine.T, cosine.T]]) / YD
    return np.kron(np.eye(4), forward), np.kron(np.eye(4), inverse)


def stacked_rows(matrix):
    top, rest = np_halves(matrix)
    return np.concatenate([top, rest], axis=0)


def stacked_cols(matrix):
    top, rest = np_halves(matrix)
    return np.concatenate([top, rest], axis=1)


def right_product(value, matrix_ref):
    top, rest = halves(value)
    return (
        mm(top, matrix_ref[:256, :]) + mm(top, matrix_ref[256:, :]) + mm(rest, matrix_ref[:256, :])
    )


def left_product(matrix_ref, value):
    top, rest = halves(value)
    return (
        mm(matrix_ref[:, :256], top) + mm(matrix_ref[:, 256:], top) + mm(matrix_ref[:, :256], rest)
    )


def special_mask(copies, rows):
    lane = lax.broadcasted_iota(jnp.int32, (rows, 128), 1)
    row = lax.broadcasted_iota(jnp.int32, (rows, 128), 0)
    return (lane & (128 // copies - 1)) == 0, row


def forward_chunk(value, z_ref, y_ref, copies):
    z_freq = right_product(value, z_ref)
    stacks = []
    for h in range(2):
        pieces = []
        for q in range(4):
            slab = z_freq[(h * 4 + q) * YD : (h * 4 + q + 1) * YD]
            pieces += [slab[:, :128], slab[:, 128:]]
        stacks.append(jnp.concatenate(pieces, axis=0))
    freq = left_product(y_ref, jnp.concatenate(stacks, axis=1))
    lane_special, row = special_mask(copies, 16)
    special = lane_special & (row != 0)
    slabs = []
    for h in range(2):
        for q in range(4):
            slab = freq[q * 64 : (q + 1) * 64, h * 128 : (h + 1) * 128]
            ar, br, ai, bi = slab[:16], slab[16:32], slab[32:48], slab[48:]
            slabs.append(
                jnp.concatenate(
                    [
                        jnp.where(special, 0.5 * (ar + br), ar),
                        jnp.where(special, 0.5 * (ai + bi), br),
                        jnp.where(special, 0.5 * (ai - bi), ai),
                        jnp.where(special, 0.5 * (br - ar), bi),
                    ],
                    axis=0,
                )
            )
    return slabs


def inverse_chunk(slabs, z_ref, y_ref):
    stacks = [jnp.concatenate(slabs[h * 4 : h * 4 + 4], axis=0) for h in range(2)]
    space = left_product(y_ref, jnp.concatenate(stacks, axis=1))
    rows = []
    for h in range(2):
        for q in range(4):
            slab = space[q * 64 : (q + 1) * 64, h * 128 : (h + 1) * 128]
            rows.append(jnp.concatenate([slab[:YD], slab[YD:]], axis=1))
    return right_product(jnp.concatenate(rows, axis=0), z_ref)


def taps_kernel(copies, in_ref, z_ref, y_ref, after_ref, out_ref):
    for p in range(2):
        slabs = forward_chunk(in_ref[p * 256 : (p + 1) * 256, :], z_ref, y_ref, copies)
        for j in range(8):
            dx = p * 8 + j
            if dx > 8:
                break
            real, imag = slabs[j][:YD], slabs[j][YD:]
            values = (real, imag, real + imag)
            for part in range(3):
                at = (part * 9 + dx) * YD
                out_ref[at : at + YD, :] = values[part]


def taps(kernel, copies, z_matrix, y_matrix, after):
    flipped = kernel[:, ::-1, ::-1]
    tall = jnp.concatenate(
        [flipped[:, 4:], jnp.zeros((9, YD - 9, 9), F32), flipped[:, :4]], axis=1
    )
    period = 256 // copies
    wide = jnp.concatenate(
        [tall[:, :, 4:], jnp.zeros((9, YD, period - 9), F32), tall[:, :, :4]], axis=2
    )
    wide = jnp.concatenate([wide] * copies, axis=2)
    wide = jnp.concatenate([wide, jnp.zeros((7, YD, 256), F32)], axis=0)
    return call(
        functools.partial(taps_kernel, copies), array(27 * YD, 128), [VM] * 3 + [HB]
    )(wide.reshape(16 * YD, 256), z_matrix, y_matrix, after)


def own_kernel(fine_s, halo_s, z_ref, y_ref, out_ref):
    for p in range(CX // 8):
        columns = []
        for h in range(2):
            rows = []
            for j in range(8):
                n = h * CX + p * 8 + j
                rows += [fine_s[n * CY : (n + 1) * CY, :], halo_s[n * 8 : (n + 1) * 8, :]]
            columns.append(jnp.concatenate(rows, axis=0))
        slabs = forward_chunk(jnp.concatenate(columns, axis=1), z_ref, y_ref, 1)
        for j in range(8):
            out_ref[(p * 8 + j) * 64 : (p * 8 + j + 1) * 64, :] = slabs[j]


def convolve(copies, first, count, taps_ref, freq_s, conv_s):
    lane_special, row = special_mask(copies, 8)
    whole = lane_special & (row == 0)
    for v in range(2):
        sums = [[None] * 6 for _ in range(count)]
        for dx in range(9):
            coefs = []
            for half in range(2):
                at = dx * YD + half * 16 + v * 8
                coefs.append([taps_ref[at + part * 288 : at + part * 288 + 8, :] for part in range(3)])
            for j in range(count):
                for half in range(2):
                    at = (first + j + dx) * 96 + v * 8 + half * 16
                    for part in range(3):
                        term = coefs[half][part] * freq_s[at + part * 32 : at + part * 32 + 8, :]
                        n = 3 * half + part
                        sums[j][n] = term if dx == 0 else sums[j][n] + term
        for j in range(count):
            values = []
            for half in range(2):
                re, im, both = sums[j][3 * half : 3 * half + 3]
                real, imag = re - im, both - re - im
                if v == 0:
                    real, imag = jnp.where(whole, re, real), jnp.where(whole, im, imag)
                values += [real, imag]
            ar, ai, br, bi = values
            special = lane_special & (row != 0) if v == 0 else lane_special
            at = (first + j) * 64 + v * 8
            conv_s[at : at + 8, :] = jnp.where(special, ar - bi, ar)
            conv_s[at + 16 : at + 24, :] = jnp.where(special, ar + bi, br)
            conv_s[at + 32 : at + 40, :] = jnp.where(special, ai + br, ai)
            conv_s[at + 48 : at + 56, :] = jnp.where(special, br - ai, bi)


def with_sum(slab):
    return jnp.concatenate([slab, slab[:YD] + slab[YD:]], axis=0)


def wide_slab(ref, index):
    at = 256 + index * 24
    last = ref[at + 16 : at + 24, :]
    row = lax.broadcasted_iota(jnp.int32, (8, 128), 0)
    return jnp.concatenate(
        [ref[at : at + 16, :], jnp.where(row < 4, last, 0.0), jnp.where(row < 4, 0.0, last)], axis=0
    )


def levels_kernel(
    own_ref, before_ref, behind_ref, *refs
):
    zf_ref, yf_ref = refs[:2]
    near_ref, mid_ref, grow_ref, freq_s, conv_s, mid_freq_s, mid_conv_s = refs[10:17]
    wide_ref, mzf_ref, near_taps, mid_taps, zi_ref, yi_ref, mzi_ref, sems = refs[17:]
    copies = started(list(zip(refs[2:10], (*refs[17:24], grow_ref))), sems)
    for x in range(CX):
        freq_s[(x + 4) * 96 : (x + 5) * 96, :] = with_sum(own_ref[x * 64 : (x + 1) * 64, :])
    edges = [
        jnp.concatenate([ref[:128, :], ref[128:256, :]], axis=1) for ref in (before_ref, behind_ref)
    ]
    slabs = forward_chunk(jnp.concatenate(edges, axis=0), zf_ref, yf_ref, 1)
    for j in range(8):
        at = j if j < 4 else 32 + j
        freq_s[at * 96 : (at + 1) * 96, :] = with_sum(slabs[j])
    zero = jnp.zeros((YD, 128), F32)
    copies[0].wait()
    copies[1].wait()
    for p in range(3):
        pairs = []
        for j in range(8):
            pair = []
            for n in (p * 8 + j, p * 8 + j + 9):
                if n > 24 or (n == p * 8 + j and n > 16):
                    slab = zero
                elif n < 4:
                    slab = wide_slab(before_ref, n)
                elif n > 20:
                    slab = wide_slab(behind_ref, n - 20)
                else:
                    slab = wide_ref[(n - 4) * YD : (n - 3) * YD, :]
                    if n == 4:
                        slab = slab + wide_slab(before_ref, 4)
                    if n == 20:
                        slab = slab + wide_slab(behind_ref, 0)
                pair.append(slab)
            pairs.append(jnp.concatenate(pair, axis=1))
        slabs = forward_chunk(jnp.concatenate(pairs, axis=0), mzf_ref, yf_ref, 2)
        for j in range(8):
            at = p * 8 + j
            mid_freq_s[at * 96 : (at + 1) * 96, :] = with_sum(slabs[j])
    for copy in copies[2:]:
        copy.wait()
    for p in range(4):
        convolve(1, p * 8, 8, near_taps, freq_s, conv_s)
        slabs = [conv_s[(p * 8 + j) * 64 : (p * 8 + j + 1) * 64, :] for j in range(8)]
        space = inverse_chunk(slabs, zi_ref, yi_ref)
        for j in range(8):
            x = p * 8 + j
            near_ref[x * CY : (x + 1) * CY, :] = space[j * YD : j * YD + CY]
    mid_conv_s[9 * 64 :, :] = jnp.zeros((7 * 64, 128), F32)
    for first, count in ((0, 5), (5, 4)):
        convolve(2, first, count, mid_taps, mid_freq_s, mid_conv_s)
    for p in range(2):
        slabs = [mid_conv_s[(p * 8 + j) * 64 : (p * 8 + j + 1) * 64, :] for j in range(8)]
        space = inverse_chunk(slabs, mzi_ref, yi_ref)
        for j in range(8):
            i = p * 8 + j
            if i < 9:
                mid_ref[i * 16 : (i + 1) * 16, :] = space[j * YD : j * YD + 16]


def gauss(index, period, width):
    distance = jnp.minimum(index, period - index).astype(F32)
    return jnp.exp(-(distance * distance) / (width * width))


def gauss_kernel(weights_ref, widths_ref, info_ref, after_ref, x_ref, y_ref, z_ref):
    first_x = info_ref[2] * 8
    first_y = info_ref[3] * 6
    row = lax.broadcasted_iota(jnp.int32, (16, 256), 0)
    column = lax.broadcasted_iota(jnp.int32, (16, 256), 1)
    source = jnp.where(column < 128, column, (column - 128) * 8 + 8)
    offset = (first_x + row - source) & 127
    for k in range(4):
        value = jnp.where(column < 144, gauss(offset, 128, widths_ref[k]), 0.0)
        for n, part in enumerate(halves(value)):
            x_ref[n * 64 + k * 16 : n * 64 + (k + 1) * 16, :] = part
    row = lax.broadcasted_iota(jnp.int32, (128, 128), 0)
    column = lax.broadcasted_iota(jnp.int32, (128, 128), 1)
    for k in range(4):
        value = gauss((row - column) & 63, 64, widths_ref[k]) * weights_ref[k]
        value = jnp.where((row >> 6) == (column >> 6), value, 0.0)
        for n, part in enumerate(halves(value)):
            z_ref[(n * 4 + k) * 128 : (n * 4 + k + 1) * 128, :] = part
    row = lax.broadcasted_iota(jnp.int32, (64, 128), 0)
    column = lax.broadcasted_iota(jnp.int32, (64, 128), 1)
    target = (row >> 3) * 6 + (row & 7)
    source = first_y + (column & 3) * 2 + ((column >> 4) & 1)
    offset = target - source
    offset = jnp.where(offset < 0, offset + 48, offset)
    offset = jnp.where(offset >= 48, offset - 48, offset)
    chosen = (column >> 2) & 3
    value = jnp.zeros((64, 128), F32)
    for k in range(4):
        value = jnp.where(chosen == k, gauss(offset, 48, widths_ref[k]), value)
    for n, part in enumerate(halves(jnp.where(column < 32, value, 0.0))):
        y_ref[n * 64 : (n + 1) * 64, :] = part


def top_kernel(in_ref, x_ref, y_ref, z_ref, out_ref, plane_s, depth_s):
    left = (x_ref[:64, :], x_ref[64:, :])
    columns = []
    for jp in range(4):
        tiles = [in_ref[s * TOP_ROWS + jp * 8 : s * TOP_ROWS + jp * 8 + 8, :] for s in range(16)]
        tiles.append(in_ref[pl.ds(32 + jp, SIZE_X, stride=TOP_ROWS), :])
        tiles.append(jnp.zeros((112, 128), F32))
        columns.append(jnp.concatenate(tiles, axis=0))
    right = halves(jnp.concatenate(columns, axis=1))
    plane = mm(left[0], right[0]) + mm(left[0], right[1]) + mm(left[1], right[0])
    for jp in range(4):
        for k in range(4):
            part = plane[k * 16 : (k + 1) * 16, jp * 128 : (jp + 1) * 128]
            plane_s[(k * 4 + jp) * 16 : (k * 4 + jp + 1) * 16, :] = part
    for k in range(4):
        weight = [z_ref[(n * 4 + k) * 128 : (n * 4 + k + 1) * 128, :] for n in range(2)]
        value = halves(plane_s[k * 64 : (k + 1) * 64, :])
        depth_s[k * 64 : (k + 1) * 64, :] = (
            mm(value[0], weight[0]) + mm(value[0], weight[1]) + mm(value[1], weight[0])
        )
    lane = lax.broadcasted_iota(jnp.int32, (16, 128), 1)
    tiles = []
    for ip in range(5):
        first = depth_s[pl.ds(2 * ip, 16, stride=16), :]
        second = depth_s[pl.ds(2 * ip + 1, 16, stride=16), :]
        even = jnp.where(lane < 64, first, pltpu.roll(second, 64, 1))
        odd = jnp.where(lane < 64, pltpu.roll(first, 64, 1), second)
        tiles.append(jnp.concatenate([even, odd, jnp.zeros((96, 128), F32)], axis=0))
    right = halves(jnp.concatenate(tiles, axis=1))
    left = (y_ref[:64, :], y_ref[64:, :])
    out_ref[...] = mm(left[0], right[0]) + mm(left[0], right[1]) + mm(left[1], right[0])


def finish_kernel(
    near_ref, mid_ref, top_ref, *refs
):
    grow_ref, out_hbm, grown_s, out_ref, sems = refs
    grow_top, grow_z = grow_ref[:128, :], grow_ref[128:256, :]
    grow_fine, grow_y = grow_ref[256:, :128], grow_ref[256:272, 128:]
    total = top_ref[:8, :]
    for s in range(1, SIZE_Y):
        total = total + top_ref[s * 8 : (s + 1) * 8, :]
    lanes = []
    for ip in range(5):
        lanes.append(exact_right(total[:, ip * 128 : (ip + 1) * 128], grow_top))
    deep = jnp.concatenate(lanes, axis=1)
    tiles = []
    for i in range(17):
        tile = deep[:, (i // 2) * 128 : (i // 2 + 1) * 128]
        if i % 2:
            tile = 0.5 * (tile + deep[:, (i // 2 + 1) * 128 : (i // 2 + 2) * 128])
        tiles.append(tile)
    flat = jnp.concatenate(tiles, axis=1)
    flat = jnp.concatenate([flat, jnp.zeros((120, 17 * 128), F32)], axis=0)
    tall = exact_left(grow_y, flat)
    slabs = []
    for i in range(24):
        if i > 16:
            slabs.append(jnp.zeros((16, 128), F32))
            continue
        h = i // 9
        slabs.append(
            tall[:, i * 128 : (i + 1) * 128]
            + mid_ref[(i - 9 * h) * 16 : (i - 9 * h + 1) * 16, h * 128 : (h + 1) * 128]
        )
    for g in range(3):
        part = exact_right(jnp.concatenate(slabs[g * 8 : (g + 1) * 8], axis=0), grow_z)
        grown_s[g * 192 : (g + 1) * 192, :] = exact_left(grow_fine, part)
    copies = []
    for x in range(CX):
        at = slice(x * CY, (x + 1) * CY)
        i = x // 2
        value = grown_s[i * CY : (i + 1) * CY, :]
        if x % 2:
            value = 0.5 * (value + grown_s[(i + 1) * CY : (i + 2) * CY, :])
        out_ref[at, :] = near_ref[at, :] + value
        if x % 8 == 7:
            at = pl.ds((x - 7) * CY, 8 * CY)
            copies += started([(out_ref.at[at], out_hbm.at[at])], sems, x // 8)
    for copy in copies:
        copy.wait()


def swap(to_low, to_high, axis):
    count = lax.axis_size(axis)
    forward = [(i, (i + 1) % count) for i in range(count)]
    backward = [(target, source) for source, target in forward]
    before = lax.ppermute(to_high, axis, forward)
    behind = lax.ppermute(to_low, axis, backward)
    return before, behind


def on_device(
    charge_blocks, block_tile, block_count, near_kernel, mid_kernel, top_weights, top_widths
):
    at_x = lax.axis_index("gx")
    at_y = lax.axis_index("gy")
    info = jnp.stack(
        [block_count[0], ((at_x * SIZE_Y + at_y) % 4) * CAP, at_x, at_y]
    ).astype(jnp.int32)
    outgoing = send(block_tile.reshape(32, 128), info, charge_blocks)
    arrived = lax.all_to_all(
        outgoing.reshape(DEVICES, 1, ROWS * 128),
        ("gx", "gy"),
        split_axis=0,
        concat_axis=0,
        tiled=True,
    ).reshape(DEVICES * ROWS, 128)

    z_fine, z_fine_back = z_matrices(256, 1)
    z_mid, z_mid_back = z_matrices(128, 2)
    y_forward, y_back = y_matrices()
    zf, yf = stacked_rows(z_fine), stacked_cols(y_forward)
    zi, yi = stacked_rows(z_fine_back), stacked_cols(y_back)
    mzf, mzi = stacked_rows(z_mid), stacked_rows(z_mid_back)
    near_taps = taps(near_kernel, 1, zf, yf, outgoing)
    mid_taps = taps(mid_kernel, 2, mzf, yf, outgoing)

    bells = call(
        gauss_kernel,
        tuple(jax.ShapeDtypeStruct(n, BF16) for n in ((128, 256), (128, 128), (1024, 128))),
        [SM, SM, SM, HB],
    )(top_weights, top_widths, info, outgoing)

    fine, mid, low, high, top = collect(arrived, near_taps, mid_taps, bells[0])
    before, behind = swap(low, high, "gy")
    tops = lax.all_to_all(
        top.reshape(SIZE_X, TOP_ROWS, 128), "gx", split_axis=0, concat_axis=0, tiled=True
    )
    tops = tops.reshape(SIZE_X * TOP_ROWS, 128)
    partial = call(
        top_kernel,
        array(64, 640),
        [VM] * 4,
        [pltpu.VMEM((256, 128), F32), pltpu.VMEM((256, 128), F32)],
    )(tops, *bells)
    partial = lax.all_to_all(
        partial.reshape(SIZE_Y, 8, 640), "gy", split_axis=0, concat_axis=0, tiled=True
    ).reshape(64, 640)
    fine, halo, wide, low, high = merge(fine, mid, before, behind)
    before, behind = swap(low, high, "gx")
    own = call(own_kernel, array(CX * 64, 128), [VM] * 4)(fine, halo, zf, yf)
    grow_z = grow_matrix(2 * 64, 65)
    grow_z[:, 0] += grow_z[:, 64]
    grow_fine_z = grow_matrix(2 * 128, 129)
    grow_fine_z[:, 0] += grow_fine_z[:, 128]
    grow_y = np.zeros((192, 256))
    grow_y[:, :128] = np.kron(np.eye(8), padded(grow_matrix(CY, 13), CY, 16))
    grow_y[:16, 128:135] = padded(grow_matrix(13, 7), 16, 7)
    grow = plain(np.concatenate([twice(grow_z[:, :64].T), grow_fine_z[:, :128].T, grow_y]))
    tables = (wide, mzf, near_taps, mid_taps, zi, yi, mzi)
    near, mid_near, grow = call(
        levels_kernel,
        (array(CX * CY, NZ), array(9 * 16, 256), jax.ShapeDtypeStruct(grow.shape, BF16)),
        [VM] * 5 + [HB] * 8,
        [
            pltpu.VMEM((40 * 96, 128), F32),
            pltpu.VMEM((32 * 64, 128), F32),
            pltpu.VMEM((24 * 96, 128), F32),
            pltpu.VMEM((16 * 64, 128), F32),
            *buffers(*tables),
            pltpu.SemaphoreType.DMA((8,)),
        ],
        limit=14,
    )(own, before, behind, zf, yf, *tables, grow)
    out = call(
        finish_kernel,
        array(CX * CY, NZ),
        [VM] * 4,
        [
            pltpu.VMEM((24 * CY, NZ), F32),
            pltpu.VMEM((CX * CY, NZ), F32),
            pltpu.SemaphoreType.DMA((4,)),
        ],
        outs=HB,
    )(near, mid_near, partial, grow)
    return out.reshape(CX, CY, NZ)


def solution(mesh):
    placed = (P(("gx", "gy"), None), P(("gx", "gy")), P(("gx", "gy")), P(), P(), P(), P())
    return jax.shard_map(
        on_device, mesh=mesh, in_specs=placed, out_specs=P("gx", "gy", None), check_vma=False
    )
```

```python
import functools

import jax
import jax.numpy as jnp
import numpy as np
from jax import lax
from jax.experimental import pallas as pl
from jax.experimental.pallas import tpu as pltpu
from jax.sharding import PartitionSpec as P


CX = 32
CY = 24
NZ = 256
CAP = 32
DEVICES = 128
ROWS = CAP + 1
SIZE_X = 16
SIZE_Y = 8
DEAD = 2047
SEND = 376
TOP_ROWS = 40
TOP_SENT = 36
YD = 32
F32 = jnp.float32
BF16 = jnp.bfloat16
VM = pl.BlockSpec(memory_space=pltpu.VMEM)
SM = pl.BlockSpec(memory_space=pltpu.SMEM)
HB = pl.BlockSpec(memory_space=pltpu.HBM)


def call(body, out, ins, scratch=(), limit=10, flops=0, moved=0, outs=VM):
    many = isinstance(out, tuple)
    outs = outs if isinstance(outs, tuple) else (outs,) * (len(out) if many else 1)
    shapes = tuple(
        pltpu.HBM(shape.shape, shape.dtype) if spec is HB else shape
        for shape, spec in zip(out if many else (out,), outs)
    )
    kernel = pl.pallas_call(
        body,
        out_shape=shapes if many else shapes[0],
        in_specs=ins,
        out_specs=outs if many else outs[0],
        scratch_shapes=list(scratch),
        compiler_params=pltpu.CompilerParams(vmem_limit_bytes=limit << 20),
        cost_estimate=pl.CostEstimate(flops=flops, bytes_accessed=moved, transcendentals=0),
    )

    def run(*args):
        placed = [
            pltpu.with_memory_space_constraint(jnp.asarray(arg), pltpu.HBM) if spec is HB else arg
            for arg, spec in zip(args, ins)
        ]
        return kernel(*placed)

    return run


def started(pairs, sems, first=0):
    copies = []
    for n, (source, target) in enumerate(pairs):
        copy = pltpu.make_async_copy(source, target, sems.at[first + n])
        copy.start()
        copies.append(copy)
    return copies


def buffers(*tables):
    return [pltpu.VMEM(table.shape, table.dtype) for table in tables]


def array(*shape):
    return jax.ShapeDtypeStruct(shape, F32)


def mm(a, b):
    return jnp.dot(a, b, preferred_element_type=F32)


def halves(value):
    top = value.astype(BF16)
    return top, (value - top.astype(F32)).astype(BF16)


def np_halves(matrix):
    matrix = np.asarray(matrix, np.float32)
    top = matrix.astype(BF16)
    return top, (matrix - top.astype(np.float32)).astype(BF16)


def send_kernel(
    tile_ref, info_ref, data_ref, out_ref,
    data_s, out_s, hit_s, count_s, place_s, source_s, source_smem, sems,
):
    (data_copy,) = started([(data_ref, data_s)], sems)
    tile = tile_ref[...]
    column = tile >> 1
    high_part = column >> 6
    grid_x = (high_part * 43691) >> 17
    grid_y = column - grid_x * (CY * SIZE_Y)
    owner_y = ((grid_y >> 3) * 43) >> 7
    owner = (grid_x >> 5) * SIZE_Y + owner_y
    cell = (tile & 1) * (CX * CY) + (grid_x & (CX - 1)) * CY + (grid_y - owner_y * CY)
    slot = lax.broadcasted_iota(jnp.int32, tile.shape, 0) * 128 + lax.broadcasted_iota(
        jnp.int32, tile.shape, 1
    )
    code = jnp.where(slot < info_ref[0], cell, DEAD)
    rows = lax.broadcasted_iota(jnp.int32, (128, 128), 0)
    before = lax.broadcasted_iota(jnp.int32, (128, 256), 0)
    after = lax.broadcasted_iota(jnp.int32, (128, 256), 1)
    prefix = jnp.where((before < after) | (after >= 128), 1.0, 0.0).astype(BF16)
    for c in range(32):
        hit = jnp.where(rows == owner[c : c + 1], 1.0, 0.0)
        hit_s[:, c * 128 : (c + 1) * 128] = hit.astype(BF16)
    for g in range(8):
        chunks = [hit_s[:, c * 128 : (c + 1) * 128] for c in range(g * 4, g * 4 + 4)]
        count_s[g * 512 : (g + 1) * 512, :] = mm(jnp.concatenate(chunks, axis=0), prefix)
    base = jnp.zeros((128, 128), F32)
    lane = lax.broadcasted_iota(jnp.int32, (1, 128), 1)
    for c in range(32):
        counted = count_s[c * 128 : (c + 1) * 128, :128] + base
        base = base + count_s[c * 128 : (c + 1) * 128, 128:]
        hit = rows == owner[c : c + 1]
        rank = jnp.sum(jnp.where(hit, counted, 0.0), axis=0, keepdims=True)
        place = rows[:CAP] == rank.astype(jnp.int32)
        ids = code[c : c + 1]
        values = (ids >> 4, ids & 15, c * 2 + (lane >> 6), lane & 63)
        both = [jnp.where(place, value.astype(F32), 0.0) for value in values]
        place_s[:, c * 128 : (c + 1) * 128] = jnp.concatenate(both, axis=0).astype(BF16)
    found = lax.dot_general(
        hit_s[...], place_s[...], (((1,), (1,)), ((), ())), preferred_element_type=F32
    )
    source = found * 64.0 + pltpu.roll(found, 128 - CAP, 1)
    source_s[...] = pltpu.roll(source, 64, 1).astype(jnp.int32)
    quarters = [pl.ds(part * 32, 32) for part in range(4)]
    source_copies = started([(source_s.at[at], source_smem.at[at]) for at in quarters], sems, 5)
    lane = lax.broadcasted_iota(jnp.int32, (128, 128), 1)
    ids = jnp.where(lane < CAP, found * 16.0 + pltpu.roll(found, 128 - CAP, 1), 0.0)
    ids = pltpu.roll(ids, info_ref[1], 1)
    for d in range(DEVICES):
        at = d * ROWS + CAP
        out_s[at : at + 1, :] = ids[d : d + 1]
    data_copy.wait()
    copies = []
    for part in range(4):
        source_copies[part].wait()

        def body(n, carry):
            for q in range(4):
                d = part * 32 + n * 4 + q
                for r in range(CAP):
                    out_s[pl.ds(d * ROWS + r, 1), :] = data_s[pl.ds(source_smem[d, r], 1), :]
            return carry

        lax.fori_loop(0, 8, body, 0)
        at = pl.ds(part * 32 * ROWS, 32 * ROWS)
        copies += started([(out_s.at[at], out_ref.at[at])], sems, 1 + part)
    for copy in copies:
        copy.wait()


def send(tile, info, data):
    return call(
        send_kernel,
        array(DEVICES * ROWS, 128),
        [VM, SM, HB],
        [
            pltpu.VMEM((4096, 128), F32),
            pltpu.VMEM((DEVICES * ROWS, 128), F32),
            pltpu.VMEM((128, 4096), BF16),
            pltpu.VMEM((4096, 256), F32),
            pltpu.VMEM((128, 4096), BF16),
            pltpu.VMEM((128, 128), jnp.int32),
            pltpu.SMEM((128, 128), jnp.int32),
            pltpu.SemaphoreType.DMA((9,)),
        ],
        outs=HB,
        limit=20,
    )(tile, info, data)


def thin_pair(count):
    matrix = np.zeros((count // 2 + 1, count))
    for i in range(count // 2 + 1):
        for source, weight in ((2 * i - 1, 0.5), (2 * i, 1.0), (2 * i + 1, 0.5)):
            if 0 <= source < count:
                matrix[i, source] = weight
    return matrix


def thin_cycle(length):
    matrix = np.zeros((length, length // 2))
    for i in range(length // 2):
        matrix[2 * i, i] += 1.0
        matrix[(2 * i - 1) % length, i] += 0.5
        matrix[(2 * i + 1) % length, i] += 0.5
    return matrix


def grow_matrix(count, source):
    matrix = np.zeros((count, source))
    for i in range(count):
        if i % 2 == 0:
            matrix[i, i // 2] = 1.0
        else:
            matrix[i, i // 2] = 0.5
            matrix[i, i // 2 + 1] = 0.5
    return matrix


def padded(matrix, rows, columns):
    out = np.zeros((rows, columns))
    out[: matrix.shape[0], : matrix.shape[1]] = matrix
    return out


def twice(matrix):
    return np.kron(np.eye(2), matrix)


def plain(matrix):
    return np.asarray(matrix, np.float32).astype(BF16)


def top_rows_matrix():
    rows_x = padded(thin_pair(17), 9, 17)
    rows_y = padded(thin_pair(13), 8, 16)
    rows_y[7] = 0.0
    matrix = np.zeros((2 * TOP_ROWS, 17 * 16))
    for i in range(9):
        for j in range(8):
            line = (j // 2) * 8 + i if i < 8 else 32 + j // 2
            matrix[(j % 2) * TOP_ROWS + line] = np.kron(rows_x[i], rows_y[j])
    return matrix


def exact_left(matrix, value):
    matrix = matrix[...]
    top, rest = halves(value)
    return mm(matrix, top) + mm(matrix, rest)


def exact_right(value, matrix):
    matrix = matrix[...]
    top, rest = halves(value)
    return mm(top, matrix) + mm(rest, matrix)


def collect_kernel(in_ref, *refs):
    tables = refs[:4]
    *outs, low_ref, high_ref, top_out = refs[-16:-11]
    data_s, ids_s, slab_s = refs[-11:-8]
    thin_z_ref, thin_y_ref, top_rows_ref, top_z_ref = refs[-8:-4]
    fine_ref, mid_ref, top_ref, sems = refs[-4:]
    table_copies = started(list(zip(tables, refs[-8:-4])), sems)

    def unpack(c):
        total = None
        for j in range(4):
            base = (c * 4 + j) * ROWS
            top, rest = halves(in_ref[base : base + CAP, :])
            start = (c * 4 + j) * CAP
            data_s[start : start + CAP, :128] = top
            data_s[start : start + CAP, 128:] = rest
            line = in_ref[base + CAP : base + CAP + 1, :]
            total = line if total is None else total + line
        ids_s[c : c + 1, :] = total.astype(jnp.int32)

    rows = lax.broadcasted_iota(jnp.int32, (256, 128), 0).astype(F32).astype(BF16)
    one, zero = jnp.ones((256, 128), BF16), jnp.zeros((256, 128), BF16)

    def block(b, carry):
        first = b * 512 if isinstance(b, int) else pl.multiple_of(b * 512, 512)
        acc = [jnp.zeros((256, 256), F32)] * 2
        for k in range(16):
            if isinstance(b, int):
                unpack(2 * k)
                unpack(2 * k + 1)
            for m in range(2):
                parts = []
                for q in range(2):
                    ids = ids_s[2 * k + q : 2 * k + q + 1, :] - (first + m * 256)
                    line = jnp.clip(ids, -1, 256).astype(F32)
                    line = jnp.broadcast_to(line, (16, 128)).astype(BF16)
                    parts.append(jnp.where(rows == jnp.concatenate([line] * 16, axis=0), one, zero))
                hit = jnp.concatenate(parts, axis=1)
                acc[m] = acc[m] + mm(hit, data_s[k * 256 : (k + 1) * 256, :])
        for m in range(2):
            value = acc[m][:, :128] + acc[m][:, 128:]
            at = first + m * 256
            fine_ref[pl.ds(at if isinstance(b, int) else pl.multiple_of(at, 256), 256), :] = value
        return carry

    block(0, 0)
    lax.fori_loop(1, 3, block, 0)
    out_copies = started([(fine_ref, outs[0])], sems, 4)
    for i in range(17):
        total = None
        for x, weight in ((2 * i, 1.0), (2 * i - 1, 0.5), (2 * i + 1, 0.5)):
            if 0 <= x < CX:
                term = jnp.concatenate(
                    [
                        fine_ref[h * CX * CY + x * CY : h * CX * CY + (x + 1) * CY, :]
                        for h in range(2)
                    ],
                    axis=1,
                )
                term = term if weight == 1.0 else weight * term
                total = term if total is None else total + term
        slab_s[i * CY : (i + 1) * CY, :] = total
    slab_s[17 * CY :, :] = jnp.zeros((7 * CY, NZ), F32)
    for copy in table_copies:
        copy.wait()
    for g in range(3):
        part = exact_right(slab_s[g * 192 : (g + 1) * 192, :], thin_z_ref)
        mid_ref[g * 128 : (g + 1) * 128, :] = exact_left(thin_y_ref, part)
    out_copies += started([(mid_ref, outs[1])], sems, 5)
    stacked = exact_left(top_rows_ref, mid_ref[: 17 * 16, :])
    pair = jnp.concatenate([stacked[:TOP_ROWS], stacked[TOP_ROWS:]], axis=1)
    top_charge = exact_right(pair, top_z_ref)
    for s in range(SIZE_X):
        top_ref[s * TOP_SENT : (s + 1) * TOP_SENT, :] = top_charge[:TOP_SENT]
    out_copies += started([(top_ref, top_out)], sems, 6)
    for h in range(2):
        for c in range(4):
            at = slice((h * 4 + c) * CX, (h * 4 + c + 1) * CX)
            low_ref[at, :] = fine_ref[pl.ds(h * CX * CY + c, CX, stride=CY), :]
            high_ref[at, :] = fine_ref[pl.ds(h * CX * CY + CY - 4 + c, CX, stride=CY), :]
    for j in range(5):
        at = slice(256 + j * 24, 256 + (j + 1) * 24)
        low_ref[at, :] = mid_ref[pl.ds(j, 24, stride=16), :]
        high_ref[at, :] = mid_ref[pl.ds(8 + j, 24, stride=16), :]
    for copy in out_copies:
        copy.wait()


def collect(arrived, *after):
    tables = (
        plain(thin_cycle(NZ)),
        plain(np.kron(np.eye(8), padded(thin_pair(CY), 16, CY))),
        plain(top_rows_matrix()),
        plain(twice(thin_cycle(128))),
    )
    out = (
        array(2 * CX * CY, 128),
        array(24 * 16, 128),
        array(SEND, 128),
        array(SEND, 128),
        array(SIZE_X * TOP_SENT, 128),
    )
    return call(
        collect_kernel,
        out,
        [VM] + [HB] * (4 + len(after)),
        [
            pltpu.VMEM((DEVICES * CAP, 256), BF16),
            pltpu.VMEM((DEVICES // 4, 128), jnp.int32),
            pltpu.VMEM((24 * CY, NZ), F32),
            *buffers(*tables),
            *buffers(out[0], out[1], out[4]),
            pltpu.SemaphoreType.DMA((7,)),
        ],
        outs=(HB, HB, VM, VM, HB),
        limit=20,
    )(arrived, *tables, *after)


def merge_kernel(
    fine_hbm, mid_hbm, before_ref, behind_ref, fine_s, halo_ref, wide_hbm, low_hbm, high_hbm,
    mid_ref, wide_ref, low_ref, high_ref, sems,
):
    mid_copy, fine_copy = started([(mid_hbm, mid_ref), (fine_hbm, fine_s)], sems)
    for h in range(2):
        for c in range(4):
            at = slice((h * 4 + c) * CX, (h * 4 + c + 1) * CX)
            start = h * CX * 8 + c
            halo_ref[pl.ds(start, CX, stride=8), :] = behind_ref[at, :]
            halo_ref[pl.ds(start + 4, CX, stride=8), :] = before_ref[at, :]
    mid_copy.wait()
    for i in range(24):
        wide_ref[i * YD : i * YD + 16, :] = mid_ref[i * 16 : (i + 1) * 16, :]
        wide_ref[i * YD + 16 : (i + 1) * YD, :] = jnp.zeros((16, 128), F32)
    for j in range(5):
        at = slice(256 + j * 24, 256 + (j + 1) * 24)
        behind = behind_ref[at, :]
        if j == 0:
            behind = behind + wide_ref[pl.ds(12, 24, stride=YD), :]
        wide_ref[pl.ds(12 + j, 24, stride=YD), :] = behind
        before = before_ref[at, :]
        row = 28 + j if j < 4 else 0
        if j == 4:
            before = before + wide_ref[pl.ds(0, 24, stride=YD), :]
        wide_ref[pl.ds(row, 24, stride=YD), :] = before
    out_copies = started([(wide_ref, wide_hbm)], sems, 2)
    fine_copy.wait()
    for ref, first, mid_first in ((low_ref, 0, 0), (high_ref, CX - 4, 12)):
        for h in range(2):
            for x in range(4):
                at = h * 128 + x * YD
                source = (h * CX + first + x) * CY
                ref[at : at + CY, :] = fine_s[source : source + CY, :]
                source = (h * CX + first + x) * 8
                ref[at + CY : at + YD, :] = halo_ref[source : source + 8, :]
        for i in range(5):
            base = (mid_first + i) * YD
            at = 256 + i * 24
            ref[at : at + 16, :] = wide_ref[base : base + 16, :]
            ref[at + 16 : at + 24, :] = (
                wide_ref[base + 16 : base + 24, :] + wide_ref[base + 24 : base + 32, :]
            )
    out_copies += started([(low_ref, low_hbm), (high_ref, high_hbm)], sems, 3)
    for copy in out_copies:
        copy.wait()


def merge(fine, mid, before, behind):
    out = (
        array(2 * CX * CY, 128),
        array(2 * CX * 8, 128),
        array(24 * YD, 128),
        array(SEND, 128),
        array(SEND, 128),
    )
    return call(
        merge_kernel,
        out,
        [HB, HB, VM, VM],
        [
            pltpu.VMEM((24 * 16, 128), F32),
            *buffers(*out[2:]),
            pltpu.SemaphoreType.DMA((5,)),
        ],
        outs=(VM, VM, HB, HB, HB),
    )(fine, mid, before, behind)


def z_matrices(period, copies):
    half = period // 2
    z = np.arange(period)[:, None]
    f = np.arange(half)[None, :]
    angle = 2 * np.pi * ((z * f) % period) / period
    cosine, sine = np.cos(angle), -np.sin(angle)
    sine[:, 0] = (-1.0) ** np.arange(period)
    scale = np.full((half, 1), 2.0 / period)
    scale[0] = 1.0 / period
    forward = np.zeros((256, 256))
    inverse = np.zeros((256, 256))
    for c in range(copies):
        rows = slice(c * period, (c + 1) * period)
        real = slice(c * half, (c + 1) * half)
        imag = slice(128 + c * half, 128 + (c + 1) * half)
        forward[rows, real] = cosine
        forward[rows, imag] = sine
        inverse[real, rows] = scale * cosine.T
        inverse[imag, rows] = scale * sine.T
    return forward, inverse


def y_matrices():
    order = np.concatenate([np.arange(17), np.arange(31, 16, -1)])
    y = np.arange(YD)
    angle = 2 * np.pi * ((order[:, None] * y[None, :]) % YD) / YD
    cosine, sine = np.cos(angle), np.sin(angle)
    forward = np.block([[cosine, sine], [-sine, cosine]])
    inverse = np.block([[cosine.T, -sine.T], [sine.T, cosine.T]]) / YD
    return np.kron(np.eye(4), forward), np.kron(np.eye(4), inverse)


def stacked_rows(matrix):
    top, rest = np_halves(matrix)
    return np.concatenate([top, rest], axis=0)


def stacked_cols(matrix):
    top, rest = np_halves(matrix)
    return np.concatenate([top, rest], axis=1)


def right_product(value, matrix_ref):
    top, rest = halves(value)
    return (
        mm(top, matrix_ref[:256, :]) + mm(top, matrix_ref[256:, :]) + mm(rest, matrix_ref[:256, :])
    )


def left_product(matrix_ref, value):
    top, rest = halves(value)
    return (
        mm(matrix_ref[:, :256], top) + mm(matrix_ref[:, 256:], top) + mm(matrix_ref[:, :256], rest)
    )


def special_mask(copies, rows):
    lane = lax.broadcasted_iota(jnp.int32, (rows, 128), 1)
    row = lax.broadcasted_iota(jnp.int32, (rows, 128), 0)
    return (lane & (128 // copies - 1)) == 0, row


def forward_chunk(value, z_ref, y_ref, copies):
    z_freq = right_product(value, z_ref)
    stacks = []
    for h in range(2):
        pieces = []
        for q in range(4):
            slab = z_freq[(h * 4 + q) * YD : (h * 4 + q + 1) * YD]
            pieces += [slab[:, :128], slab[:, 128:]]
        stacks.append(jnp.concatenate(pieces, axis=0))
    freq = left_product(y_ref, jnp.concatenate(stacks, axis=1))
    lane_special, row = special_mask(copies, 16)
    special = lane_special & (row != 0)
    slabs = []
    for h in range(2):
        for q in range(4):
            slab = freq[q * 64 : (q + 1) * 64, h * 128 : (h + 1) * 128]
            ar, br, ai, bi = slab[:16], slab[16:32], slab[32:48], slab[48:]
            slabs.append(
                jnp.concatenate(
                    [
                        jnp.where(special, 0.5 * (ar + br), ar),
                        jnp.where(special, 0.5 * (ai + bi), br),
                        jnp.where(special, 0.5 * (ai - bi), ai),
                        jnp.where(special, 0.5 * (br - ar), bi),
                    ],
                    axis=0,
                )
            )
    return slabs


def inverse_chunk(slabs, z_ref, y_ref):
    stacks = [jnp.concatenate(slabs[h * 4 : h * 4 + 4], axis=0) for h in range(2)]
    space = left_product(y_ref, jnp.concatenate(stacks, axis=1))
    rows = []
    for h in range(2):
        for q in range(4):
            slab = space[q * 64 : (q + 1) * 64, h * 128 : (h + 1) * 128]
            rows.append(jnp.concatenate([slab[:YD], slab[YD:]], axis=1))
    return right_product(jnp.concatenate(rows, axis=0), z_ref)


def taps_kernel(copies, in_ref, z_ref, y_ref, after_ref, out_ref):
    for p in range(2):
        slabs = forward_chunk(in_ref[p * 256 : (p + 1) * 256, :], z_ref, y_ref, copies)
        for j in range(8):
            dx = p * 8 + j
            if dx > 8:
                break
            real, imag = slabs[j][:YD], slabs[j][YD:]
            values = (real, imag, real + imag)
            for part in range(3):
                at = (part * 9 + dx) * YD
                out_ref[at : at + YD, :] = values[part]


def taps(kernel, copies, z_matrix, y_matrix, after):
    flipped = kernel[:, ::-1, ::-1]
    tall = jnp.concatenate(
        [flipped[:, 4:], jnp.zeros((9, YD - 9, 9), F32), flipped[:, :4]], axis=1
    )
    period = 256 // copies
    wide = jnp.concatenate(
        [tall[:, :, 4:], jnp.zeros((9, YD, period - 9), F32), tall[:, :, :4]], axis=2
    )
    wide = jnp.concatenate([wide] * copies, axis=2)
    wide = jnp.concatenate([wide, jnp.zeros((7, YD, 256), F32)], axis=0)
    return call(
        functools.partial(taps_kernel, copies), array(27 * YD, 128), [VM] * 3 + [HB]
    )(wide.reshape(16 * YD, 256), z_matrix, y_matrix, after)


def own_kernel(fine_s, halo_s, z_ref, y_ref, out_ref):
    for p in range(CX // 8):
        columns = []
        for h in range(2):
            rows = []
            for j in range(8):
                n = h * CX + p * 8 + j
                rows += [fine_s[n * CY : (n + 1) * CY, :], halo_s[n * 8 : (n + 1) * 8, :]]
            columns.append(jnp.concatenate(rows, axis=0))
        slabs = forward_chunk(jnp.concatenate(columns, axis=1), z_ref, y_ref, 1)
        for j in range(8):
            out_ref[(p * 8 + j) * 64 : (p * 8 + j + 1) * 64, :] = slabs[j]


def convolve(copies, first, count, taps_ref, freq_s, conv_s):
    lane_special, row = special_mask(copies, 8)
    whole = lane_special & (row == 0)
    for v in range(2):
        sums = [[None] * 6 for _ in range(count)]
        for dx in range(9):
            coefs = []
            for half in range(2):
                at = dx * YD + half * 16 + v * 8
                coefs.append([taps_ref[at + part * 288 : at + part * 288 + 8, :] for part in range(3)])
            for j in range(count):
                for half in range(2):
                    at = (first + j + dx) * 96 + v * 8 + half * 16
                    for part in range(3):
                        term = coefs[half][part] * freq_s[at + part * 32 : at + part * 32 + 8, :]
                        n = 3 * half + part
                        sums[j][n] = term if dx == 0 else sums[j][n] + term
        for j in range(count):
            values = []
            for half in range(2):
                re, im, both = sums[j][3 * half : 3 * half + 3]
                real, imag = re - im, both - re - im
                if v == 0:
                    real, imag = jnp.where(whole, re, real), jnp.where(whole, im, imag)
                values += [real, imag]
            ar, ai, br, bi = values
            special = lane_special & (row != 0) if v == 0 else lane_special
            at = (first + j) * 64 + v * 8
            conv_s[at : at + 8, :] = jnp.where(special, ar - bi, ar)
            conv_s[at + 16 : at + 24, :] = jnp.where(special, ar + bi, br)
            conv_s[at + 32 : at + 40, :] = jnp.where(special, ai + br, ai)
            conv_s[at + 48 : at + 56, :] = jnp.where(special, br - ai, bi)


def with_sum(slab):
    return jnp.concatenate([slab, slab[:YD] + slab[YD:]], axis=0)


def wide_slab(ref, index):
    at = 256 + index * 24
    last = ref[at + 16 : at + 24, :]
    row = lax.broadcasted_iota(jnp.int32, (8, 128), 0)
    return jnp.concatenate(
        [ref[at : at + 16, :], jnp.where(row < 4, last, 0.0), jnp.where(row < 4, 0.0, last)], axis=0
    )


def levels_kernel(
    own_ref, before_ref, behind_ref, *refs
):
    zf_ref, yf_ref = refs[:2]
    near_ref, mid_ref, grow_ref, freq_s, conv_s, mid_freq_s, mid_conv_s = refs[10:17]
    wide_ref, mzf_ref, near_taps, mid_taps, zi_ref, yi_ref, mzi_ref, sems = refs[17:]
    copies = started(list(zip(refs[2:10], (*refs[17:24], grow_ref))), sems)
    for x in range(CX):
        freq_s[(x + 4) * 96 : (x + 5) * 96, :] = with_sum(own_ref[x * 64 : (x + 1) * 64, :])
    edges = [
        jnp.concatenate([ref[:128, :], ref[128:256, :]], axis=1) for ref in (before_ref, behind_ref)
    ]
    slabs = forward_chunk(jnp.concatenate(edges, axis=0), zf_ref, yf_ref, 1)
    for j in range(8):
        at = j if j < 4 else 32 + j
        freq_s[at * 96 : (at + 1) * 96, :] = with_sum(slabs[j])
    zero = jnp.zeros((YD, 128), F32)
    copies[0].wait()
    copies[1].wait()
    for p in range(3):
        pairs = []
        for j in range(8):
            pair = []
            for n in (p * 8 + j, p * 8 + j + 9):
                if n > 24 or (n == p * 8 + j and n > 16):
                    slab = zero
                elif n < 4:
                    slab = wide_slab(before_ref, n)
                elif n > 20:
                    slab = wide_slab(behind_ref, n - 20)
                else:
                    slab = wide_ref[(n - 4) * YD : (n - 3) * YD, :]
                    if n == 4:
                        slab = slab + wide_slab(before_ref, 4)
                    if n == 20:
                        slab = slab + wide_slab(behind_ref, 0)
                pair.append(slab)
            pairs.append(jnp.concatenate(pair, axis=1))
        slabs = forward_chunk(jnp.concatenate(pairs, axis=0), mzf_ref, yf_ref, 2)
        for j in range(8):
            at = p * 8 + j
            mid_freq_s[at * 96 : (at + 1) * 96, :] = with_sum(slabs[j])
    for copy in copies[2:]:
        copy.wait()
    for p in range(4):
        convolve(1, p * 8, 8, near_taps, freq_s, conv_s)
        slabs = [conv_s[(p * 8 + j) * 64 : (p * 8 + j + 1) * 64, :] for j in range(8)]
        space = inverse_chunk(slabs, zi_ref, yi_ref)
        for j in range(8):
            x = p * 8 + j
            near_ref[x * CY : (x + 1) * CY, :] = space[j * YD : j * YD + CY]
    mid_conv_s[9 * 64 :, :] = jnp.zeros((7 * 64, 128), F32)
    for first, count in ((0, 5), (5, 4)):
        convolve(2, first, count, mid_taps, mid_freq_s, mid_conv_s)
    for p in range(2):
        slabs = [mid_conv_s[(p * 8 + j) * 64 : (p * 8 + j + 1) * 64, :] for j in range(8)]
        space = inverse_chunk(slabs, mzi_ref, yi_ref)
        for j in range(8):
            i = p * 8 + j
            if i < 9:
                mid_ref[i * 16 : (i + 1) * 16, :] = space[j * YD : j * YD + 16]


def gauss(index, period, width):
    distance = jnp.minimum(index, period - index).astype(F32)
    return jnp.exp(-(distance * distance) / (width * width))


def gauss_kernel(weights_ref, widths_ref, info_ref, after_ref, x_ref, y_ref, z_ref):
    first_x = info_ref[2] * 8
    first_y = info_ref[3] * 6
    row = lax.broadcasted_iota(jnp.int32, (16, 256), 0)
    column = lax.broadcasted_iota(jnp.int32, (16, 256), 1)
    source = jnp.where(column < 128, column, (column - 128) * 8 + 8)
    offset = (first_x + row - source) & 127
    for k in range(4):
        value = jnp.where(column < 144, gauss(offset, 128, widths_ref[k]), 0.0)
        for n, part in enumerate(halves(value)):
            x_ref[n * 64 + k * 16 : n * 64 + (k + 1) * 16, :] = part
    row = lax.broadcasted_iota(jnp.int32, (128, 128), 0)
    column = lax.broadcasted_iota(jnp.int32, (128, 128), 1)
    for k in range(4):
        value = gauss((row - column) & 63, 64, widths_ref[k]) * weights_ref[k]
        value = jnp.where((row >> 6) == (column >> 6), value, 0.0)
        for n, part in enumerate(halves(value)):
            z_ref[(n * 4 + k) * 128 : (n * 4 + k + 1) * 128, :] = part
    row = lax.broadcasted_iota(jnp.int32, (64, 128), 0)
    column = lax.broadcasted_iota(jnp.int32, (64, 128), 1)
    target = (row >> 3) * 6 + (row & 7)
    source = first_y + (column & 3) * 2 + ((column >> 4) & 1)
    offset = target - source
    offset = jnp.where(offset < 0, offset + 48, offset)
    offset = jnp.where(offset >= 48, offset - 48, offset)
    chosen = (column >> 2) & 3
    value = jnp.zeros((64, 128), F32)
    for k in range(4):
        value = jnp.where(chosen == k, gauss(offset, 48, widths_ref[k]), value)
    for n, part in enumerate(halves(jnp.where(column < 32, value, 0.0))):
        y_ref[n * 64 : (n + 1) * 64, :] = part


def top_kernel(in_ref, x_ref, y_ref, z_ref, out_ref, plane_s, depth_s):
    left = (x_ref[:64, :], x_ref[64:, :])
    columns = []
    for jp in range(4):
        tiles = [in_ref[s * TOP_SENT + jp * 8 : s * TOP_SENT + jp * 8 + 8, :] for s in range(16)]
        tiles.append(in_ref[pl.ds(32 + jp, SIZE_X, stride=TOP_SENT), :])
        tiles.append(jnp.zeros((112, 128), F32))
        columns.append(jnp.concatenate(tiles, axis=0))
    right = halves(jnp.concatenate(columns, axis=1))
    plane = mm(left[0], right[0]) + mm(left[0], right[1]) + mm(left[1], right[0])
    for jp in range(4):
        for k in range(4):
            part = plane[k * 16 : (k + 1) * 16, jp * 128 : (jp + 1) * 128]
            plane_s[(k * 4 + jp) * 16 : (k * 4 + jp + 1) * 16, :] = part
    for k in range(4):
        weight = [z_ref[(n * 4 + k) * 128 : (n * 4 + k + 1) * 128, :] for n in range(2)]
        value = halves(plane_s[k * 64 : (k + 1) * 64, :])
        depth_s[k * 64 : (k + 1) * 64, :] = (
            mm(value[0], weight[0]) + mm(value[0], weight[1]) + mm(value[1], weight[0])
        )
    lane = lax.broadcasted_iota(jnp.int32, (16, 128), 1)
    tiles = []
    for ip in range(5):
        first = depth_s[pl.ds(2 * ip, 16, stride=16), :]
        second = depth_s[pl.ds(2 * ip + 1, 16, stride=16), :]
        even = jnp.where(lane < 64, first, pltpu.roll(second, 64, 1))
        odd = jnp.where(lane < 64, pltpu.roll(first, 64, 1), second)
        tiles.append(jnp.concatenate([even, odd, jnp.zeros((96, 128), F32)], axis=0))
    right = halves(jnp.concatenate(tiles, axis=1))
    left = (y_ref[:64, :], y_ref[64:, :])
    out_ref[...] = mm(left[0], right[0]) + mm(left[0], right[1]) + mm(left[1], right[0])


def finish_kernel(
    near_ref, mid_ref, top_ref, *refs
):
    grow_ref, out_hbm, grown_s, out_ref, sems = refs
    grow_top, grow_z = grow_ref[:128, :], grow_ref[128:256, :]
    grow_fine, grow_y = grow_ref[256:, :128], grow_ref[256:272, 128:]
    total = top_ref[:8, :]
    for s in range(1, SIZE_Y):
        total = total + top_ref[s * 8 : (s + 1) * 8, :]
    lanes = []
    for ip in range(5):
        lanes.append(exact_right(total[:, ip * 128 : (ip + 1) * 128], grow_top))
    deep = jnp.concatenate(lanes, axis=1)
    tiles = []
    for i in range(17):
        tile = deep[:, (i // 2) * 128 : (i // 2 + 1) * 128]
        if i % 2:
            tile = 0.5 * (tile + deep[:, (i // 2 + 1) * 128 : (i // 2 + 2) * 128])
        tiles.append(tile)
    flat = jnp.concatenate(tiles, axis=1)
    flat = jnp.concatenate([flat, jnp.zeros((120, 17 * 128), F32)], axis=0)
    tall = exact_left(grow_y, flat)
    slabs = []
    for i in range(24):
        if i > 16:
            slabs.append(jnp.zeros((16, 128), F32))
            continue
        h = i // 9
        slabs.append(
            tall[:, i * 128 : (i + 1) * 128]
            + mid_ref[(i - 9 * h) * 16 : (i - 9 * h + 1) * 16, h * 128 : (h + 1) * 128]
        )
    for g in range(3):
        part = exact_right(jnp.concatenate(slabs[g * 8 : (g + 1) * 8], axis=0), grow_z)
        grown_s[g * 192 : (g + 1) * 192, :] = exact_left(grow_fine, part)
    copies = []
    for x in range(CX):
        at = slice(x * CY, (x + 1) * CY)
        i = x // 2
        value = grown_s[i * CY : (i + 1) * CY, :]
        if x % 2:
            value = 0.5 * (value + grown_s[(i + 1) * CY : (i + 2) * CY, :])
        out_ref[at, :] = near_ref[at, :] + value
        if x % 8 == 7:
            at = pl.ds((x - 7) * CY, 8 * CY)
            copies += started([(out_ref.at[at], out_hbm.at[at])], sems, x // 8)
    for copy in copies:
        copy.wait()


def swap(to_low, to_high, axis):
    count = lax.axis_size(axis)
    forward = [(i, (i + 1) % count) for i in range(count)]
    backward = [(target, source) for source, target in forward]
    before = lax.ppermute(to_high, axis, forward)
    behind = lax.ppermute(to_low, axis, backward)
    return before, behind


def on_device(
    charge_blocks, block_tile, block_count, near_kernel, mid_kernel, top_weights, top_widths
):
    at_x = lax.axis_index("gx")
    at_y = lax.axis_index("gy")
    info = jnp.stack(
        [block_count[0], ((at_x * SIZE_Y + at_y) % 4) * CAP, at_x, at_y]
    ).astype(jnp.int32)
    outgoing = send(block_tile.reshape(32, 128), info, charge_blocks)
    arrived = lax.all_to_all(
        outgoing.reshape(DEVICES, 1, ROWS * 128),
        ("gx", "gy"),
        split_axis=0,
        concat_axis=0,
        tiled=True,
    ).reshape(DEVICES * ROWS, 128)

    z_fine, z_fine_back = z_matrices(256, 1)
    z_mid, z_mid_back = z_matrices(128, 2)
    y_forward, y_back = y_matrices()
    zf, yf = stacked_rows(z_fine), stacked_cols(y_forward)
    zi, yi = stacked_rows(z_fine_back), stacked_cols(y_back)
    mzf, mzi = stacked_rows(z_mid), stacked_rows(z_mid_back)
    near_taps = taps(near_kernel, 1, zf, yf, outgoing)
    mid_taps = taps(mid_kernel, 2, mzf, yf, outgoing)

    bells = call(
        gauss_kernel,
        tuple(jax.ShapeDtypeStruct(n, BF16) for n in ((128, 256), (128, 128), (1024, 128))),
        [SM, SM, SM, HB],
    )(top_weights, top_widths, info, outgoing)

    fine, mid, low, high, top = collect(arrived, near_taps, mid_taps, bells[0])
    before, behind = swap(low, high, "gy")
    tops = lax.all_to_all(
        top.reshape(SIZE_X, 1, TOP_SENT * 128), "gx", split_axis=0, concat_axis=0, tiled=True
    )
    tops = tops.reshape(SIZE_X * TOP_SENT, 128)
    partial = call(
        top_kernel,
        array(64, 640),
        [VM] * 4,
        [pltpu.VMEM((256, 128), F32), pltpu.VMEM((256, 128), F32)],
    )(tops, *bells)
    partial = lax.all_to_all(
        partial.reshape(SIZE_Y, 8, 640), "gy", split_axis=0, concat_axis=0, tiled=True
    ).reshape(64, 640)
    fine, halo, wide, low, high = merge(fine, mid, before, behind)
    before, behind = swap(low, high, "gx")
    own = call(own_kernel, array(CX * 64, 128), [VM] * 4)(fine, halo, zf, yf)
    grow_z = grow_matrix(2 * 64, 65)
    grow_z[:, 0] += grow_z[:, 64]
    grow_fine_z = grow_matrix(2 * 128, 129)
    grow_fine_z[:, 0] += grow_fine_z[:, 128]
    grow_y = np.zeros((192, 256))
    grow_y[:, :128] = np.kron(np.eye(8), padded(grow_matrix(CY, 13), CY, 16))
    grow_y[:16, 128:135] = padded(grow_matrix(13, 7), 16, 7)
    grow = plain(np.concatenate([twice(grow_z[:, :64].T), grow_fine_z[:, :128].T, grow_y]))
    tables = (wide, mzf, near_taps, mid_taps, zi, yi, mzi)
    near, mid_near, grow = call(
        levels_kernel,
        (array(CX * CY, NZ), array(9 * 16, 256), jax.ShapeDtypeStruct(grow.shape, BF16)),
        [VM] * 5 + [HB] * 8,
        [
            pltpu.VMEM((40 * 96, 128), F32),
            pltpu.VMEM((32 * 64, 128), F32),
            pltpu.VMEM((24 * 96, 128), F32),
            pltpu.VMEM((16 * 64, 128), F32),
            *buffers(*tables),
            pltpu.SemaphoreType.DMA((8,)),
        ],
        limit=14,
    )(own, before, behind, zf, yf, *tables, grow)
    out = call(
        finish_kernel,
        array(CX * CY, NZ),
        [VM] * 4,
        [
            pltpu.VMEM((24 * CY, NZ), F32),
            pltpu.VMEM((CX * CY, NZ), F32),
            pltpu.SemaphoreType.DMA((4,)),
        ],
        outs=HB,
    )(near, mid_near, partial, grow)
    return out.reshape(CX, CY, NZ)


def solution(mesh):
    placed = (P(("gx", "gy"), None), P(("gx", "gy")), P(("gx", "gy")), P(), P(), P(), P())
    return jax.shard_map(
        on_device, mesh=mesh, in_specs=placed, out_specs=P("gx", "gy", None), check_vma=False
    )
```
